32 devices in a mesh: dp: 32 (over z, y, x, core).
Axes of the slice: x: 2, y: 2, z: 4, core: 2. Of those that a mesh axis runs over, the one named last changes fastest.
Arguments:
- images: bfloat16 [256, 196, 512], P('dp'), may hold values from -6 to 6
- cotangent: bfloat16 [256, 196, 512], P('dp'), may hold values from -6 to 6
- image_counts: int32 [32], P('dp'), may hold values from 1 to 8, as said below
- shift_mask: int32 [4, 49, 49], replicated, may hold values from 0 to 1, as said below
- rel_index: int32 [49, 49], replicated, may hold values from 0 to 168
- step_count: int32 [1], replicated, may hold values from 1 to 20
- attend_weight: bfloat16 [512, 1536], P('dp'), may hold values from -0.25 to 0.25
- merge_weight: bfloat16 [512, 512], P('dp'), may hold values from -1 to 1
- expand_weight: bfloat16 [512, 2048], P('dp'), may hold values from -0.25 to 0.25
- project_weight: bfloat16 [2048, 512], P('dp'), may hold values from -0.125 to 0.125
- norm_gains: float32 [2, 512], replicated, may hold values from 0.1 to 1.9
- norm_shifts: float32 [2, 512], replicated, may hold values from -2 to 2
- layer_biases: float32 [4608], replicated, may hold values from -2 to 2
- bias_table: float32 [169, 16], replicated, may hold values from -4 to 4
- attend_momentum: float32 [512, 1536], P('dp'), may hold values from -1.2 to 1.2
- merge_momentum: float32 [512, 512], P('dp'), may hold values from -1.2 to 1.2
- expand_momentum: float32 [512, 2048], P('dp'), may hold values from -1.2 to 1.2
- project_momentum: float32 [2048, 512], P('dp'), may hold values from -1.2 to 1.2
- gains_mean: float32 [2, 512], replicated, may hold values from -0.6 to 0.6
- gains_square: float32 [2, 512], replicated, may hold values from 0.0001 to 0.001
- shifts_mean: float32 [2, 512], replicated, may hold values from -0.6 to 0.6
- shifts_square: float32 [2, 512], replicated, may hold values from 0.0001 to 0.001
- biases_mean: float32 [4608], replicated, may hold values from -0.6 to 0.6
- biases_square: float32 [4608], replicated, may hold values from 0.0001 to 0.001
- table_mean: float32 [169, 16], replicated, may hold values from -0.6 to 0.6
- table_square: float32 [169, 16], replicated, may hold values from 0.0001 to 0.001
Outputs:
- block_out: bfloat16 [256, 196, 512], P('dp')
- input_grad: float32 [256, 196, 512], P('dp')
- attend_grad: float32 [512, 1536], P('dp')
- attend_momentum_next: float32 [512, 1536], P('dp')
- attend_update: float32 [512, 1536], P('dp')
- merge_grad: float32 [512, 512], P('dp')
- merge_momentum_next: float32 [512, 512], P('dp')
- merge_update: float32 [512, 512], P('dp')
- expand_grad: float32 [512, 2048], P('dp')
- expand_momentum_next: float32 [512, 2048], P('dp')
- expand_update: float32 [512, 2048], P('dp')
- project_grad: float32 [2048, 512], P('dp')
- project_momentum_next: float32 [2048, 512], P('dp')
- project_update: float32 [2048, 512], P('dp')
- gains_grad: float32 [2, 512], replicated
- gains_mean_next: float32 [2, 512], replicated
- gains_square_next: float32 [2, 512], replicated
- gains_update: float32 [2, 512], replicated
- shifts_grad: float32 [2, 512], replicated
- shifts_mean_next: float32 [2, 512], replicated
- shifts_square_next: float32 [2, 512], replicated
- shifts_update: float32 [2, 512], replicated
- biases_grad: float32 [4608], replicated
- biases_mean_next: float32 [4608], replicated
- biases_square_next: float32 [4608], replicated
- biases_update: float32 [4608], replicated
- table_grad: float32 [169, 16], replicated
- table_mean_next: float32 [169, 16], replicated
- table_square_next: float32 [169, 16], replicated
- table_update: float32 [169, 16], replicated
The draws below stay inside these ranges and needn't reach their ends.
Inputs may be any that keep to these rules, and one draw needn't show every extreme that they name: `image_counts`: one device holds 8 live images and another holds 1; live images fill a device's first slots. `shift_mask`: 1 where two patches of a window may attend to each other; symmetric, with ones on the diagonal.
All inputs are finite; a program needn't handle non-finite values.
Results may differ from the reference program's by a relative error of at most 0.0095.
The reference program's roundings to bfloat16 on the way count: a program that leaves them out, or rounds other values in their place, can miss the bound.
Values may be sent and summed in bfloat16 or wider, within the bound.
No kernel may reach another device: no remote copies, remote signals or barrier semaphores. Data moves between devices by JAX's collectives and lax.ppermute only.
A program may use at most 256 MiB of HBM per device.

```python
import math
import jax
import jax.numpy as jnp
from jax import lax

D = 512
HEADS = 16
FF = 2048
WIN = 7
SIDE = 14
SHIFT = 3
WIN_TOK = 49
PATCHES = 196
WINDOWS = 4
TABLE = 169
BIAS = 4608
IMG_DEV = 8
IMAGES = 256
N_DP = 32


def draw_image_counts(key, part):
    devices = IMAGES // IMG_DEV
    key_one, key_two, key_three = jax.random.split(jax.random.fold_in(key, 11), 3)
    counts = jax.random.randint(key_one, (devices,), 1, IMG_DEV + 1)
    busiest = jax.random.randint(key_two, (), 0, devices)
    lightest = (busiest + 1 + jax.random.randint(key_three, (), 0, devices - 1)) % devices
    places = jnp.arange(devices)
    counts = jnp.where(places == busiest, IMG_DEV, counts)
    counts = jnp.where(places == lightest, 1, counts)
    return counts.astype(jnp.int32)


def draw_shift_mask(key, part):
    labels = jax.random.randint(jax.random.fold_in(key, 23), (WINDOWS, WIN_TOK), 0, 3)
    return (labels[:, :, None] == labels[:, None, :]).astype(jnp.int32)


def place_ends(values, key, smallest, largest):
    index_at = [jax.random.randint(jax.random.fold_in(key, axis), (), 0, length) for axis, length in enumerate(values.shape)]
    longest = values.shape.index(max(values.shape))
    beside = index_at[:longest] + [(index_at[longest] + 1) % values.shape[longest]] + index_at[longest + 1:]
    return values.at[tuple(index_at)].set(smallest).at[tuple(beside)].set(largest)


def shard_levels(rng, extent, shards, least, top_value):
    level = 1.0
    for dim, blocks in shards:
        draws = jax.random.uniform(jax.random.fold_in(jax.random.fold_in(rng, 6), dim), (blocks,), jnp.float32, least / len(shards), top_value / len(shards))
        level = level * jnp.repeat(jnp.exp(draws), extent[dim] // blocks).reshape((-1,) + (1,) * (len(extent) - 1 - dim))
    return level


def centred(rng, shape, scale, bound, pieces=(), dtype=jnp.bfloat16):
    factor_of = shard_levels(rng, shape, pieces, -0.22, 0.18) if pieces else 1.0
    entries = jax.random.normal(rng, shape, jnp.float32) * scale * factor_of
    return jnp.minimum(jnp.maximum(entries, -bound), bound).astype(dtype)


def setup_inputs(seed: int = 0) -> dict:
    key_of = jax.random.split(jax.random.key(seed), 27)
    images = centred(key_of[0], (IMAGES, PATCHES, D), 1.0, 6.0, ((0, 32),))
    cotangent = centred(key_of[1], (IMAGES, PATCHES, D), 1.0, 6.0, ((0, 32),))
    image_counts = draw_image_counts(jax.random.fold_in(key_of[26], 71), 0)
    shift_mask = draw_shift_mask(jax.random.fold_in(key_of[26], 71), 0)
    rel_index = place_ends(jax.random.randint(key_of[4], (WIN_TOK, WIN_TOK), 0, TABLE), jax.random.fold_in(key_of[4], 1), 0, TABLE - 1).astype(jnp.int32)
    step_count = jax.random.randint(key_of[5], (1,), 1, 21).astype(jnp.int32)
    attend_weight = centred(key_of[6], (D, 3 * D), D ** -0.5, 0.25, ((0, 32),))
    merge_weight = centred(key_of[7], (D, D), (D // HEADS) ** -0.5, 1.0, ((0, 32),))
    expand_weight = centred(key_of[8], (D, FF), D ** -0.5, 0.25, ((0, 32),))
    project_weight = centred(key_of[9], (FF, D), FF ** -0.5, 0.125, ((0, 32),))
    norm_gains = jnp.clip(1.0 + 0.18 * jax.random.normal(key_of[10], (2, D), jnp.float32), 0.1, 1.9)
    norm_shifts = centred(key_of[11], (2, D), 0.3, 2.0, (), jnp.float32)
    layer_biases = centred(key_of[12], (BIAS,), 0.3, 2.0, (), jnp.float32)
    bias_table = centred(key_of[13], (TABLE, HEADS), 1.0, 4.0, (), jnp.float32)
    attend_momentum = centred(key_of[14], (D, 3 * D), 0.2, 1.2, ((0, 32),), jnp.float32)
    merge_momentum = centred(key_of[15], (D, D), 0.2, 1.2, ((0, 32),), jnp.float32)
    expand_momentum = centred(key_of[16], (D, FF), 0.2, 1.2, ((0, 32),), jnp.float32)
    project_momentum = centred(key_of[17], (FF, D), 0.2, 1.2, ((0, 32),), jnp.float32)
    gains_mean = centred(key_of[18], (2, D), 0.1, 0.6, (), jnp.float32)
    gains_square = jnp.clip(jnp.exp(jax.random.uniform(key_of[19], (2, D), jnp.float32, math.log(0.0001), math.log(0.001))), 0.0001, 0.001)
    shifts_mean = centred(key_of[20], (2, D), 0.1, 0.6, (), jnp.float32)
    shifts_square = jnp.clip(jnp.exp(jax.random.uniform(key_of[21], (2, D), jnp.float32, math.log(0.0001), math.log(0.001))), 0.0001, 0.001)
    biases_mean = centred(key_of[22], (BIAS,), 0.1, 0.6, (), jnp.float32)
    biases_square = jnp.clip(jnp.exp(jax.random.uniform(key_of[23], (BIAS,), jnp.float32, math.log(0.0001), math.log(0.001))), 0.0001, 0.001)
    table_mean = centred(key_of[24], (TABLE, HEADS), 0.1, 0.6, (), jnp.float32)
    table_square = jnp.clip(jnp.exp(jax.random.uniform(key_of[25], (TABLE, HEADS), jnp.float32, math.log(0.0001), math.log(0.001))), 0.0001, 0.001)
    return {"images": images, "cotangent": cotangent, "image_counts": image_counts, "shift_mask": shift_mask, "rel_index": rel_index, "step_count": step_count, "attend_weight": attend_weight, "merge_weight": merge_weight, "expand_weight": expand_weight, "project_weight": project_weight, "norm_gains": norm_gains, "norm_shifts": norm_shifts, "layer_biases": layer_biases, "bias_table": bias_table, "attend_momentum": attend_momentum, "merge_momentum": merge_momentum, "expand_momentum": expand_momentum, "project_momentum": project_momentum, "gains_mean": gains_mean, "gains_square": gains_square, "shifts_mean": shifts_mean, "shifts_square": shifts_square, "biases_mean": biases_mean, "biases_square": biases_square, "table_mean": table_mean, "table_square": table_square}


@jax.custom_vjp
def low(v):
    return lax.optimization_barrier(v.astype(jnp.bfloat16)).astype(jnp.float32)

@jax.custom_vjp
def low_back(v):
    return v

def low_keep(v):
    return (low(v), None)

def low_pass(kept, grad):
    return (grad,)

def back_keep(v):
    return (v, None)

def back_low(kept, grad):
    return (low(grad),)
low.defvjp(low_keep, low_pass)
low_back.defvjp(back_keep, back_low)
highest = lax.Precision.HIGHEST
newton_first = 3.4445
newton_second = -4.775
newton_third = 2.0315

def layer_norm(values, gain, shift):
    center = values - lax.optimization_barrier(jnp.mean(values, axis=-1, keepdims=True))
    spread = lax.optimization_barrier(jnp.mean(center * center, axis=-1, keepdims=True))
    return center * lax.rsqrt(spread + 1e-05) * gain + shift

def to_windows(field):
    count = field.shape[0]
    blocks = SIDE // WIN
    square = field.reshape(count, SIDE, SIDE, field.shape[-1])
    rolled = jnp.roll(square, (-SHIFT, -SHIFT), (1, 2))
    parted = rolled.reshape(count, blocks, WIN, blocks, WIN, field.shape[-1])
    return parted.transpose(0, 1, 3, 2, 4, 5).reshape(count * blocks * blocks, WIN * WIN, field.shape[-1])

def from_windows(windows, count):
    blocks = SIDE // WIN
    parted = windows.reshape(count, blocks, blocks, WIN, WIN, windows.shape[-1])
    square = parted.transpose(0, 1, 3, 2, 4, 5).reshape(count, SIDE, SIDE, windows.shape[-1])
    return jnp.roll(square, (SHIFT, SHIFT), (1, 2)).reshape(count, SIDE * SIDE, windows.shape[-1])

def split_heads(rows):
    return rows.reshape(rows.shape[0], rows.shape[1], HEADS, -1).transpose(0, 2, 1, 3)

def merge_heads(rows):
    return rows.transpose(0, 2, 1, 3).reshape(rows.shape[0], rows.shape[2], -1)

def block(features, mats, params, rel_index, mask_add, valid):
    attend, merge, expand, project = mats
    gains, shifts, biases, table = params
    width = features.shape[-1]
    count = features.shape[0]
    hidden_units = expand.shape[1]
    scale = 1.0 / math.sqrt(width // HEADS)
    normed = low(layer_norm(features, gains[0], shifts[0]))
    windows = to_windows(normed)
    triple = low_back(jnp.einsum('wtd,de->wte', windows, attend, precision=highest) + biases[:3 * width])
    queries = low(split_heads(triple[..., :width] * scale))
    keys_low = low(split_heads(triple[..., width:2 * width]))
    values_low = low(split_heads(triple[..., 2 * width:]))
    position = table[rel_index].transpose(2, 0, 1)
    masking = jnp.tile(mask_add, (count, 1, 1))[:, None]
    scores = low_back(jnp.einsum('whqc,whkc->whqk', queries, keys_low, precision=highest) + position + masking)
    attention = low(jax.nn.softmax(scores, axis=-1))
    mixed = low(low_back(merge_heads(jnp.einsum('whqk,whkc->whqc', attention, values_low, precision=highest))))
    branch = low_back(jnp.einsum('wtd,de->wte', mixed, merge, precision=highest) + biases[3 * width:4 * width])
    middle = features + from_windows(branch, count)
    normed_two = low(layer_norm(middle, gains[1], shifts[1]))
    pre_act = low_back(jnp.einsum('itd,df->itf', normed_two, expand, precision=highest) + biases[4 * width:4 * width + hidden_units])
    activated = low(jax.nn.gelu(pre_act, approximate=False))
    mlp_out = low_back(jnp.einsum('itf,fd->itd', activated, project, precision=highest) + biases[4 * width + hidden_units:])
    return (middle + mlp_out) * valid[:, None, None]

def orthogonalize(matrix):
    tall = matrix.shape[0] > matrix.shape[1]
    current = matrix.T if tall else matrix
    current = current / (jnp.sqrt(jnp.sum(current * current)) + 1e-07)
    for sweep in range(5):
        square = jnp.dot(current, current.T, precision=highest)
        mixer = newton_second * square + newton_third * jnp.dot(square, square, precision=highest)
        current = newton_first * current + jnp.dot(mixer, current, precision=highest)
    return current.T if tall else current

def adamw_step(param, grad, first, second, steps):
    first_next = 0.9 * first + 0.1 * grad
    second_next = 0.999 * second + 0.001 * grad * grad
    first_hat = first_next / (1.0 - jnp.power(0.9, steps))
    second_hat = second_next / (1.0 - jnp.power(0.999, steps))
    update = -0.05 * (first_hat / (jnp.sqrt(second_hat) + 1e-08) + 0.05 * param)
    return (first_next, second_next, update)

def reference(images, cotangent, image_counts, shift_mask, rel_index, step_count, attend_weight, merge_weight, expand_weight, project_weight, norm_gains, norm_shifts, layer_biases, bias_table, attend_momentum, merge_momentum, expand_momentum, project_momentum, gains_mean, gains_square, shifts_mean, shifts_square, biases_mean, biases_square, table_mean, table_square):
    mask_add = -100.0 * (1 - shift_mask).astype(jnp.float32)
    weights = (attend_weight.astype(jnp.float32), merge_weight.astype(jnp.float32), expand_weight.astype(jnp.float32), project_weight.astype(jnp.float32))
    small = (norm_gains, norm_shifts, layer_biases, bias_table)
    stacked = images.reshape(N_DP, IMG_DEV, PATCHES, D)
    cot_stack = cotangent.reshape(N_DP, IMG_DEV, PATCHES, D)

    def one_device(totals, item):
        block_in, block_cot, count = item
        valid = (jnp.arange(IMG_DEV) < count).astype(jnp.float32)

        def forward(features, mats, params):
            return block(features, mats, params, rel_index, mask_add, valid)
        result, pull = jax.vjp(forward, block_in.astype(jnp.float32), weights, small)
        grad_feat, grad_mats, grad_params = pull(block_cot.astype(jnp.float32))
        totals = jax.tree.map(jnp.add, totals, (grad_mats, grad_params))
        return (totals, (result.astype(jnp.bfloat16), grad_feat))
    zeros = jax.tree.map(jnp.zeros_like, (weights, small))
    totals, (outs, grads) = lax.scan(one_device, zeros, (stacked, cot_stack, image_counts))
    grad_scale = 1.0 / math.sqrt(IMAGES * PATCHES)
    mat_grads = tuple((term * grad_scale for term in totals[0]))
    small_grads = tuple((term * grad_scale for term in totals[1]))
    block_out = outs.reshape(IMAGES, PATCHES, D)
    input_grad = grads.reshape(IMAGES, PATCHES, D)
    results = [block_out, input_grad]
    momenta = (attend_momentum, merge_momentum, expand_momentum, project_momentum)
    for grad, moment in zip(mat_grads, momenta):
        moment_next = 0.95 * moment + grad
        update = -0.02 * math.sqrt(max(moment.shape)) * orthogonalize(moment_next)
        results += [grad, moment_next, update]
    steps = step_count[0].astype(jnp.float32)
    states = ((gains_mean, gains_square), (shifts_mean, shifts_square), (biases_mean, biases_square), (table_mean, table_square))
    for param, grad, state in zip(small, small_grads, states):
        first_next, second_next, update = adamw_step(param, grad, state[0], state[1], steps)
        results += [grad, first_next, second_next, update]
    return tuple(results)
```

```python
import math

import jax
import jax.numpy as jnp
from jax import lax
from jax.experimental import pallas as pl
from jax.experimental.pallas import tpu as pltpu
from jax.sharding import PartitionSpec as P

HEADS = 16
WIN = 7
SIDE = 14
SHIFT = 3
WIN_TOK = 49
PATCHES = 196
TABLE = 169


highest = lax.Precision.HIGHEST
newton_first = 3.4445
newton_second = -4.775
newton_third = 2.0315


LANE = 512
CELL = 8


def device_bits(devices):
    return devices.bit_length() - 1


def swap(payload, devices, bit):
    return lax.ppermute(payload, "dp", [(i, i ^ (1 << bit)) for i in range(devices)])


def my_bit(rank, bit):
    return (rank >> bit) & 1


def gather_rows(pieces, rank, devices):
    bits = device_bits(devices)
    k, rows, lanes = pieces.shape
    current = pieces.reshape((k,) + (1,) * bits + (rows, lanes))
    for bit in list(range(3, bits)) + [2, 1, 0]:
        axis = bits - bit
        other = swap(current, devices, bit)
        high = my_bit(rank, bit) == 1
        current = jnp.concatenate(
            [jnp.where(high, other, current), jnp.where(high, current, other)], axis=axis
        )
    return current.reshape(k, devices * rows, lanes)


def split_wide(values):
    high = lax.reduce_precision(values, 8, 7)
    return high.astype(jnp.bfloat16), (values - high).astype(jnp.bfloat16)


def reduce_rows(parts, wide, rank, devices):
    bits = device_bits(devices)
    planes = devices // CELL
    running = []
    for part in parts:
        blocks, _, rows, lanes = part.shape
        running.append(part.reshape(blocks, planes, 2, 2, 2, rows, lanes))

    def encode(values):
        sent = []
        for value, keep in zip(values, wide):
            for piece in split_wide(value) if keep else (value.astype(jnp.bfloat16),):
                flat = jnp.moveaxis(piece, 0, -3)
                sent.append(flat.reshape(flat.shape[:-3] + (-1, flat.shape[-1])))
        return jnp.concatenate(sent, axis=-2)

    def decode(payload, values):
        out, start = [], 0
        for value, keep in zip(values, wide):
            blocks, rows = value.shape[0], value.shape[-2]
            total = None
            for _ in range(2 if keep else 1):
                piece = payload[..., start : start + blocks * rows, :].astype(jnp.float32)
                start += blocks * rows
                piece = piece.reshape(piece.shape[:-2] + (blocks, rows, piece.shape[-1]))
                piece = jnp.moveaxis(piece, -3, 0)
                total = piece if total is None else total + piece
            out.append(total)
        return out

    for bit, axis in ((0, 4), (1, 3), (2, 2)):
        mine = my_bit(rank, bit)
        give = [lax.dynamic_index_in_dim(r, 1 - mine, axis, keepdims=False) for r in running]
        keep = [lax.dynamic_index_in_dim(r, mine, axis, keepdims=False) for r in running]
        got = decode(swap(encode(give), devices, bit), give)
        running = [k + g for k, g in zip(keep, got)]
    plane = rank // CELL
    total = [lax.dynamic_index_in_dim(r, plane, 1, keepdims=False) for r in running]
    for step in range(1, planes):
        target = (plane + step) % planes
        give = [lax.dynamic_index_in_dim(r, target, 1, keepdims=False) for r in running]
        pairs = [(i, (i + step * CELL) % devices) for i in range(devices)]
        got = decode(lax.ppermute(encode(give), "dp", pairs), give)
        total = [t + g for t, g in zip(total, got)]
    return total


def collect(rows, owners, rank, devices):
    planes = devices // CELL
    plane = rank // CELL
    stacked = jnp.stack(rows)
    pieces = [lax.dynamic_index_in_dim(stacked, jnp.clip(plane - owners[0], 0, len(owners) - 1), 0, keepdims=False)]
    for step in range(1, planes):
        target = (plane + step) % planes
        give = lax.dynamic_index_in_dim(stacked, jnp.clip(target - owners[0], 0, len(owners) - 1), 0, keepdims=False)
        pairs = [
            (i, (i + step * CELL) % devices)
            for i in range(devices)
            if ((i // CELL + step) % planes) in owners
        ]
        pieces.append(lax.ppermute(give, "dp", pairs))
    current = jnp.stack(pieces)[None]
    for bit in (2, 1, 0):
        pairs = [(i, i ^ (1 << bit)) for i in range(devices) if i // CELL in owners]
        current = jnp.concatenate([current, lax.ppermute(current, "dp", pairs)], axis=0)
    return current


def split_bf16(values):
    high = values.astype(jnp.bfloat16)
    return high, (values - high.astype(jnp.float32)).astype(jnp.bfloat16)


def dot_three(left, right, dims):
    left_high, left_low = split_bf16(left)
    right_high, right_low = split_bf16(right)

    def one(a, b):
        return lax.dot_general(a, b, (dims, ((), ())), preferred_element_type=jnp.float32)

    return one(left_high, right_high) + (one(left_low, right_high) + one(left_high, right_low))


PLAIN = ((1,), (0,))


def newton_kernel(tall_ref, stack_ref, out_ref, gram_ref, poly_ref, total_ref):
    tall = tall_ref[0] == 1
    blocks = stack_ref.shape[0]
    side = gram_ref.shape[0]
    chunk = out_ref.shape[1]

    @pl.when(tall)
    def _():
        total = jnp.zeros((side, side), jnp.float32)
        for block in range(blocks):
            values = stack_ref[block]
            total = total + dot_three(values, values, ((0,), (0,)))
        gram_ref[...] = total

    @pl.when(jnp.logical_not(tall))
    def _():
        total = jnp.zeros((side, side), jnp.float32)
        for block in range(blocks):
            values = stack_ref[block]
            total = total + dot_three(values, values, ((1,), (1,)))
        gram_ref[...] = total

    gram = gram_ref[...]
    row = lax.broadcasted_iota(jnp.int32, (side, side), 0)
    column = lax.broadcasted_iota(jnp.int32, (side, side), 1)
    eye = (row == column).astype(jnp.float32)
    norm = jnp.sqrt(jnp.sum(gram * eye)) + 1e-07
    inverse = 1.0 / norm
    gram_ref[...] = gram * (inverse * inverse)
    poly_ref[...] = eye * inverse

    def sweep(step, carry):
        gram = gram_ref[...]
        mixer = newton_first * eye + newton_second * gram + newton_third * dot_three(gram, gram, PLAIN)
        poly_ref[...] = dot_three(poly_ref[...], mixer, PLAIN)
        gram_ref[...] = dot_three(dot_three(gram, mixer, PLAIN), mixer, PLAIN)
        return carry

    lax.fori_loop(0, 5, sweep, 0)

    @pl.when(tall)
    def _():
        for block in range(blocks):
            out_ref[block] = dot_three(stack_ref[block, :chunk], poly_ref[...], PLAIN).astype(out_ref.dtype)

    @pl.when(jnp.logical_not(tall))
    def _():
        for block in range(blocks):
            out_ref[block] = dot_three(poly_ref[:chunk], stack_ref[block], PLAIN).astype(out_ref.dtype)


def newton_rows(stack, tall, chunk):
    blocks, side, lanes = stack.shape
    return pl.pallas_call(
        newton_kernel,
        out_shape=jax.ShapeDtypeStruct((blocks, chunk, lanes), jnp.bfloat16),
        in_specs=[
            pl.BlockSpec(memory_space=pltpu.SMEM),
            pl.BlockSpec(memory_space=pltpu.VMEM),
        ],
        out_specs=pl.BlockSpec(memory_space=pltpu.VMEM),
        scratch_shapes=[pltpu.VMEM((side, side), jnp.float32)] * 3,
        compiler_params=pltpu.CompilerParams(vmem_limit_bytes=48 << 20),
    )(tall, stack)


def layer_norm(values, gain, shift):
    center = values - jnp.mean(values, axis=-1, keepdims=True)
    spread = jnp.mean(center * center, axis=-1, keepdims=True)
    return center * lax.rsqrt(spread + 1e-05) * gain + shift


def gelu_exact(values):
    return jax.nn.gelu(values, approximate=False)


def to_windows(field):
    count = field.shape[0]
    blocks = SIDE // WIN
    square = field.reshape(count, SIDE, SIDE, field.shape[-1])
    rolled = jnp.roll(square, (-SHIFT, -SHIFT), (1, 2))
    parted = rolled.reshape(count, blocks, WIN, blocks, WIN, field.shape[-1])
    return parted.transpose(0, 1, 3, 2, 4, 5).reshape(
        count * blocks * blocks, WIN * WIN, field.shape[-1]
    )


def from_windows(windows, count):
    blocks = SIDE // WIN
    parted = windows.reshape(count, blocks, blocks, WIN, WIN, windows.shape[-1])
    square = parted.transpose(0, 1, 3, 2, 4, 5).reshape(count, SIDE, SIDE, windows.shape[-1])
    return jnp.roll(square, (SHIFT, SHIFT), (1, 2)).reshape(count, SIDE * SIDE, windows.shape[-1])


def split_heads(rows):
    return rows.reshape(rows.shape[0], rows.shape[1], HEADS, -1).transpose(0, 2, 1, 3)


def merge_heads(rows):
    return rows.transpose(0, 2, 1, 3).reshape(rows.shape[0], rows.shape[2], -1)


def adamw_step(param, grad, first, second, steps):
    first_next = 0.9 * first + 0.1 * grad
    second_next = 0.999 * second + 0.001 * grad * grad
    first_hat = first_next / (1.0 - jnp.power(0.9, steps))
    second_hat = second_next / (1.0 - jnp.power(0.999, steps))
    update = -0.05 * (first_hat / (jnp.sqrt(second_hat) + 1e-08) + 0.05 * param)
    return (first_next, second_next, update)


def column_blocks(matrix):
    rows, columns = matrix.shape
    return jnp.transpose(matrix.reshape(rows, columns // LANE, LANE), (1, 0, 2))


def from_blocks(blocks):
    count, rows, lanes = blocks.shape
    return jnp.transpose(blocks, (1, 0, 2)).reshape(rows, count * lanes)


def by_owner(term, devices):
    blocks = column_blocks(term)
    return blocks.reshape(blocks.shape[0], devices, -1, LANE)


def owner_form(moment, largest):
    flat = column_blocks(moment).reshape(-1, LANE)
    rows = largest - flat.shape[0]
    return jnp.pad(flat, ((0, rows), (0, 0))).reshape(4, -1, LANE)


def local(
    images,
    cotangent,
    image_counts,
    shift_mask,
    rel_index,
    step_count,
    attend_weight,
    merge_weight,
    expand_weight,
    project_weight,
    norm_gains,
    norm_shifts,
    layer_biases,
    bias_table,
    attend_momentum,
    merge_momentum,
    expand_momentum,
    project_momentum,
    gains_mean,
    gains_square,
    shifts_mean,
    shifts_square,
    biases_mean,
    biases_square,
    table_mean,
    table_square,
):
    f32 = jnp.float32
    bf16 = jnp.bfloat16
    slots = images.shape[0]
    width = images.shape[2]
    devices = lax.axis_size("dp")
    hidden_units = expand_weight.shape[1]
    scale = 1.0 / math.sqrt(width // HEADS)
    grad_scale = 1.0 / math.sqrt(slots * devices * PATCHES)
    rank = lax.axis_index("dp")
    planes = devices // CELL
    first = jnp.concatenate([column_blocks(attend_weight), column_blocks(merge_weight)])
    first_full = gather_rows(first, rank, devices)
    attend_full = from_blocks(first_full[:3])
    merge_full = first_full[3]
    expand_full = from_blocks(gather_rows(column_blocks(expand_weight), rank, devices))
    project_full = gather_rows(project_weight[None], rank, devices)[0]
    valid = (jnp.arange(slots) < image_counts[0]).astype(f32)[:, None, None]
    mask_add = -100.0 * (1 - shift_mask).astype(f32)
    masking = jnp.tile(mask_add, (slots, 1, 1))[:, None]
    one_hot = (rel_index.reshape(-1)[:, None] == jnp.arange(TABLE)[None, :]).astype(f32)
    position = jnp.dot(one_hot, bias_table, precision=highest).T.reshape(HEADS, WIN_TOK, WIN_TOK)
    features = images.astype(f32)
    normed, norm_pull = jax.vjp(layer_norm, features, norm_gains[0], norm_shifts[0])
    windows = to_windows(normed.astype(bf16))
    triple = (
        jnp.einsum("wtd,de->wte", windows, attend_full, preferred_element_type=f32)
        + layer_biases[: 3 * width]
    )
    queries = split_heads(triple[..., :width] * scale).astype(bf16)
    keys_low = split_heads(triple[..., width : 2 * width]).astype(bf16)
    values_low = split_heads(triple[..., 2 * width :]).astype(bf16)
    scores = (
        jnp.einsum("whqc,whkc->whqk", queries, keys_low, preferred_element_type=f32)
        + position
        + masking
    )
    attention = jax.nn.softmax(scores, axis=-1)
    attention_low = attention.astype(bf16)
    mixed = merge_heads(
        jnp.einsum("whqk,whkc->whqc", attention_low, values_low, preferred_element_type=f32)
    ).astype(bf16)
    branch = (
        jnp.einsum("wtd,de->wte", mixed, merge_full, preferred_element_type=f32)
        + layer_biases[3 * width : 4 * width]
    )
    middle = features + from_windows(branch, slots)
    normed_two, norm_two_pull = jax.vjp(layer_norm, middle, norm_gains[1], norm_shifts[1])
    normed_low = normed_two.astype(bf16)
    pre_act = (
        jnp.einsum("itd,df->itf", normed_low, expand_full, preferred_element_type=f32)
        + layer_biases[4 * width : 4 * width + hidden_units]
    )
    activated, gelu_pull = jax.vjp(gelu_exact, pre_act)
    active_low = activated.astype(bf16)
    mlp_out = (
        jnp.einsum("itf,fd->itd", active_low, project_full, preferred_element_type=f32)
        + layer_biases[4 * width + hidden_units :]
    )
    block_out = (valid * (middle + mlp_out)).astype(bf16)
    attend_back, merge_back, expand_back, project_back = (attend_full, merge_full, expand_full, project_full)
    grad_out = valid * cotangent.astype(f32)
    grad_out_low = grad_out.astype(bf16)
    project_term = jnp.einsum("itf,itd->fd", active_low, grad_out_low, preferred_element_type=f32)
    grad_act = jnp.einsum("itd,fd->itf", grad_out_low, project_back, preferred_element_type=f32)
    grad_pre = gelu_pull(grad_act)[0].astype(bf16)
    expand_term = jnp.einsum("itd,itf->df", normed_low, grad_pre, preferred_element_type=f32)
    grad_normed_two = jnp.einsum("itf,df->itd", grad_pre, expand_back, preferred_element_type=f32)
    grad_mid_norm, gain_two, shift_two = norm_two_pull(grad_normed_two)
    grad_middle = grad_out + grad_mid_norm
    grad_branch = to_windows(grad_middle).astype(bf16)
    merge_term = jnp.einsum("wtd,wte->de", mixed, grad_branch, preferred_element_type=f32)
    grad_mixed = split_heads(
        jnp.einsum("wte,de->wtd", grad_branch, merge_back, preferred_element_type=f32).astype(bf16)
    )
    grad_values = jnp.einsum(
        "whqk,whqc->whkc", attention_low, grad_mixed, preferred_element_type=f32
    )
    grad_attention = jnp.einsum(
        "whqc,whkc->whqk", grad_mixed, values_low, preferred_element_type=f32
    )
    grad_scores = (
        attention * (grad_attention - jnp.sum(grad_attention * attention, axis=-1, keepdims=True))
    ).astype(bf16)
    position_grad = jnp.sum(grad_scores, axis=0, dtype=f32).reshape(HEADS, WIN_TOK * WIN_TOK)
    table_term = jnp.dot(one_hot.T, position_grad.T, precision=highest)
    grad_queries = jnp.einsum("whqk,whkc->whqc", grad_scores, keys_low, preferred_element_type=f32)
    grad_keys = jnp.einsum("whqk,whqc->whkc", grad_scores, queries, preferred_element_type=f32)
    grad_triple = jnp.concatenate(
        [merge_heads(grad_queries) * scale, merge_heads(grad_keys), merge_heads(grad_values)],
        axis=-1,
    ).astype(bf16)
    attend_term = jnp.einsum("wtd,wte->de", windows, grad_triple, preferred_element_type=f32)
    grad_normed = from_windows(
        jnp.einsum("wte,de->wtd", grad_triple, attend_back, preferred_element_type=f32), slots
    )
    grad_feat, gain_one, shift_one = norm_pull(grad_normed)
    input_grad = grad_middle + grad_feat
    bias_term = jnp.concatenate(
        [
            jnp.sum(grad_triple, axis=(0, 1), dtype=f32),
            jnp.sum(grad_branch, axis=(0, 1), dtype=f32),
            jnp.sum(grad_pre, axis=(0, 1), dtype=f32),
            jnp.sum(grad_out_low, axis=(0, 1), dtype=f32),
        ]
    )
    merge_sum, expand_sum, project_sum = reduce_rows(
        [by_owner(merge_term, devices), by_owner(expand_term, devices), by_owner(project_term, devices)],
        (True, False, False),
        rank,
        devices,
    )
    (attend_sum,) = reduce_rows([by_owner(attend_term, devices)], (False,), rank, devices)
    mat_sums = tuple(from_blocks(term) for term in (attend_sum, merge_sum, expand_sum, project_sum))
    small_sums = lax.psum(
        (jnp.stack([gain_one, gain_two]), jnp.stack([shift_one, shift_two]), bias_term, table_term),
        "dp",
    )
    mat_grads = tuple((term * grad_scale for term in mat_sums))
    small_grads = tuple((term * grad_scale for term in small_sums))
    momenta = (attend_momentum, merge_momentum, expand_momentum, project_momentum)
    momenta_next = tuple((0.95 * moment + grad for moment, grad in zip(momenta, mat_grads)))
    largest = project_momentum.shape[0]
    packed = [owner_form(moment, largest) for moment in momenta_next]
    rest = collect(packed[1:], (1, 2, 3), rank, devices)
    head = collect(packed[:1], (0,), rank, devices)
    plane = rank // CELL
    whole = jnp.where(plane == 0, head, rest)
    stack = jnp.transpose(whole, (2, 0, 1, 3, 4)).reshape(4, -1, LANE)
    tall = (plane == 3).astype(jnp.int32).reshape(1)
    chunk = planes * packed[0].shape[1]
    orth = newton_rows(stack, tall, chunk).reshape(4, planes, -1, LANE)
    pieces = []
    for step in range(planes):
        give = orth[:, (planes - step) % planes]
        if step:
            pairs = [(i, (i + step * CELL) % devices) for i in range(devices) if i // CELL < 4]
            give = lax.ppermute(give, "dp", pairs)
        pieces.append(give)
    received = jnp.stack(pieces)
    orth_rows = []
    for order, moment in enumerate(momenta_next):
        piece = lax.dynamic_index_in_dim(received, (plane - order) % planes, 0, keepdims=False)
        blocks, rows = max(moment.shape[1] // LANE, 1), moment.shape[0]
        piece = piece.reshape(-1, LANE)[: blocks * rows].reshape(blocks, rows, LANE)
        orth_rows.append(from_blocks(piece).astype(f32))
    results = [block_out, input_grad]
    for grad, moment_next, orth_part in zip(mat_grads, momenta_next, orth_rows):
        extent = max(devices * moment_next.shape[0], moment_next.shape[1])
        update = -0.02 * math.sqrt(extent) * orth_part
        results += [grad, moment_next, update]
    steps = step_count[0].astype(f32)
    params = (norm_gains, norm_shifts, layer_biases, bias_table)
    states = (
        (gains_mean, gains_square),
        (shifts_mean, shifts_square),
        (biases_mean, biases_square),
        (table_mean, table_square),
    )
    for param, grad, state in zip(params, small_grads, states):
        first_next, second_next, update = adamw_step(param, grad, state[0], state[1], steps)
        results += [grad, first_next, second_next, update]
    return tuple(results)


def solution(mesh):
    return jax.shard_map(
        local,
        mesh=mesh,
        in_specs=(
            P("dp", None, None),
            P("dp", None, None),
            P("dp"),
            P(),
            P(),
            P(),
            P("dp", None),
            P("dp", None),
            P("dp", None),
            P("dp", None),
            P(),
            P(),
            P(),
            P(),
            P("dp", None),
            P("dp", None),
            P("dp", None),
            P("dp", None),
            P(),
            P(),
            P(),
            P(),
            P(),
            P(),
            P(),
            P(),
        ),
        out_specs=(
            P("dp", None, None),
            P("dp", None, None),
            P("dp", None),
            P("dp", None),
            P("dp", None),
            P("dp", None),
            P("dp", None),
            P("dp", None),
            P("dp", None),
            P("dp", None),
            P("dp", None),
            P("dp", None),
            P("dp", None),
            P("dp", None),
            P(),
            P(),
            P(),
            P(),
            P(),
            P(),
            P(),
            P(),
            P(),
            P(),
            P(),
            P(),
            P(),
            P(),
            P(),
            P(),
        ),
        check_vma=False,
    )
```

```python
from functools import partial
import math

import jax
import jax.numpy as jnp
import numpy as np
from jax import lax
from jax.experimental import pallas as pl
from jax.experimental.pallas import tpu as pltpu
from jax.sharding import PartitionSpec as P

HEADS = 16
WIN = 7
SIDE = 14
SHIFT = 3
WIN_TOK = 49
PATCHES = 196
TABLE = 169


newton_first = 3.4445
newton_second = -4.775
newton_third = 2.0315


LANE = 512
CELL = 8


def device_bits(devices):
    return devices.bit_length() - 1


def swap(payload, devices, bit):
    return lax.ppermute(payload, "dp", [(i, i ^ (1 << bit)) for i in range(devices)])


def my_bit(rank, bit):
    return (rank >> bit) & 1


def gather_rows(pieces, rank, devices):
    bits = device_bits(devices)
    k, rows, lanes = pieces.shape
    current = pieces.reshape((k,) + (1,) * bits + (rows, lanes))
    for bit in list(range(3, bits)) + [2, 1, 0]:
        axis = bits - bit
        other = swap(current, devices, bit)
        high = my_bit(rank, bit) == 1
        current = jnp.concatenate(
            [jnp.where(high, other, current), jnp.where(high, current, other)], axis=axis
        )
    return current.reshape(k, devices * rows, lanes)


def split_wide(values):
    high = lax.reduce_precision(values, 8, 7)
    return high.astype(jnp.bfloat16), (values - high).astype(jnp.bfloat16)


def reduce_rows(parts, wide, rank, devices):
    bits = device_bits(devices)
    planes = devices // CELL
    running = []
    for part in parts:
        blocks, _, rows, lanes = part.shape
        running.append(part.reshape(blocks, planes, 2, 2, 2, rows, lanes))

    def encode(values):
        sent = []
        for value, keep in zip(values, wide):
            for piece in split_wide(value) if keep else (value.astype(jnp.bfloat16),):
                flat = jnp.moveaxis(piece, 0, -3)
                sent.append(flat.reshape(flat.shape[:-3] + (-1, flat.shape[-1])))
        return jnp.concatenate(sent, axis=-2)

    def decode(payload, values):
        out, start = [], 0
        for value, keep in zip(values, wide):
            blocks, rows = value.shape[0], value.shape[-2]
            total = None
            for _ in range(2 if keep else 1):
                piece = payload[..., start : start + blocks * rows, :].astype(jnp.float32)
                start += blocks * rows
                piece = piece.reshape(piece.shape[:-2] + (blocks, rows, piece.shape[-1]))
                piece = jnp.moveaxis(piece, -3, 0)
                total = piece if total is None else total + piece
            out.append(total)
        return out

    for bit, axis in ((0, 4), (1, 3), (2, 2)):
        mine = my_bit(rank, bit)
        give = [lax.dynamic_index_in_dim(r, 1 - mine, axis, keepdims=False) for r in running]
        keep = [lax.dynamic_index_in_dim(r, mine, axis, keepdims=False) for r in running]
        got = decode(swap(encode(give), devices, bit), give)
        running = [k + g for k, g in zip(keep, got)]
    plane = rank // CELL
    total = [lax.dynamic_index_in_dim(r, plane, 1, keepdims=False) for r in running]
    for step in range(1, planes):
        target = (plane + step) % planes
        give = [lax.dynamic_index_in_dim(r, target, 1, keepdims=False) for r in running]
        pairs = [(i, (i + step * CELL) % devices) for i in range(devices)]
        got = decode(lax.ppermute(encode(give), "dp", pairs), give)
        total = [t + g for t, g in zip(total, got)]
    return total


def collect(rows, owners, rank, devices):
    planes = devices // CELL
    plane = rank // CELL
    stacked = jnp.stack(rows)
    pieces = [lax.dynamic_index_in_dim(stacked, jnp.clip(plane - owners[0], 0, len(owners) - 1), 0, keepdims=False)]
    for step in range(1, planes):
        target = (plane + step) % planes
        give = lax.dynamic_index_in_dim(stacked, jnp.clip(target - owners[0], 0, len(owners) - 1), 0, keepdims=False)
        pairs = [
            (i, (i + step * CELL) % devices)
            for i in range(devices)
            if ((i // CELL + step) % planes) in owners
        ]
        pieces.append(lax.ppermute(give, "dp", pairs))
    current = jnp.stack(pieces)[None]
    for bit in (2, 1, 0):
        pairs = [(i, i ^ (1 << bit)) for i in range(devices) if i // CELL in owners]
        current = jnp.concatenate([current, lax.ppermute(current, "dp", pairs)], axis=0)
    return current


def split_bf16(values):
    high = values.astype(jnp.bfloat16)
    return high, (values - high.astype(jnp.float32)).astype(jnp.bfloat16)


def dot_three(left, right, dims):
    left_high, left_low = split_bf16(left)
    right_high, right_low = split_bf16(right)

    def one(a, b):
        return lax.dot_general(a, b, (dims, ((), ())), preferred_element_type=jnp.float32)

    return one(left_high, right_high) + (one(left_low, right_high) + one(left_high, right_low))


PLAIN = ((1,), (0,))


def newton_kernel(tall_ref, stack_ref, out_ref, gram_ref, poly_ref, total_ref):
    tall = tall_ref[0] == 1
    blocks = stack_ref.shape[0]
    side = gram_ref.shape[0]
    chunk = out_ref.shape[1]

    @pl.when(tall)
    def _():
        total = jnp.zeros((side, side), jnp.float32)
        for block in range(blocks):
            values = stack_ref[block]
            total = total + dot_three(values, values, ((0,), (0,)))
        gram_ref[...] = total

    @pl.when(jnp.logical_not(tall))
    def _():
        total = jnp.zeros((side, side), jnp.float32)
        for block in range(blocks):
            values = stack_ref[block]
            total = total + dot_three(values, values, ((1,), (1,)))
        gram_ref[...] = total

    gram = gram_ref[...]
    row = lax.broadcasted_iota(jnp.int32, (side, side), 0)
    column = lax.broadcasted_iota(jnp.int32, (side, side), 1)
    eye = (row == column).astype(jnp.float32)
    norm = jnp.sqrt(jnp.sum(gram * eye)) + 1e-07
    inverse = 1.0 / norm
    gram_ref[...] = gram * (inverse * inverse)
    poly_ref[...] = eye * inverse

    def sweep(step, carry):
        gram = gram_ref[...]
        mixer = newton_first * eye + newton_second * gram + newton_third * dot_three(gram, gram, PLAIN)
        poly_ref[...] = dot_three(poly_ref[...], mixer, PLAIN)
        gram_ref[...] = dot_three(dot_three(gram, mixer, PLAIN), mixer, PLAIN)
        return carry

    lax.fori_loop(0, 5, sweep, 0)

    @pl.when(tall)
    def _():
        for block in range(blocks):
            out_ref[block] = dot_three(stack_ref[block, :chunk], poly_ref[...], PLAIN).astype(out_ref.dtype)

    @pl.when(jnp.logical_not(tall))
    def _():
        for block in range(blocks):
            out_ref[block] = dot_three(poly_ref[:chunk], stack_ref[block], PLAIN).astype(out_ref.dtype)


def newton_rows(stack, tall, chunk):
    blocks, side, lanes = stack.shape
    return pl.pallas_call(
        newton_kernel,
        out_shape=jax.ShapeDtypeStruct((blocks, chunk, lanes), jnp.bfloat16),
        in_specs=[
            pl.BlockSpec(memory_space=pltpu.SMEM),
            pl.BlockSpec(memory_space=pltpu.VMEM),
        ],
        out_specs=pl.BlockSpec(memory_space=pltpu.VMEM),
        scratch_shapes=[pltpu.VMEM((side, side), jnp.float32)] * 3,
        compiler_params=pltpu.CompilerParams(vmem_limit_bytes=48 << 20),
    )(tall, stack)


PAD_TOK = 64
KEY_ROWS = 56
PAD_IMG = 256
GROUPS = 4
NEVER = -1e30
f32 = jnp.float32
bf16 = jnp.bfloat16


def window_matrix():
    table = np.zeros((PAD_IMG, PATCHES), np.float32)
    blocks = SIDE // WIN
    for window in range(blocks * blocks):
        for token in range(WIN_TOK):
            row = (window // blocks) * WIN + token // WIN
            column = (window % blocks) * WIN + token % WIN
            patch = ((row + SHIFT) % SIDE) * SIDE + (column + SHIFT) % SIDE
            table[window * PAD_TOK + token, patch] = 1.0
    return table


def dot(left, right, left_dim=1, right_dim=0):
    return lax.dot_general(
        left, right, (((left_dim,), (right_dim,)), ((), ())), preferred_element_type=jnp.float32
    )


def normalize(values):
    center = values - jnp.mean(values, axis=-1, keepdims=True)
    spread = jnp.mean(center * center, axis=-1, keepdims=True)
    factor = lax.rsqrt(spread + 1e-05)
    return center * factor, factor


def normalize_back(grad, gain, hat, factor):
    inner = grad * gain
    return factor * (
        inner
        - jnp.mean(inner, axis=-1, keepdims=True)
        - hat * jnp.mean(inner * hat, axis=-1, keepdims=True)
    )


def head_masks(dtype):
    lane = lax.broadcasted_iota(jnp.int32, (1, 128), 1) // 32
    return [(lane == head).astype(dtype) for head in range(GROUPS)]


def spread_heads(rows, masks):
    return jnp.concatenate([rows * mask for mask in masks], axis=0)


def fold_heads(blocks, masks):
    total = None
    for head, mask in enumerate(masks):
        part = blocks[head * PAD_TOK : (head + 1) * PAD_TOK] * mask
        total = part if total is None else total + part
    return total


def load_image(ref, image, slots):
    return jnp.concatenate([ref[lane, pl.ds(image, PATCHES, stride=slots), :] for lane in range(ref.shape[0])], axis=1)


def store_image(ref, image, slots, values):
    for lane in range(ref.shape[0]):
        ref[lane, pl.ds(image, PATCHES, stride=slots), :] = values[:, lane * 128 : (lane + 1) * 128]


def cut_lanes(ref, values):
    for lane in range(ref.shape[0]):
        ref[lane] = values[:, lane * 128 : (lane + 1) * 128]


def join_lanes(ref):
    return jnp.concatenate([ref[lane] for lane in range(ref.shape[0])], axis=1)


def attend_kernel(
    images_ref, weights_ref, gains_ref, shifts_ref, biases_ref, combined_ref, take_ref, put_ref,
    windows_ref, triple_ref, attention_ref, mixed_ref, middle_ref, features_ref, scratch_ref,
):
    image = pl.program_id(0)
    width = images_ref.shape[-1]
    slots = images_ref.shape[0] // PATCHES
    scale = 1.0 / math.sqrt(width // HEADS)

    @pl.when(image == 0)
    def _():
        cut_lanes(features_ref, images_ref[...].astype(f32))

    features = load_image(features_ref, image, slots)
    hat, _ = normalize(features)
    normed = (hat * gains_ref[0:1] + shifts_ref[0:1]).astype(bf16)
    windows = dot(take_ref[...], normed).astype(bf16)
    windows_ref[0] = windows
    for part in range(3):
        columns = slice(part * width, (part + 1) * width)
        values = dot(windows, weights_ref[part]) + biases_ref[0:1, columns]
        if part == 0:
            values = values * scale
        triple_ref[0, :, columns] = values.astype(bf16)
    masks = head_masks(bf16)
    masks_wide = head_masks(f32)
    for window in range(4):
        rows = slice(window * PAD_TOK, (window + 1) * PAD_TOK)
        for group in range(GROUPS):
            lanes = slice(group * 128, (group + 1) * 128)
            query = triple_ref[0, rows, group * 128 : (group + 1) * 128]
            key = triple_ref[0, rows, width + group * 128 : width + (group + 1) * 128]
            value = triple_ref[0, rows, 2 * width + group * 128 : 2 * width + (group + 1) * 128]
            scores = dot(key, spread_heads(query, masks), 1, 1)[:KEY_ROWS] + combined_ref[window, group]
            top = jnp.max(scores, axis=0, keepdims=True)
            raised = jnp.exp(scores - top)
            attention = raised * (1.0 / jnp.sum(raised, axis=0, keepdims=True))
            attention_ref[0, window, group] = attention
            low = jnp.concatenate([attention, jnp.zeros((PAD_TOK - KEY_ROWS, attention.shape[1]), f32)], axis=0).astype(bf16)
            out = dot(low, value, 0, 0)
            scratch_ref[rows, lanes] = fold_heads(out, masks_wide).astype(bf16)
    mixed = dot(put_ref[...], scratch_ref[...])
    store_image(mixed_ref, image, slots, mixed)
    branch = dot(mixed.astype(bf16), weights_ref[3]) + biases_ref[0:1, 3 * width : 4 * width]
    store_image(middle_ref, image, slots, features + branch)


def whole(shape):
    return pl.BlockSpec(shape, lambda i: (0,) * len(shape))


def one(shape):
    return pl.BlockSpec((1,) + shape, lambda i: (i,) + (0,) * len(shape))


def attend_forward(images, weights, gains, shifts, biases, combined, take, put):
    rows, width = images.shape
    slots = rows // PATCHES
    return pl.pallas_call(
        attend_kernel,
        grid=(slots,),
        in_specs=[
            whole(images.shape), whole(weights.shape), whole(gains.shape), whole(shifts.shape),
            whole(biases.shape), whole(combined.shape), whole(take.shape), whole(put.shape),
        ],
        out_specs=[
            one((PAD_IMG, width)), one((PAD_IMG, 3 * width)), one((4, GROUPS, KEY_ROWS, 256)),
            whole((width // 128, rows, 128)), whole((width // 128, rows, 128)),
        ],
        out_shape=[
            jax.ShapeDtypeStruct((slots, PAD_IMG, width), bf16),
            jax.ShapeDtypeStruct((slots, PAD_IMG, 3 * width), bf16),
            jax.ShapeDtypeStruct((slots, 4, GROUPS, KEY_ROWS, 256), f32),
            jax.ShapeDtypeStruct((width // 128, rows, 128), f32),
            jax.ShapeDtypeStruct((width // 128, rows, 128), f32),
        ],
        scratch_shapes=[pltpu.VMEM((width // 128, rows, 128), f32), pltpu.VMEM((PAD_IMG, width), bf16)],
        compiler_params=pltpu.CompilerParams(vmem_limit_bytes=56 << 20),
        name="attend_forward",
    )(images, weights, gains, shifts, biases, combined, take, put)


def gelu_parts(values):
    size = jnp.abs(values) * math.sqrt(0.5)
    bell = jnp.exp(-0.5 * values * values)
    turn = 1.0 / (1.0 + 0.3275911 * size)
    tail = 1.061405429
    for factor in (-1.453152027, 1.421413741, -0.284496736, 0.254829592):
        tail = tail * turn + factor
    tail = 0.5 * tail * turn * bell
    share = jnp.where(values < 0.0, tail, 1.0 - tail)
    return share, values * bell * (1.0 / math.sqrt(2.0 * math.pi))


def feed_kernel(
    count_ref, middle_ref, cotangent_ref, mixed_ref, expand_ref, project_ref, gains_ref, shifts_ref, biases_ref,
    block_ref, project_grad_ref, expand_grad_ref, merge_grad_ref, grad_middle_ref, sums_ref, hidden_sums_ref, *, slots,
):
    step = pl.program_id(0)
    rows, width = cotangent_ref.shape
    pieces, _, piece = expand_ref.shape
    hidden = pieces * piece
    middle = join_lanes(middle_ref)
    slot = lax.broadcasted_iota(jnp.int32, (rows, 1), 0) % slots
    live = slot < count_ref[0]

    @pl.when(step == 0)
    def _():
        project_grad_ref[...] = jnp.zeros_like(project_grad_ref)
        expand_grad_ref[...] = jnp.zeros_like(expand_grad_ref)
        merge_grad_ref[...] = jnp.zeros_like(merge_grad_ref)
        sums_ref[...] = jnp.zeros_like(sums_ref)
        hidden_sums_ref[...] = jnp.zeros_like(hidden_sums_ref)

    hat, factor = normalize(middle)
    gain = gains_ref[1:2]
    normed = (hat * gain + shifts_ref[1:2]).astype(bf16)
    grad_out = jnp.where(live, cotangent_ref[...].astype(f32), 0.0)
    grad_low = grad_out.astype(bf16)
    out = biases_ref[0:1, 4 * width + hidden : 5 * width + hidden]
    back = 0.0
    for index in range(pieces):
        columns = slice(index * piece, (index + 1) * piece)
        offset = 4 * width + index * piece
        pre = dot(normed, expand_ref[index]) + biases_ref[0:1, offset : offset + piece]
        share, slope = gelu_parts(pre)
        active = (pre * share).astype(bf16)
        out = out + dot(active, project_ref[columns])
        project_grad_ref[columns] += dot(active, grad_low, 0, 0)
        grad_pre = (dot(grad_low, project_ref[columns], 1, 1) * (share + slope)).astype(bf16)
        expand_grad_ref[index] += dot(normed, grad_pre, 0, 0)
        hidden_sums_ref[0:1, columns] += jnp.sum(grad_pre.astype(f32), axis=0, keepdims=True)
        back = back + dot(grad_pre, expand_ref[index], 1, 1)
    block_ref[...] = jnp.where(live, middle + out, 0.0).astype(bf16)
    grad_middle = grad_out + normalize_back(back, gain, hat, factor)
    cut_lanes(grad_middle_ref, grad_middle)
    grad_branch = grad_middle.astype(bf16)
    merge_grad_ref[...] += dot(join_lanes(mixed_ref).astype(bf16), grad_branch, 0, 0)
    sums_ref[0:1] += jnp.sum(back * hat, axis=0, keepdims=True)
    sums_ref[1:2] += jnp.sum(back, axis=0, keepdims=True)
    sums_ref[2:3] += jnp.sum(grad_out, axis=0, keepdims=True)
    sums_ref[3:4] += jnp.sum(grad_branch.astype(f32), axis=0, keepdims=True)


def feed_forward(count, middle, cotangent, mixed, expand, project, gains, shifts, biases, slots, tile):
    rows, width = cotangent.shape
    hidden = project.shape[0]
    lanes = pl.BlockSpec((width // 128, tile, 128), lambda i: (0, i, 0))

    def tiled(columns):
        return pl.BlockSpec((tile, columns), lambda i: (i, 0))

    return pl.pallas_call(
        partial(feed_kernel, slots=slots),
        grid=(rows // tile,),
        in_specs=[
            pl.BlockSpec(memory_space=pltpu.SMEM), lanes, tiled(width), lanes, whole(expand.shape),
            whole(project.shape), whole(gains.shape), whole(shifts.shape), whole(biases.shape),
        ],
        out_specs=[
            tiled(width), whole((hidden, width)), whole(expand.shape), whole((width, width)), lanes,
            whole((8, width)), whole((8, hidden)),
        ],
        out_shape=[
            jax.ShapeDtypeStruct((rows, width), bf16),
            jax.ShapeDtypeStruct((hidden, width), f32),
            jax.ShapeDtypeStruct(expand.shape, f32),
            jax.ShapeDtypeStruct((width, width), f32),
            jax.ShapeDtypeStruct((width // 128, rows, 128), f32),
            jax.ShapeDtypeStruct((8, width), f32),
            jax.ShapeDtypeStruct((8, hidden), f32),
        ],
        compiler_params=pltpu.CompilerParams(vmem_limit_bytes=60 << 20),
        name="feed_forward",
    )(count, middle, cotangent, mixed, expand, project, gains, shifts, biases)


def attend_back_kernel(
    grad_middle_ref, weights_ref, triple_ref, attention_ref, windows_ref, take_ref,
    attend_grad_ref, grad_triple_ref, table_ref, sums_ref,
):
    step = pl.program_id(0)
    width = weights_ref.shape[-1]
    slots = grad_middle_ref.shape[1] // PATCHES
    scale = 1.0 / math.sqrt(width // HEADS)

    @pl.when(step == 0)
    def _():
        attend_grad_ref[...] = jnp.zeros_like(attend_grad_ref)
        table_ref[...] = jnp.zeros_like(table_ref)
        sums_ref[...] = jnp.zeros_like(sums_ref)

    grad_branch = load_image(grad_middle_ref, step, slots).astype(bf16)
    grad_mixed = dot(grad_branch, weights_ref[0], 1, 1).astype(bf16)
    grad_mixed = dot(take_ref[...], grad_mixed).astype(bf16)
    masks = head_masks(bf16)
    masks_wide = head_masks(f32)
    pad = jnp.zeros((PAD_TOK - KEY_ROWS, 256), f32)
    for group in range(GROUPS):
        table = table_ref[group]
        for window in range(4):
            rows = slice(window * PAD_TOK, (window + 1) * PAD_TOK)
            query = triple_ref[0, rows, group * 128 : (group + 1) * 128]
            key = triple_ref[0, rows, width + group * 128 : width + (group + 1) * 128]
            value = triple_ref[0, rows, 2 * width + group * 128 : 2 * width + (group + 1) * 128]
            grad_heads = spread_heads(grad_mixed[rows, group * 128 : (group + 1) * 128], masks)
            attention = attention_ref[0, window, group]
            grad_attention = dot(value, grad_heads, 1, 1)[:KEY_ROWS]
            inner = jnp.sum(grad_attention * attention, axis=0, keepdims=True)
            grad_scores = attention * (grad_attention - inner)
            low = jnp.concatenate([grad_scores, pad], axis=0).astype(bf16)
            table = table + low.astype(f32)[:KEY_ROWS]
            attention_low = jnp.concatenate([attention, pad], axis=0).astype(bf16)
            grad_value = dot(attention_low, grad_heads)
            grad_key = dot(low, spread_heads(query, masks))
            grad_query = fold_heads(dot(low, key, 0, 0), masks_wide) * scale
            grad_triple_ref[0, rows, group * 128 : (group + 1) * 128] = grad_query.astype(bf16)
            grad_triple_ref[0, rows, width + group * 128 : width + (group + 1) * 128] = grad_key.astype(bf16)
            grad_triple_ref[0, rows, 2 * width + group * 128 : 2 * width + (group + 1) * 128] = grad_value.astype(bf16)
        table_ref[group] = table
    for part in range(3):
        columns = slice(part * width, (part + 1) * width)
        grad = grad_triple_ref[0, :, columns]
        attend_grad_ref[part] += dot(windows_ref[0], grad, 0, 0)
        sums_ref[0:1, columns] += jnp.sum(grad.astype(f32), axis=0, keepdims=True)


def attend_backward(grad_middle, weights, triple, attention, windows, take):
    width = weights.shape[-1]
    slots = triple.shape[0]
    return pl.pallas_call(
        attend_back_kernel,
        grid=(slots,),
        in_specs=[
            whole(grad_middle.shape), pl.BlockSpec((1, width, width), lambda i: (3, 0, 0)), one((PAD_IMG, 3 * width)),
            one((4, GROUPS, KEY_ROWS, 256)), one((PAD_IMG, width)), whole(take.shape),
        ],
        out_specs=[
            whole((3, width, width)), one((PAD_IMG, 3 * width)), whole((GROUPS, KEY_ROWS, 256)), whole((8, 3 * width)),
        ],
        out_shape=[
            jax.ShapeDtypeStruct((3, width, width), f32),
            jax.ShapeDtypeStruct((slots, PAD_IMG, 3 * width), bf16),
            jax.ShapeDtypeStruct((GROUPS, KEY_ROWS, 256), f32),
            jax.ShapeDtypeStruct((8, 3 * width), f32),
        ],
        compiler_params=pltpu.CompilerParams(vmem_limit_bytes=56 << 20),
        name="attend_backward",
    )(grad_middle, weights, triple, attention, windows, take)


def input_kernel(images_ref, grad_triple_ref, grad_middle_ref, weights_ref, gains_ref, put_ref, out_ref, sums_ref, features_ref, grads_ref):
    step = pl.program_id(0)
    width = images_ref.shape[-1]
    slots = images_ref.shape[0] // PATCHES

    @pl.when(step == 0)
    def _():
        sums_ref[...] = jnp.zeros_like(sums_ref)
        cut_lanes(features_ref, images_ref[...].astype(f32))

    hat, factor = normalize(load_image(features_ref, step, slots))
    grad = 0.0
    for part in range(3):
        grad = grad + dot(grad_triple_ref[0, :, part * width : (part + 1) * width], weights_ref[part], 1, 1)
    high = grad.astype(bf16)
    low = (grad - high.astype(f32)).astype(bf16)
    grad = dot(put_ref[...], high) + dot(put_ref[...], low)
    total = load_image(grad_middle_ref, step, slots) + normalize_back(grad, gains_ref[0:1], hat, factor)
    store_image(grads_ref, step, slots, total)
    sums_ref[0:1] += jnp.sum(grad * hat, axis=0, keepdims=True)
    sums_ref[1:2] += jnp.sum(grad, axis=0, keepdims=True)

    @pl.when(step == slots - 1)
    def _():
        out_ref[...] = join_lanes(grads_ref)


def input_backward(images, grad_triple, grad_middle, weights, gains, put):
    rows, width = images.shape
    slots = rows // PATCHES
    return pl.pallas_call(
        input_kernel,
        grid=(slots,),
        in_specs=[
            whole((rows, width)), one((PAD_IMG, 3 * width)), whole(grad_middle.shape),
            pl.BlockSpec((3, width, width), lambda i: (0, 0, 0)), whole(gains.shape), whole(put.shape),
        ],
        out_specs=[whole((rows, width)), whole((8, width))],
        out_shape=[
            jax.ShapeDtypeStruct((rows, width), f32),
            jax.ShapeDtypeStruct((8, width), f32),
        ],
        scratch_shapes=[pltpu.VMEM((width // 128, rows, 128), f32)] * 2,
        compiler_params=pltpu.CompilerParams(vmem_limit_bytes=56 << 20),
        name="input_backward",
    )(images, grad_triple, grad_middle, weights, gains, put)


def combine_bias(bias_table, rel_index, shift_mask):
    one_hot = (rel_index.reshape(-1)[:, None] == jnp.arange(TABLE)[None, :]).astype(f32)
    position = jnp.dot(one_hot, bias_table, precision=lax.Precision.HIGHEST).T
    position = position.reshape(GROUPS, 4, WIN_TOK, WIN_TOK)
    position = jnp.transpose(position, (0, 3, 1, 2))
    position = jnp.pad(
        position, ((0, 0), (0, KEY_ROWS - WIN_TOK), (0, 0), (0, PAD_TOK - WIN_TOK))
    ).reshape(GROUPS, KEY_ROWS, 256)
    mask = jnp.transpose(-100.0 * (1 - shift_mask).astype(f32), (0, 2, 1))
    mask = jnp.pad(mask, ((0, 0), (0, 0), (0, PAD_TOK - WIN_TOK)))
    mask = jnp.pad(mask, ((0, 0), (0, KEY_ROWS - WIN_TOK), (0, 0)), constant_values=NEVER)
    mask = jnp.tile(mask, (1, 1, 4))
    return position[None] + mask[:, None], one_hot


def table_gradient(table, one_hot):
    grad = table.reshape(GROUPS, KEY_ROWS, 4, PAD_TOK)[:, :WIN_TOK, :, :WIN_TOK]
    grad = jnp.transpose(grad, (3, 1, 0, 2)).reshape(WIN_TOK * WIN_TOK, HEADS)
    return jnp.dot(one_hot.T, grad, precision=lax.Precision.HIGHEST)


def flat_rows(images):
    return jnp.transpose(images, (1, 0, 2)).reshape(-1, images.shape[-1])


def image_form(rows, slots):
    return jnp.transpose(rows.reshape(-1, slots, rows.shape[-1]), (1, 0, 2))


def adamw_step(param, grad, first, second, steps):
    first_next = 0.9 * first + 0.1 * grad
    second_next = 0.999 * second + 0.001 * grad * grad
    first_hat = first_next / (1.0 - jnp.power(0.9, steps))
    second_hat = second_next / (1.0 - jnp.power(0.999, steps))
    update = -0.05 * (first_hat / (jnp.sqrt(second_hat) + 1e-08) + 0.05 * param)
    return (first_next, second_next, update)


def column_blocks(matrix):
    rows, columns = matrix.shape
    return jnp.transpose(matrix.reshape(rows, columns // LANE, LANE), (1, 0, 2))


def from_blocks(blocks):
    count, rows, lanes = blocks.shape
    return jnp.transpose(blocks, (1, 0, 2)).reshape(rows, count * lanes)


def owner_form(moment, largest):
    flat = column_blocks(moment).reshape(-1, LANE)
    rows = largest - flat.shape[0]
    return jnp.pad(flat, ((0, rows), (0, 0))).reshape(4, -1, LANE)


def sum_small(parts, devices):
    flat = jnp.concatenate([part.reshape(-1) for part in parts])
    size = flat.shape[0]
    total = jnp.pad(flat, (0, -size % 1024)).reshape(-1, 128)
    for bit in range(device_bits(devices)):
        total = total + swap(total, devices, bit)
    flat, out, start = total.reshape(-1), [], 0
    for part in parts:
        out.append(flat[start : start + part.size].reshape(part.shape))
        start += part.size
    return out


def local(
    images,
    cotangent,
    image_counts,
    shift_mask,
    rel_index,
    step_count,
    attend_weight,
    merge_weight,
    expand_weight,
    project_weight,
    norm_gains,
    norm_shifts,
    layer_biases,
    bias_table,
    attend_momentum,
    merge_momentum,
    expand_momentum,
    project_momentum,
    gains_mean,
    gains_square,
    shifts_mean,
    shifts_square,
    biases_mean,
    biases_square,
    table_mean,
    table_square,
):
    slots, patches, width = images.shape
    devices = lax.axis_size("dp")
    hidden_units = expand_weight.shape[1]
    grad_scale = 1.0 / math.sqrt(slots * devices * PATCHES)
    rank = lax.axis_index("dp")
    planes = devices // CELL
    first = jnp.concatenate([column_blocks(attend_weight), column_blocks(merge_weight)])
    weights = gather_rows(first, rank, devices)
    expand = gather_rows(column_blocks(expand_weight), rank, devices)
    project = gather_rows(project_weight[None], rank, devices)[0]
    take = jnp.asarray(window_matrix(), bf16)
    put = jnp.asarray(window_matrix().T, bf16)
    combined, one_hot = combine_bias(bias_table, rel_index, shift_mask)
    bias_row = layer_biases.reshape(1, -1)
    rows = flat_rows(images)
    windows, triple, attention, mixed, middle = attend_forward(
        rows, weights, norm_gains, norm_shifts, bias_row, combined, take, put
    )
    block_rows, project_term, expand_term, merge_term, grad_middle, feed_sums, hidden_sums = feed_forward(
        image_counts, middle, flat_rows(cotangent), mixed, expand, project, norm_gains, norm_shifts, bias_row, slots,
        slots * patches // 4,
    )
    block_out = image_form(block_rows, slots)
    merge_sum, expand_sum, project_sum = reduce_rows(
        [
            merge_term.reshape(1, devices, -1, LANE),
            expand_term.reshape(expand_term.shape[0], devices, -1, LANE),
            project_term.reshape(1, devices, -1, LANE),
        ],
        (True, False, False),
        rank,
        devices,
    )
    attend_term, grad_triple, table_sums, triple_sums = attend_backward(
        grad_middle, weights, triple, attention, windows, take
    )
    (attend_sum,) = reduce_rows(
        [attend_term.reshape(attend_term.shape[0], devices, -1, LANE)], (False,), rank, devices
    )
    input_rows, input_sums = input_backward(rows, grad_triple, grad_middle, weights, norm_gains, put)
    input_grad = image_form(input_rows, slots)
    table_term = table_gradient(table_sums, one_hot)
    small_parts = (
        jnp.stack([input_sums[0], feed_sums[0]]),
        jnp.stack([input_sums[1], feed_sums[1]]),
        jnp.concatenate([triple_sums[0], feed_sums[3], hidden_sums[0], feed_sums[2]]),
        table_term,
    )
    small_sums = sum_small(small_parts, devices)
    mat_sums = tuple(from_blocks(term) for term in (attend_sum, merge_sum, expand_sum, project_sum))
    mat_grads = tuple((term * grad_scale for term in mat_sums))
    small_grads = tuple((term * grad_scale for term in small_sums))
    momenta = (attend_momentum, merge_momentum, expand_momentum, project_momentum)
    momenta_next = tuple((0.95 * moment + grad for moment, grad in zip(momenta, mat_grads)))
    largest = project_momentum.shape[0]
    packed = [owner_form(moment, largest) for moment in momenta_next]
    rest = collect(packed[1:], (1, 2, 3), rank, devices)
    head = collect(packed[:1], (0,), rank, devices)
    plane = rank // CELL
    whole = jnp.where(plane == 0, head, rest)
    stack = jnp.transpose(whole, (2, 0, 1, 3, 4)).reshape(4, -1, LANE)
    tall = (plane == 3).astype(jnp.int32).reshape(1)
    chunk = planes * packed[0].shape[1]
    orth = newton_rows(stack, tall, chunk).reshape(4, planes, -1, LANE)
    pieces = []
    for step in range(planes):
        give = orth[:, (planes - step) % planes]
        if step:
            pairs = [(i, (i + step * CELL) % devices) for i in range(devices) if i // CELL < 4]
            give = lax.ppermute(give, "dp", pairs)
        pieces.append(give)
    received = jnp.stack(pieces)
    orth_rows = []
    for order, moment in enumerate(momenta_next):
        piece = lax.dynamic_index_in_dim(received, (plane - order) % planes, 0, keepdims=False)
        blocks, rows = max(moment.shape[1] // LANE, 1), moment.shape[0]
        piece = piece.reshape(-1, LANE)[: blocks * rows].reshape(blocks, rows, LANE)
        orth_rows.append(from_blocks(piece).astype(f32))
    results = [block_out, input_grad]
    for grad, moment_next, orth_part in zip(mat_grads, momenta_next, orth_rows):
        extent = max(devices * moment_next.shape[0], moment_next.shape[1])
        update = -0.02 * math.sqrt(extent) * orth_part
        results += [grad, moment_next, update]
    steps = step_count[0].astype(f32)
    params = (norm_gains, norm_shifts, layer_biases, bias_table)
    states = (
        (gains_mean, gains_square),
        (shifts_mean, shifts_square),
        (biases_mean, biases_square),
        (table_mean, table_square),
    )
    for param, grad, state in zip(params, small_grads, states):
        first_next, second_next, update = adamw_step(param, grad, state[0], state[1], steps)
        results += [grad, first_next, second_next, update]
    return tuple(results)


def solution(mesh):
    return jax.shard_map(
        local,
        mesh=mesh,
        in_specs=(
            P("dp", None, None),
            P("dp", None, None),
            P("dp"),
            P(),
            P(),
            P(),
            P("dp", None),
            P("dp", None),
            P("dp", None),
            P("dp", None),
            P(),
            P(),
            P(),
            P(),
            P("dp", None),
            P("dp", None),
            P("dp", None),
            P("dp", None),
            P(),
            P(),
            P(),
            P(),
            P(),
            P(),
            P(),
            P(),
        ),
        out_specs=(
            P("dp", None, None),
            P("dp", None, None),
            P("dp", None),
            P("dp", None),
            P("dp", None),
            P("dp", None),
            P("dp", None),
            P("dp", None),
            P("dp", None),
            P("dp", None),
            P("dp", None),
            P("dp", None),
            P("dp", None),
            P("dp", None),
            P(),
            P(),
            P(),
            P(),
            P(),
            P(),
            P(),
            P(),
            P(),
            P(),
            P(),
            P(),
            P(),
            P(),
            P(),
            P(),
        ),
        check_vma=False,
    )
```

```python
from functools import partial
import math

import jax
import jax.numpy as jnp
import numpy as np
from jax import lax
from jax.experimental import pallas as pl
from jax.experimental.pallas import tpu as pltpu
from jax.sharding import PartitionSpec as P

HEADS = 16
WIN = 7
SIDE = 14
SHIFT = 3
WIN_TOK = 49
PATCHES = 196
TABLE = 169


newton_first = 3.4445
newton_second = -4.775
newton_third = 2.0315


LANE = 512
CELL = 8
MATRICES = 4


def exchange(payload, devices, mask):
    return lax.ppermute(payload, "dp", [(i, i ^ mask) for i in range(devices)])


def pick(values, index, axis):
    return lax.dynamic_index_in_dim(values, index, axis, keepdims=False)


def split_wide(values):
    high = lax.reduce_precision(values, 8, 7)
    return high.astype(jnp.bfloat16), lax.reduce_precision(values - high, 8, 7).astype(jnp.bfloat16)


def join_wide(high, low):
    return high.astype(jnp.float32) + low.astype(jnp.float32)


def order_kernel(rank_ref, near_ref, far_ref, *out_refs, spans):
    rank = rank_ref[0]
    corners, planes = near_ref.shape[:2]
    for core, source in enumerate((near_ref, far_ref)):
        for corner in range(corners):
            for plane in range(planes):
                owner = jnp.bitwise_xor(rank, core + 2 * corner + CELL * plane)
                start = 0
                for out_ref, (blocks, rows) in zip(out_refs, spans):
                    place = pl.ds(pl.multiple_of(owner * rows, rows), rows)
                    for block in range(blocks):
                        out_ref[block, place, :] = source[corner, plane, start : start + rows, :]
                        start += rows


def order_rows(near, far, spans, rank):
    corners, planes, _, lanes = near.shape
    devices = 2 * corners * planes
    shapes = [(blocks, devices * rows, lanes) for blocks, rows in spans]
    if all(rows % 16 == 0 for _, rows in spans):
        return pl.pallas_call(
            partial(order_kernel, spans=spans),
            out_shape=[jax.ShapeDtypeStruct(shape, near.dtype) for shape in shapes],
            in_specs=[pl.BlockSpec(memory_space=pltpu.SMEM)] + [pl.BlockSpec(memory_space=pltpu.VMEM)] * 2,
            out_specs=[pl.BlockSpec(memory_space=pltpu.VMEM)] * len(shapes),
            compiler_params=pltpu.CompilerParams(vmem_limit_bytes=32 << 20),
            cost_estimate=pl.CostEstimate(flops=0, bytes_accessed=4 * near.size * 2, transcendentals=0),
            name="order_rows",
        )(rank.reshape(1), near, far)
    both = jnp.stack([near, far]).reshape(devices, -1, lanes)
    offset = jnp.arange(devices) ^ rank
    both = jnp.take(both, (offset & 1) * (corners * planes) + ((offset >> 1) & 3) * planes + (offset >> 3), axis=0)
    out, start = [], 0
    for (blocks, rows), shape in zip(spans, shapes):
        part = both[:, start : start + blocks * rows].reshape(devices, blocks, rows, lanes)
        out.append(jnp.transpose(part, (1, 0, 2, 3)).reshape(shape))
        start += blocks * rows
    return out


def gather_planes(rows, devices):
    return [rows] + [exchange(rows, devices, CELL * step) for step in range(1, devices // CELL)]


def gather_corners(rows, devices):
    return [rows] + [exchange(rows, devices, 2 * step) for step in range(1, 4)]


def encode(values, wide):
    sent = []
    for value, keep in zip(values, wide):
        for piece in split_wide(value) if keep else (value.astype(jnp.bfloat16),):
            flat = jnp.moveaxis(piece, 0, -3)
            sent.append(flat.reshape(flat.shape[:-3] + (-1, flat.shape[-1])))
    return jnp.concatenate(sent, axis=-2)


def decode(payload, values, wide):
    out, start = [], 0
    for value, keep in zip(values, wide):
        blocks, rows = value.shape[0], value.shape[-2]
        total = None
        for _ in range(2 if keep else 1):
            piece = payload[..., start : start + blocks * rows, :].astype(jnp.float32)
            start += blocks * rows
            piece = piece.reshape(piece.shape[:-2] + (blocks, rows, piece.shape[-1]))
            piece = jnp.moveaxis(piece, -3, 0)
            total = piece if total is None else total + piece
        out.append(total)
    return out


def reduce_core(parts, wide, rank, devices):
    running = [part.reshape(part.shape[0], devices // 2, 2, part.shape[2], LANE) for part in parts]
    mine = rank & 1
    give = [pick(r, 1 - mine, 2) for r in running]
    payload = exchange(encode(give, wide), devices, 1)
    return [pick(r, mine, 2) + g for r, g in zip(running, decode(payload, give, wide))]


def reduce_sent(parts, wide, own, count, axis, mask, devices):
    got = []
    for step in range(1, count):
        give = [pick(r, own ^ step, axis) for r in parts]
        got.append((exchange(encode(give, wide), devices, mask * step), give))
    return got


def reduce_added(parts, wide, own, axis, got):
    total = [pick(r, own, axis) for r in parts]
    for payload, give in got:
        total = [t + g for t, g in zip(total, decode(payload, give, wide))]
    return total


def by_corner(parts, devices):
    return [part.reshape(part.shape[0], devices // CELL, 4, part.shape[-2], LANE) for part in parts]


def newton_kernel(kind_ref, stack_ref, out_ref, gram_ref, rows_ref):
    kind = kind_ref[0]
    blocks, side, _ = stack_ref.shape
    chunk = out_ref.shape[1]
    tall = kind == 3
    paired = kind == 1

    @pl.when(tall)
    def _():
        total = dot(stack_ref[0], stack_ref[0], 0, 0)
        for block in range(1, blocks):
            total = total + dot(stack_ref[block], stack_ref[block], 0, 0)
        gram_ref[...] = total

    @pl.when(paired)
    def _():
        cross = dot(stack_ref[0], stack_ref[1], 1, 1)
        cross = cross + dot(stack_ref[1], stack_ref[0], 1, 1)
        gram_ref[...] = dot(stack_ref[0], stack_ref[0], 1, 1) + cross

    @pl.when(jnp.logical_not(jnp.logical_or(tall, paired)))
    def _():
        total = dot(stack_ref[0], stack_ref[0], 1, 1)
        for block in range(1, blocks):
            total = total + dot(stack_ref[block], stack_ref[block], 1, 1)
        gram_ref[...] = total

    row = lax.broadcasted_iota(jnp.int32, (side, side), 0)
    column = lax.broadcasted_iota(jnp.int32, (side, side), 1)
    eye = (row == column).astype(jnp.float32)
    gram = gram_ref[...]
    inverse = 1.0 / (jnp.sqrt(jnp.sum(gram * eye)) + 1e-07)
    gram_ref[...] = gram * (inverse * inverse)

    @pl.when(tall)
    def _():
        for block in range(blocks):
            rows_ref[block * chunk : (block + 1) * chunk] = stack_ref[block, :chunk].astype(jnp.float32) * inverse

    @pl.when(jnp.logical_not(tall))
    def _():
        rows_ref[...] = eye[: blocks * chunk] * inverse

    def halves(values):
        high = values.astype(jnp.bfloat16)
        return high, (values - high.astype(jnp.float32)).astype(jnp.bfloat16)

    def product(left, right):
        return dot(left[0], right[0]) + (dot(left[1], right[0]) + dot(left[0], right[1]))

    def mix(gram, parts):
        return halves(newton_first * eye + newton_second * gram + newton_third * product(parts, parts))

    def sweep(step, carry):
        gram = gram_ref[...]
        parts = halves(gram)
        mixer = mix(gram, parts)
        rows_ref[...] = product(halves(rows_ref[...]), mixer)
        gram_ref[...] = product(halves(product(parts, mixer)), mixer)
        return carry

    lax.fori_loop(0, 4, sweep, 0)
    gram = gram_ref[...]
    rows = product(halves(rows_ref[...]), mix(gram, halves(gram)))

    @pl.when(tall)
    def _():
        for block in range(blocks):
            out_ref[block] = rows[block * chunk : (block + 1) * chunk].astype(out_ref.dtype)

    @pl.when(jnp.logical_not(tall))
    def _():
        own = halves(rows[:chunk])
        first = dot(own[0], stack_ref[0]) + dot(own[1], stack_ref[0])
        second = dot(own[0], stack_ref[1])
        out_ref[0] = jnp.where(paired, first + second, first).astype(out_ref.dtype)
        out_ref[1] = (second + dot(own[1], stack_ref[1])).astype(out_ref.dtype)
        for block in range(2, blocks):
            out_ref[block] = (dot(own[0], stack_ref[block]) + dot(own[1], stack_ref[block])).astype(out_ref.dtype)


def newton_rows(stack, kind, chunk):
    blocks, side, lanes = stack.shape
    return pl.pallas_call(
        newton_kernel,
        out_shape=jax.ShapeDtypeStruct((blocks, chunk, lanes), jnp.bfloat16),
        in_specs=[
            pl.BlockSpec(memory_space=pltpu.SMEM),
            pl.BlockSpec(memory_space=pltpu.VMEM),
        ],
        out_specs=pl.BlockSpec(memory_space=pltpu.VMEM),
        scratch_shapes=[pltpu.VMEM((side, side), jnp.float32), pltpu.VMEM((blocks * chunk, side), jnp.float32)],
        compiler_params=pltpu.CompilerParams(vmem_limit_bytes=48 << 20),
        cost_estimate=pl.CostEstimate(flops=20 * 10**9, bytes_accessed=1 << 22, transcendentals=0),
        name="newton_rows",
    )(kind, stack)


def pad_rows(rows, length):
    return jnp.pad(rows, ((0, length - rows.shape[0]), (0, 0)))


def add_tree(values):
    while len(values) > 1:
        values = [left + right for left, right in zip(values[::2], values[1::2])]
    return values[0]


def collect(packed, small, rank, devices):
    planes = devices // CELL
    plane = rank // CELL
    rows = packed.shape[1]
    count = small.shape[0]

    def pair(values):
        high, low = split_wide(values)
        return jnp.concatenate([high, low])

    def value(sent):
        return join_wide(sent[:count], sent[count:])

    sent = pair(small)
    pieces, sums = [pick(packed, jnp.minimum(plane, MATRICES - 1), 0)], [value(sent)]
    for step in range(1, planes):
        give = pick(packed, jnp.minimum(plane ^ step, MATRICES - 1), 0)
        got = exchange(jnp.concatenate([give, sent]), devices, CELL * step)
        pieces.append(got[:rows])
        sums.append(value(got[rows:]))
    current = jnp.concatenate(pieces)
    total = add_tree(sums)
    for mask in (4, 2, 1):
        sent = pair(total)
        got = exchange(jnp.concatenate([current, sent]), devices, mask)
        length = current.shape[0]
        current = jnp.concatenate([current, got[:length]])
        total = value(sent) + value(got[length:])
    return current.reshape(CELL, planes, rows, LANE), total


PAD_TOK = 64
KEY_ROWS = 56
PAD_IMG = 256
GROUPS = 4
NEVER = -1e30
f32 = jnp.float32
bf16 = jnp.bfloat16


def window_matrix():
    table = np.zeros((PAD_IMG, PATCHES), np.float32)
    blocks = SIDE // WIN
    for window in range(blocks * blocks):
        for token in range(WIN_TOK):
            row = (window // blocks) * WIN + token // WIN
            column = (window % blocks) * WIN + token % WIN
            patch = ((row + SHIFT) % SIDE) * SIDE + (column + SHIFT) % SIDE
            table[window * PAD_TOK + token, patch] = 1.0
    return table


def dot(left, right, left_dim=1, right_dim=0):
    return lax.dot_general(
        left, right, (((left_dim,), (right_dim,)), ((), ())), preferred_element_type=jnp.float32
    )


def normalize(values):
    center = values - jnp.mean(values, axis=-1, keepdims=True)
    spread = jnp.mean(center * center, axis=-1, keepdims=True)
    factor = lax.rsqrt(spread + 1e-05)
    return center * factor, factor


def normalize_back(grad, gain, hat, factor):
    inner = grad * gain
    return factor * (
        inner
        - jnp.mean(inner, axis=-1, keepdims=True)
        - hat * jnp.mean(inner * hat, axis=-1, keepdims=True)
    )


def head_masks(dtype):
    lane = lax.broadcasted_iota(jnp.int32, (1, 128), 1) // 32
    return [(lane == head).astype(dtype) for head in range(GROUPS)]


def spread_heads(rows, masks):
    return jnp.concatenate([rows * mask for mask in masks], axis=0)


def fold_heads(blocks, masks):
    total = None
    for head, mask in enumerate(masks):
        part = blocks[head * PAD_TOK : (head + 1) * PAD_TOK] * mask
        total = part if total is None else total + part
    return total


def load_image(ref, image, slots):
    return jnp.concatenate([ref[lane, pl.ds(image, PATCHES, stride=slots), :] for lane in range(ref.shape[0])], axis=1)


def store_image(ref, image, slots, values):
    for lane in range(ref.shape[0]):
        ref[lane, pl.ds(image, PATCHES, stride=slots), :] = values[:, lane * 128 : (lane + 1) * 128]


def cut_lanes(ref, values):
    for lane in range(ref.shape[0]):
        ref[lane] = values[:, lane * 128 : (lane + 1) * 128]


def join_lanes(ref):
    return jnp.concatenate([ref[lane] for lane in range(ref.shape[0])], axis=1)


def attend_kernel(
    images_ref, weights_ref, gains_ref, shifts_ref, biases_ref, combined_ref, take_ref, put_ref,
    windows_ref, triple_ref, attention_ref, mixed_ref, features_ref, scratch_ref,
):
    image = pl.program_id(0)
    width = images_ref.shape[-1]
    slots = images_ref.shape[0] // PATCHES
    scale = 1.0 / math.sqrt(width // HEADS)

    @pl.when(image == 0)
    def _():
        cut_lanes(features_ref, images_ref[...].astype(f32))

    features = load_image(features_ref, image, slots)
    hat, _ = normalize(features)
    normed = (hat * gains_ref[0:1] + shifts_ref[0:1]).astype(bf16)
    windows = dot(take_ref[...], normed).astype(bf16)
    windows_ref[0] = windows
    for part in range(3):
        columns = slice(part * width, (part + 1) * width)
        values = dot(windows, weights_ref[part]) + biases_ref[0:1, columns]
        if part == 0:
            values = values * scale
        triple_ref[0, :, columns] = values.astype(bf16)
    masks = head_masks(bf16)
    masks_wide = head_masks(f32)
    for window in range(4):
        rows = slice(window * PAD_TOK, (window + 1) * PAD_TOK)
        for group in range(GROUPS):
            lanes = slice(group * 128, (group + 1) * 128)
            query = triple_ref[0, rows, group * 128 : (group + 1) * 128]
            key = triple_ref[0, rows, width + group * 128 : width + (group + 1) * 128]
            value = triple_ref[0, rows, 2 * width + group * 128 : 2 * width + (group + 1) * 128]
            scores = dot(key, spread_heads(query, masks), 1, 1)[:KEY_ROWS] + combined_ref[window, group]
            top = jnp.max(scores, axis=0, keepdims=True)
            raised = jnp.exp(scores - top)
            attention = raised * (1.0 / jnp.sum(raised, axis=0, keepdims=True))
            attention_ref[0, window, group] = attention
            low = jnp.concatenate([attention, jnp.zeros((PAD_TOK - KEY_ROWS, attention.shape[1]), f32)], axis=0).astype(bf16)
            out = dot(low, value, 0, 0)
            scratch_ref[rows, lanes] = fold_heads(out, masks_wide).astype(bf16)
    store_image(mixed_ref, image, slots, dot(put_ref[...], scratch_ref[...]))


def whole(shape):
    return pl.BlockSpec(shape, lambda i: (0,) * len(shape))


def one(shape):
    return pl.BlockSpec((1,) + shape, lambda i: (i,) + (0,) * len(shape))


def attend_forward(images, weights, gains, shifts, biases, combined, take, put):
    rows, width = images.shape
    slots = rows // PATCHES
    return pl.pallas_call(
        attend_kernel,
        grid=(slots,),
        in_specs=[
            whole(images.shape), whole(weights.shape), whole(gains.shape), whole(shifts.shape),
            whole(biases.shape), whole(combined.shape), whole(take.shape), whole(put.shape),
        ],
        out_specs=[
            one((PAD_IMG, width)), one((PAD_IMG, 3 * width)), one((4, GROUPS, KEY_ROWS, 256)),
            whole((width // 128, rows, 128)),
        ],
        out_shape=[
            jax.ShapeDtypeStruct((slots, PAD_IMG, width), bf16),
            jax.ShapeDtypeStruct((slots, PAD_IMG, 3 * width), bf16),
            jax.ShapeDtypeStruct((slots, 4, GROUPS, KEY_ROWS, 256), f32),
            jax.ShapeDtypeStruct((width // 128, rows, 128), f32),
        ],
        scratch_shapes=[pltpu.VMEM((width // 128, rows, 128), f32), pltpu.VMEM((PAD_IMG, width), bf16)],
        compiler_params=pltpu.CompilerParams(vmem_limit_bytes=56 << 20),
        cost_estimate=pl.CostEstimate(flops=20*10**9, bytes_accessed=1 << 24, transcendentals=0),
        name="attend_forward",
    )(images, weights, gains, shifts, biases, combined, take, put)


def gelu_parts(values):
    size = jnp.abs(values) * math.sqrt(0.5)
    bell = jnp.exp(-0.5 * values * values)
    turn = 1.0 / (1.0 + 0.3275911 * size)
    tail = 1.061405429
    for factor in (-1.453152027, 1.421413741, -0.284496736, 0.254829592):
        tail = tail * turn + factor
    tail = 0.5 * tail * turn * bell
    share = jnp.where(values < 0.0, tail, 1.0 - tail)
    return share, values * bell * (1.0 / math.sqrt(2.0 * math.pi))


def feed_kernel(
    count_ref, images_ref, cotangent_ref, mixed_ref, merge_ref, expand_ref, project_ref, gains_ref, shifts_ref, biases_ref,
    block_ref, project_grad_ref, expand_grad_ref, merge_grad_ref, grad_middle_ref, grad_mixed_ref, sums_ref, hidden_sums_ref,
    *, slots,
):
    step = pl.program_id(0)
    rows, width = cotangent_ref.shape
    pieces, _, piece = expand_ref.shape
    hidden = pieces * piece
    mixed = join_lanes(mixed_ref).astype(bf16)
    branch = dot(mixed, merge_ref[...]) + biases_ref[0:1, 3 * width : 4 * width]
    middle = images_ref[...].astype(f32) + branch
    slot = lax.broadcasted_iota(jnp.int32, (rows, 1), 0) % slots
    live = slot < count_ref[0]

    @pl.when(step == 0)
    def _():
        project_grad_ref[...] = jnp.zeros_like(project_grad_ref)
        expand_grad_ref[...] = jnp.zeros_like(expand_grad_ref)
        merge_grad_ref[...] = jnp.zeros_like(merge_grad_ref)
        sums_ref[...] = jnp.zeros_like(sums_ref)
        hidden_sums_ref[...] = jnp.zeros_like(hidden_sums_ref)

    hat, factor = normalize(middle)
    gain = gains_ref[1:2]
    normed = (hat * gain + shifts_ref[1:2]).astype(bf16)
    grad_out = jnp.where(live, cotangent_ref[...].astype(f32), 0.0)
    grad_low = grad_out.astype(bf16)
    out = biases_ref[0:1, 4 * width + hidden : 5 * width + hidden]
    back = 0.0
    for index in range(pieces):
        columns = slice(index * piece, (index + 1) * piece)
        offset = 4 * width + index * piece
        pre = dot(normed, expand_ref[index]) + biases_ref[0:1, offset : offset + piece]
        share, slope = gelu_parts(pre)
        active = (pre * share).astype(bf16)
        out = out + dot(active, project_ref[columns])
        project_grad_ref[columns] += dot(active, grad_low, 0, 0)
        grad_pre = (dot(grad_low, project_ref[columns], 1, 1) * (share + slope)).astype(bf16)
        expand_grad_ref[index] += dot(normed, grad_pre, 0, 0)
        hidden_sums_ref[0:1, columns] += jnp.sum(grad_pre.astype(f32), axis=0, keepdims=True)
        back = back + dot(grad_pre, expand_ref[index], 1, 1)
    block_ref[...] = jnp.where(live, middle + out, 0.0).astype(bf16)
    grad_middle = grad_out + normalize_back(back, gain, hat, factor)
    cut_lanes(grad_middle_ref, grad_middle)
    grad_branch = grad_middle.astype(bf16)
    merge_grad_ref[...] += dot(mixed, grad_branch, 0, 0)
    cut_lanes(grad_mixed_ref, dot(grad_branch, merge_ref[...], 1, 1))
    sums_ref[0:1] += jnp.sum(back * hat, axis=0, keepdims=True)
    sums_ref[1:2] += jnp.sum(back, axis=0, keepdims=True)
    sums_ref[2:3] += jnp.sum(grad_out, axis=0, keepdims=True)
    sums_ref[3:4] += jnp.sum(grad_branch.astype(f32), axis=0, keepdims=True)


def feed_forward(count, images, cotangent, mixed, merge, expand, project, gains, shifts, biases, slots, tile):
    rows, width = cotangent.shape
    hidden = project.shape[0]
    lanes = pl.BlockSpec((width // 128, tile, 128), lambda i: (0, i, 0))

    def tiled(columns):
        return pl.BlockSpec((tile, columns), lambda i: (i, 0))

    return pl.pallas_call(
        partial(feed_kernel, slots=slots),
        grid=(rows // tile,),
        in_specs=[
            pl.BlockSpec(memory_space=pltpu.SMEM), tiled(width), tiled(width), lanes, whole(merge.shape), whole(expand.shape),
            whole(project.shape), whole(gains.shape), whole(shifts.shape), whole(biases.shape),
        ],
        out_specs=[
            tiled(width), whole((hidden, width)), whole(expand.shape), whole((width, width)), lanes,
            lanes, whole((8, width)), whole((8, hidden)),
        ],
        out_shape=[
            jax.ShapeDtypeStruct((rows, width), bf16),
            jax.ShapeDtypeStruct((hidden, width), f32),
            jax.ShapeDtypeStruct(expand.shape, f32),
            jax.ShapeDtypeStruct((width, width), f32),
            jax.ShapeDtypeStruct((width // 128, rows, 128), f32),
            jax.ShapeDtypeStruct((width // 128, rows, 128), f32),
            jax.ShapeDtypeStruct((8, width), f32),
            jax.ShapeDtypeStruct((8, hidden), f32),
        ],
        compiler_params=pltpu.CompilerParams(vmem_limit_bytes=60 << 20),
        cost_estimate=pl.CostEstimate(flops=44*10**9, bytes_accessed=1 << 24, transcendentals=0),
        name="feed_forward",
    )(count, images, cotangent, mixed, merge, expand, project, gains, shifts, biases)


def attend_back_kernel(
    grad_mixed_ref, triple_ref, attention_ref, windows_ref, take_ref,
    attend_grad_ref, grad_triple_ref, table_ref, sums_ref,
):
    step = pl.program_id(0)
    width = windows_ref.shape[-1]
    slots = grad_mixed_ref.shape[1] // PATCHES
    scale = 1.0 / math.sqrt(width // HEADS)

    @pl.when(step == 0)
    def _():
        attend_grad_ref[...] = jnp.zeros_like(attend_grad_ref)
        table_ref[...] = jnp.zeros_like(table_ref)
        sums_ref[...] = jnp.zeros_like(sums_ref)

    grad_mixed = dot(take_ref[...], load_image(grad_mixed_ref, step, slots).astype(bf16)).astype(bf16)
    masks = head_masks(bf16)
    masks_wide = head_masks(f32)
    pad = jnp.zeros((PAD_TOK - KEY_ROWS, 256), f32)
    for group in range(GROUPS):
        table = table_ref[group]
        for window in range(4):
            rows = slice(window * PAD_TOK, (window + 1) * PAD_TOK)
            query = triple_ref[0, rows, group * 128 : (group + 1) * 128]
            key = triple_ref[0, rows, width + group * 128 : width + (group + 1) * 128]
            value = triple_ref[0, rows, 2 * width + group * 128 : 2 * width + (group + 1) * 128]
            grad_heads = spread_heads(grad_mixed[rows, group * 128 : (group + 1) * 128], masks)
            attention = attention_ref[0, window, group]
            grad_attention = dot(value, grad_heads, 1, 1)[:KEY_ROWS]
            inner = jnp.sum(grad_attention * attention, axis=0, keepdims=True)
            grad_scores = attention * (grad_attention - inner)
            low = jnp.concatenate([grad_scores, pad], axis=0).astype(bf16)
            table = table + low.astype(f32)[:KEY_ROWS]
            attention_low = jnp.concatenate([attention, pad], axis=0).astype(bf16)
            grad_value = dot(attention_low, grad_heads)
            grad_key = dot(low, spread_heads(query, masks))
            grad_query = fold_heads(dot(low, key, 0, 0), masks_wide) * scale
            grad_triple_ref[0, rows, group * 128 : (group + 1) * 128] = grad_query.astype(bf16)
            grad_triple_ref[0, rows, width + group * 128 : width + (group + 1) * 128] = grad_key.astype(bf16)
            grad_triple_ref[0, rows, 2 * width + group * 128 : 2 * width + (group + 1) * 128] = grad_value.astype(bf16)
        table_ref[group] = table
    for part in range(3):
        columns = slice(part * width, (part + 1) * width)
        grad = grad_triple_ref[0, :, columns]
        attend_grad_ref[part] += dot(windows_ref[0], grad, 0, 0)
        sums_ref[0:1, columns] += jnp.sum(grad.astype(f32), axis=0, keepdims=True)


def attend_backward(grad_mixed, triple, attention, windows, take):
    width = windows.shape[-1]
    slots = triple.shape[0]
    return pl.pallas_call(
        attend_back_kernel,
        grid=(slots,),
        in_specs=[
            whole(grad_mixed.shape), one((PAD_IMG, 3 * width)),
            one((4, GROUPS, KEY_ROWS, 256)), one((PAD_IMG, width)), whole(take.shape),
        ],
        out_specs=[
            whole((3, width, width)), one((PAD_IMG, 3 * width)), whole((GROUPS, KEY_ROWS, 256)), whole((8, 3 * width)),
        ],
        out_shape=[
            jax.ShapeDtypeStruct((3, width, width), f32),
            jax.ShapeDtypeStruct((slots, PAD_IMG, 3 * width), bf16),
            jax.ShapeDtypeStruct((GROUPS, KEY_ROWS, 256), f32),
            jax.ShapeDtypeStruct((8, 3 * width), f32),
        ],
        compiler_params=pltpu.CompilerParams(vmem_limit_bytes=56 << 20),
        cost_estimate=pl.CostEstimate(flops=37*10**9, bytes_accessed=1 << 24, transcendentals=0),
        name="attend_backward",
    )(grad_mixed, triple, attention, windows, take)


def input_kernel(images_ref, grad_triple_ref, grad_middle_ref, weights_ref, gains_ref, put_ref, out_ref, sums_ref, features_ref, grads_ref):
    step = pl.program_id(0)
    width = images_ref.shape[-1]
    slots = images_ref.shape[0] // PATCHES

    @pl.when(step == 0)
    def _():
        sums_ref[...] = jnp.zeros_like(sums_ref)
        cut_lanes(features_ref, images_ref[...].astype(f32))

    hat, factor = normalize(load_image(features_ref, step, slots))
    grad = 0.0
    for part in range(3):
        grad = grad + dot(grad_triple_ref[0, :, part * width : (part + 1) * width], weights_ref[part], 1, 1)
    high = grad.astype(bf16)
    low = (grad - high.astype(f32)).astype(bf16)
    grad = dot(put_ref[...], high) + dot(put_ref[...], low)
    total = load_image(grad_middle_ref, step, slots) + normalize_back(grad, gains_ref[0:1], hat, factor)
    store_image(grads_ref, step, slots, total)
    sums_ref[0:1] += jnp.sum(grad * hat, axis=0, keepdims=True)
    sums_ref[1:2] += jnp.sum(grad, axis=0, keepdims=True)

    @pl.when(step == slots - 1)
    def _():
        out_ref[...] = join_lanes(grads_ref)


def input_backward(images, grad_triple, grad_middle, weights, gains, put):
    rows, width = images.shape
    slots = rows // PATCHES
    return pl.pallas_call(
        input_kernel,
        grid=(slots,),
        in_specs=[
            whole((rows, width)), one((PAD_IMG, 3 * width)), whole(grad_middle.shape),
            pl.BlockSpec((3, width, width), lambda i: (0, 0, 0)), whole(gains.shape), whole(put.shape),
        ],
        out_specs=[whole((rows, width)), whole((8, width))],
        out_shape=[
            jax.ShapeDtypeStruct((rows, width), f32),
            jax.ShapeDtypeStruct((8, width), f32),
        ],
        scratch_shapes=[pltpu.VMEM((width // 128, rows, 128), f32)] * 2,
        compiler_params=pltpu.CompilerParams(vmem_limit_bytes=56 << 20),
        cost_estimate=pl.CostEstimate(flops=14*10**9, bytes_accessed=1 << 24, transcendentals=0),
        name="input_backward",
    )(images, grad_triple, grad_middle, weights, gains, put)


def combine_bias(bias_table, rel_index, shift_mask):
    one_hot = (rel_index.reshape(-1)[:, None] == jnp.arange(TABLE)[None, :]).astype(f32)
    position = jnp.dot(one_hot, bias_table, precision=lax.Precision.HIGHEST).T
    position = position.reshape(GROUPS, 4, WIN_TOK, WIN_TOK)
    position = jnp.transpose(position, (0, 3, 1, 2))
    position = jnp.pad(
        position, ((0, 0), (0, KEY_ROWS - WIN_TOK), (0, 0), (0, PAD_TOK - WIN_TOK))
    ).reshape(GROUPS, KEY_ROWS, 256)
    mask = jnp.transpose(-100.0 * (1 - shift_mask).astype(f32), (0, 2, 1))
    mask = jnp.pad(mask, ((0, 0), (0, 0), (0, PAD_TOK - WIN_TOK)))
    mask = jnp.pad(mask, ((0, 0), (0, KEY_ROWS - WIN_TOK), (0, 0)), constant_values=NEVER)
    mask = jnp.tile(mask, (1, 1, 4))
    return position[None] + mask[:, None], one_hot


def table_gradient(table, one_hot):
    grad = table.reshape(GROUPS, KEY_ROWS, 4, PAD_TOK)[:, :WIN_TOK, :, :WIN_TOK]
    grad = jnp.transpose(grad, (3, 1, 0, 2)).reshape(WIN_TOK * WIN_TOK, HEADS)
    return jnp.dot(one_hot.T, grad, precision=lax.Precision.HIGHEST)


def flat_rows(images):
    return jnp.transpose(images, (1, 0, 2)).reshape(-1, images.shape[-1])


def image_form(rows, slots):
    return jnp.transpose(rows.reshape(-1, slots, rows.shape[-1]), (1, 0, 2))


def adamw_step(param, grad, first, second, steps):
    first_next = 0.9 * first + 0.1 * grad
    second_next = 0.999 * second + 0.001 * grad * grad
    first_hat = first_next / (1.0 - jnp.power(0.9, steps))
    second_hat = second_next / (1.0 - jnp.power(0.999, steps))
    update = -0.05 * (first_hat / (jnp.sqrt(second_hat) + 1e-08) + 0.05 * param)
    return (first_next, second_next, update)


def column_blocks(matrix):
    rows, columns = matrix.shape
    return jnp.transpose(matrix.reshape(rows, columns // LANE, LANE), (1, 0, 2))


def from_blocks(blocks):
    count, rows, lanes = blocks.shape
    return jnp.transpose(blocks, (1, 0, 2)).reshape(rows, count * lanes)


def local(
    images,
    cotangent,
    image_counts,
    shift_mask,
    rel_index,
    step_count,
    attend_weight,
    merge_weight,
    expand_weight,
    project_weight,
    norm_gains,
    norm_shifts,
    layer_biases,
    bias_table,
    attend_momentum,
    merge_momentum,
    expand_momentum,
    project_momentum,
    gains_mean,
    gains_square,
    shifts_mean,
    shifts_square,
    biases_mean,
    biases_square,
    table_mean,
    table_square,
):
    slots, patches, width = images.shape
    devices = lax.axis_size("dp")
    hidden_units = expand_weight.shape[1]
    grad_scale = 1.0 / math.sqrt(slots * devices * PATCHES)
    rank = lax.axis_index("dp")
    planes = devices // CELL
    plane = rank // CELL
    corner = (rank // 2) % 4
    shard = width // devices
    tall_shard = hidden_units // devices

    attend_rows = column_blocks(attend_weight).reshape(-1, LANE)
    other_rows = jnp.concatenate(
        [column_blocks(merge_weight).reshape(-1, LANE), column_blocks(expand_weight).reshape(-1, LANE), project_weight]
    )
    near = gather_planes(attend_rows, devices)
    near[0], other_rows = lax.optimization_barrier((near[0], other_rows))
    other_near = gather_planes(other_rows, devices)
    near = gather_corners(jnp.stack(near), devices)
    near[0], other_near[1] = lax.optimization_barrier((near[0], other_near[1]))
    near = jnp.stack(near)
    far = exchange(near, devices, 1)
    far, *other_near = lax.optimization_barrier((far, *other_near))
    other_near = gather_corners(jnp.stack(other_near), devices)
    (weights,) = order_rows(near, far, ((3, shard),), rank)

    take = jnp.asarray(window_matrix(), bf16)
    put = jnp.asarray(window_matrix().T, bf16)
    combined, one_hot = combine_bias(bias_table, rel_index, shift_mask)
    bias_row = layer_biases.reshape(1, -1)
    rows = flat_rows(images)
    windows, triple, attention, mixed = attend_forward(rows, weights, norm_gains, norm_shifts, bias_row, combined, take, put)
    mixed, *other_near = lax.optimization_barrier((mixed, *other_near))
    other_near = jnp.stack(other_near)
    other_far = exchange(other_near, devices, 1)
    merge, expand, project = order_rows(
        other_near, other_far, ((1, shard), (hidden_units // LANE, shard), (1, tall_shard)), rank
    )
    block_rows, project_term, expand_term, merge_term, grad_middle, grad_mixed, feed_sums, hidden_sums = feed_forward(
        image_counts, rows, flat_rows(cotangent), mixed, merge[0], expand, project[0], norm_gains, norm_shifts, bias_row,
        slots, slots * patches // 4,
    )
    block_out = image_form(block_rows, slots)

    wide = (True, False, False)
    body_parts = reduce_core(
        [
            merge_term.reshape(1, devices, -1, LANE),
            expand_term.reshape(expand_term.shape[0], devices, -1, LANE),
            project_term.reshape(1, devices, -1, LANE),
        ],
        wide,
        rank,
        devices,
    )
    body_parts = by_corner(body_parts, devices)
    grad_mixed, *body_parts = lax.optimization_barrier((grad_mixed, *body_parts))
    body_got = reduce_sent(body_parts, wide, corner, 4, 2, 2, devices)
    attend_term, grad_triple, table_sums, triple_sums = attend_backward(grad_mixed, triple, attention, windows, take)
    head_parts = reduce_core(
        [attend_term.reshape(attend_term.shape[0], devices, -1, LANE)], (False,), rank, devices
    )
    head_parts = by_corner(head_parts, devices)
    body_parts = reduce_added(body_parts, wide, corner, 2, body_got)
    grad_triple, *parts = lax.optimization_barrier((grad_triple, *head_parts, *body_parts))
    head_parts, body_parts = parts[:1], parts[1:]
    head_got = reduce_sent(head_parts, (False,), corner, 4, 2, 2, devices)
    body_got = reduce_sent(body_parts, wide, plane, planes, 1, CELL, devices)
    grad_triple, arrived = lax.optimization_barrier((grad_triple, head_got[1][0]))
    head_got[1] = (arrived, head_got[1][1])
    input_rows, input_sums = input_backward(rows, grad_triple, grad_middle, weights, norm_gains, put)
    late = [pair[0] for pair in (head_got[0], head_got[2], *body_got)]
    input_sums, *late = lax.optimization_barrier((input_sums, *late))
    head_got[0], head_got[2] = (late[0], head_got[0][1]), (late[1], head_got[2][1])
    body_got = [(payload, pair[1]) for payload, pair in zip(late[2:], body_got)]
    input_grad = image_form(input_rows, slots)
    table_term = table_gradient(table_sums, one_hot)
    head_parts = reduce_added(head_parts, (False,), corner, 2, head_got)
    head_got = reduce_sent(head_parts, (False,), plane, planes, 1, CELL, devices)
    merge_sum, expand_sum, project_sum = reduce_added(body_parts, wide, plane, 1, body_got)
    (attend_sum,) = reduce_added(head_parts, (False,), plane, 1, head_got)

    small_parts = (
        jnp.stack([input_sums[0], feed_sums[0]]),
        jnp.stack([input_sums[1], feed_sums[1]]),
        jnp.concatenate([triple_sums[0], feed_sums[3], hidden_sums[0], feed_sums[2]]),
        table_term,
    )
    small = jnp.concatenate([part.reshape(-1) for part in small_parts])
    small = jnp.pad(small, (0, -small.shape[0] % (8 * LANE))).reshape(-1, LANE)

    block_sums = (attend_sum, merge_sum, expand_sum, project_sum)
    momenta = (attend_momentum, merge_momentum, expand_momentum, project_momentum)
    block_grads = [term * grad_scale for term in block_sums]
    block_next = [
        0.95 * column_blocks(moment) + grad for moment, grad in zip(momenta, block_grads)
    ]
    length = tall_shard
    packed = []
    for order, moment in enumerate(block_next):
        flat = moment.reshape(-1, LANE)
        if order == 1:
            flat = jnp.concatenate(split_wide(flat))
        packed.append(pad_rows(flat.astype(bf16), length))
    whole_rows, small = collect(jnp.stack(packed), small, rank, devices)
    stack = whole_rows.reshape(CELL * planes, MATRICES, -1, LANE)
    stack = jnp.transpose(stack, (1, 0, 2, 3)).reshape(MATRICES, -1, LANE)
    kind = jnp.minimum(plane, MATRICES - 1).astype(jnp.int32).reshape(1)
    chunk = planes * length // MATRICES
    orth = newton_rows(stack, kind, chunk).reshape(MATRICES, planes, -1, LANE)
    pieces = [orth[:, 0]]
    for step in range(1, planes):
        pieces.append(exchange(orth[:, step], devices, CELL * step))
    received = jnp.stack(pieces)

    flat, start, small_sums = small.reshape(-1), 0, []
    for part in small_parts:
        small_sums.append(flat[start : start + part.size].reshape(part.shape))
        start += part.size
    small_grads = tuple((term * grad_scale for term in small_sums))
    results = [block_out, input_grad]
    for order, (grad, moment_next, moment) in enumerate(zip(block_grads, block_next, momenta)):
        piece = pick(received, plane ^ order, 0)
        piece = piece.reshape(-1, LANE)[: moment.size // LANE].reshape(grad.shape)
        extent = max(devices * moment.shape[0], moment.shape[1])
        update = -0.02 * math.sqrt(extent) * from_blocks(piece).astype(f32)
        results += [from_blocks(grad), from_blocks(moment_next), update]
    steps = step_count[0].astype(f32)
    params = (norm_gains, norm_shifts, layer_biases, bias_table)
    states = (
        (gains_mean, gains_square),
        (shifts_mean, shifts_square),
        (biases_mean, biases_square),
        (table_mean, table_square),
    )
    for param, grad, state in zip(params, small_grads, states):
        first_next, second_next, update = adamw_step(param, grad, state[0], state[1], steps)
        results += [grad, first_next, second_next, update]
    return tuple(results)


def solution(mesh):
    return jax.shard_map(
        local,
        mesh=mesh,
        in_specs=(
            P("dp", None, None),
            P("dp", None, None),
            P("dp"),
            P(),
            P(),
            P(),
            P("dp", None),
            P("dp", None),
            P("dp", None),
            P("dp", None),
            P(),
            P(),
            P(),
            P(),
            P("dp", None),
            P("dp", None),
            P("dp", None),
            P("dp", None),
            P(),
            P(),
            P(),
            P(),
            P(),
            P(),
            P(),
            P(),
        ),
        out_specs=(
            P("dp", None, None),
            P("dp", None, None),
            P("dp", None),
            P("dp", None),
            P("dp", None),
            P("dp", None),
            P("dp", None),
            P("dp", None),
            P("dp", None),
            P("dp", None),
            P("dp", None),
            P("dp", None),
            P("dp", None),
            P("dp", None),
            P(),
            P(),
            P(),
            P(),
            P(),
            P(),
            P(),
            P(),
            P(),
            P(),
            P(),
            P(),
            P(),
            P(),
            P(),
            P(),
        ),
        check_vma=False,
    )
```

```python
from functools import partial
import math

import jax
import jax.numpy as jnp
import numpy as np
from jax import lax
from jax.experimental import pallas as pl
from jax.experimental.pallas import tpu as pltpu
from jax.sharding import PartitionSpec as P

HEADS = 16
WIN = 7
SIDE = 14
SHIFT = 3
WIN_TOK = 49
PATCHES = 196
TABLE = 169


newton_first = 3.4445
newton_second = -4.775
newton_third = 2.0315


LANE = 512
CELL = 8
MATRICES = 4


def exchange(payload, devices, mask):
    return lax.ppermute(payload, "dp", [(i, i ^ mask) for i in range(devices)])


def pick(values, index, axis):
    return lax.dynamic_index_in_dim(values, index, axis, keepdims=False)


def split_wide(values):
    high = lax.reduce_precision(values, 8, 7)
    return high.astype(jnp.bfloat16), lax.reduce_precision(values - high, 8, 7).astype(jnp.bfloat16)


def join_wide(high, low):
    return high.astype(jnp.float32) + low.astype(jnp.float32)


def order_kernel(rank_ref, near_ref, far_ref, *out_refs, spans):
    rank = rank_ref[0]
    corners, planes = near_ref.shape[:2]
    for core, source in enumerate((near_ref, far_ref)):
        for corner in range(corners):
            for plane in range(planes):
                owner = jnp.bitwise_xor(rank, core + 2 * corner + CELL * plane)
                start = 0
                for out_ref, (blocks, rows) in zip(out_refs, spans):
                    place = pl.ds(pl.multiple_of(owner * rows, rows), rows)
                    for block in range(blocks):
                        out_ref[block, place, :] = source[corner, plane, start : start + rows, :]
                        start += rows


def order_rows(near, far, spans, rank):
    corners, planes, _, lanes = near.shape
    devices = 2 * corners * planes
    shapes = [(blocks, devices * rows, lanes) for blocks, rows in spans]
    if all(rows % 16 == 0 for _, rows in spans):
        return pl.pallas_call(
            partial(order_kernel, spans=spans),
            out_shape=[jax.ShapeDtypeStruct(shape, near.dtype) for shape in shapes],
            in_specs=[pl.BlockSpec(memory_space=pltpu.SMEM)] + [pl.BlockSpec(memory_space=pltpu.VMEM)] * 2,
            out_specs=[pl.BlockSpec(memory_space=pltpu.VMEM)] * len(shapes),
            compiler_params=pltpu.CompilerParams(vmem_limit_bytes=32 << 20),
            cost_estimate=pl.CostEstimate(flops=0, bytes_accessed=4 * near.size * 2, transcendentals=0),
            name="order_rows",
        )(rank.reshape(1), near, far)
    both = jnp.stack([near, far]).reshape(devices, -1, lanes)
    offset = jnp.arange(devices) ^ rank
    both = jnp.take(both, (offset & 1) * (corners * planes) + ((offset >> 1) & 3) * planes + (offset >> 3), axis=0)
    out, start = [], 0
    for (blocks, rows), shape in zip(spans, shapes):
        part = both[:, start : start + blocks * rows].reshape(devices, blocks, rows, lanes)
        out.append(jnp.transpose(part, (1, 0, 2, 3)).reshape(shape))
        start += blocks * rows
    return out


def gather_planes(rows, devices):
    return [rows] + [exchange(rows, devices, CELL * step) for step in range(1, devices // CELL)]


def gather_corners(rows, devices):
    return [rows] + [exchange(rows, devices, 2 * step) for step in range(1, 4)]


BODY = ((1, True), (4, False), (4, False))
HEAD = ((3, False),)


def encode(values, spans, rows):
    sent, start = [], 0
    for blocks, wide in spans:
        part = values[..., start : start + blocks * rows, :]
        start += blocks * rows
        high = part.astype(jnp.bfloat16)
        sent.append(high)
        if wide:
            sent.append((part - high.astype(jnp.float32)).astype(jnp.bfloat16))
    return sent[0] if len(sent) == 1 else jnp.concatenate(sent, axis=-2)


def decode(payload, spans, rows):
    out, start = [], 0
    for blocks, wide in spans:
        part = payload[..., start : start + blocks * rows, :].astype(jnp.float32)
        start += blocks * rows
        if wide:
            part = part + payload[..., start : start + blocks * rows, :].astype(jnp.float32)
            start += blocks * rows
        out.append(part)
    return out[0] if len(out) == 1 else jnp.concatenate(out, axis=-2)


def aligned(rows):
    return rows % 16 == 0


def pack_core(parts, spans, rows, mine):
    packed = []
    for (blocks, _), part in zip(spans, parts):
        count = part.shape[0]
        per = blocks * rows // count
        part = part.reshape(count, -1, 2, per, LANE)
        packed.append(jnp.transpose(part, (1, 2, 0, 3, 4)).reshape(part.shape[1], 2, blocks * rows, LANE))
    packed = jnp.concatenate(packed, axis=2)
    return pick(packed, mine, 1), encode(pick(packed, 1 - mine, 1), spans, rows)


def store_core(sources, keep_ref, sent_ref, spans, rows, mine):
    for pair in range(keep_ref.shape[0]):
        start, sent = 0, 0
        for (blocks, wide), (source, count) in zip(spans, sources):
            per = blocks * rows // count
            near = pl.ds(pl.multiple_of(pair * 2 * per + mine * per, per), per)
            away = pl.ds(pl.multiple_of(pair * 2 * per + (1 - mine) * per, per), per)
            for block in range(count):
                lead = (block,) if len(source.shape) == 3 else ()
                keep_ref[pair, start : start + per, :] = source[lead + (near, slice(None))]
                values = source[lead + (away, slice(None))]
                high = values.astype(jnp.bfloat16)
                sent_ref[pair, sent : sent + per, :] = high
                if wide:
                    low = (values - high.astype(jnp.float32)).astype(jnp.bfloat16)
                    sent_ref[pair, sent + blocks * rows : sent + blocks * rows + per, :] = low
                start += per
                sent += per
            if wide:
                sent += blocks * rows


def fold_kernel(own_ref, keep_ref, *refs, gots, spans, rows):
    own = own_ref[0]
    total_ref, *sent_refs = refs[gots:]
    for step in range(keep_ref.shape[1]):
        index = jnp.bitwise_xor(own, step)
        total = keep_ref[0, index]
        for got in refs[:gots]:
            total = total + decode(got[0, index], spans, rows)
        if step:
            sent_refs[step - 1][0] = encode(total, spans, rows)
        else:
            total_ref[0] = total


def fold(keep, got, own, spans, rows):
    groups, members, length, lanes = keep.shape
    if not aligned(rows):
        total = keep
        for payload in got:
            total = total + decode(payload, spans, rows)
        return pick(total, own, 1), [encode(pick(total, own ^ step, 1), spans, rows) for step in range(1, members)]
    sent = got[0].shape[2]

    def block(*shape):
        return pl.BlockSpec((1,) + shape, lambda i: (i,) + (0,) * len(shape))

    total, *sends = pl.pallas_call(
        partial(fold_kernel, gots=len(got), spans=spans, rows=rows),
        grid=(groups,),
        in_specs=[pl.BlockSpec(memory_space=pltpu.SMEM), block(members, length, lanes)]
        + [block(members, sent, lanes)] * len(got),
        out_specs=[block(length, lanes)] + [block(sent, lanes)] * (members - 1),
        out_shape=[jax.ShapeDtypeStruct((groups, length, lanes), jnp.float32)]
        + [jax.ShapeDtypeStruct((groups, sent, lanes), jnp.bfloat16)] * (members - 1),
        compiler_params=pltpu.CompilerParams(vmem_limit_bytes=32 << 20),
        cost_estimate=pl.CostEstimate(flops=2 * 10**9, bytes_accessed=8 * keep.size, transcendentals=0),
        name="fold",
    )(own.reshape(1), keep, *got)
    return total, sends


def send_all(payloads, mask, devices):
    return [exchange(payload, devices, mask * (step + 1)) for step, payload in enumerate(payloads)]


def finish_math(head, head_got, body, body_got, momenta, rows, grad_scale):
    for payload in head_got:
        head = head + decode(payload, HEAD, rows)
    for payload in body_got:
        body = body + decode(payload, BODY, rows)
    spans = (head, body[:rows], body[rows : 5 * rows], body[5 * rows :])
    grads, following, packed = [], [], []
    for order, (span, moment) in enumerate(zip(spans, momenta)):
        blocks = moment.shape[1] // LANE
        per = moment.shape[0]
        grad = jnp.concatenate([span[block * per : (block + 1) * per] for block in range(blocks)], axis=1) * grad_scale
        after = 0.95 * moment + grad
        grads.append(grad)
        following.append(after)
        pieces = [after[:, block * LANE : (block + 1) * LANE] for block in range(blocks)]
        if order == 1:
            high = after.astype(jnp.bfloat16)
            pieces = [high, after - high.astype(jnp.float32)]
        pieces = [piece.astype(jnp.bfloat16) for piece in pieces]
        if per * len(pieces) < 4 * rows:
            pieces.append(jnp.zeros((4 * rows - per * len(pieces), LANE), jnp.bfloat16))
        packed.append(jnp.concatenate(pieces, axis=0))
    return grads, following, packed


def finish_kernel(*refs, count, rows, grad_scale):
    head, body = refs[0][0], refs[1][0]
    head_got = [ref[0] for ref in refs[2 : 2 + count]]
    body_got = [ref[0] for ref in refs[2 + count : 2 + 2 * count]]
    momenta = [ref[...] for ref in refs[2 + 2 * count : 6 + 2 * count]]
    outs = refs[6 + 2 * count :]
    grads, following, packed = finish_math(head, head_got, body, body_got, momenta, rows, grad_scale)
    for index in range(4):
        outs[index][...] = grads[index]
        outs[4 + index][...] = following[index]
        outs[8][index] = packed[index]


def finish(head, head_got, body, body_got, momenta, rows, grad_scale):
    if not aligned(rows):
        grads, following, packed = finish_math(
            head[0], [got[0] for got in head_got], body[0], [got[0] for got in body_got], momenta, rows, grad_scale
        )
        return grads, following, jnp.stack(packed)
    shapes = [jax.ShapeDtypeStruct(moment.shape, jnp.float32) for moment in momenta]
    outs = pl.pallas_call(
        partial(finish_kernel, count=len(head_got), rows=rows, grad_scale=grad_scale),
        out_shape=shapes + shapes + [jax.ShapeDtypeStruct((4, 4 * rows, LANE), jnp.bfloat16)],
        compiler_params=pltpu.CompilerParams(vmem_limit_bytes=24 << 20),
        cost_estimate=pl.CostEstimate(flops=10**9, bytes_accessed=1 << 22, transcendentals=0),
        name="finish",
    )(head, body, *head_got, *body_got, *momenta)
    return outs[:4], outs[4:8], outs[8]


def by_corner(packed):
    return packed.reshape((-1, 4) + packed.shape[1:])


def newton_kernel(kind_ref, stack_ref, out_ref, gram_ref, rows_ref):
    kind = kind_ref[0]
    blocks, side, _ = stack_ref.shape
    chunk = out_ref.shape[1]
    tall = kind == 3
    paired = kind == 1

    @pl.when(tall)
    def _():
        total = dot(stack_ref[0], stack_ref[0], 0, 0)
        for block in range(1, blocks):
            total = total + dot(stack_ref[block], stack_ref[block], 0, 0)
        gram_ref[...] = total

    @pl.when(paired)
    def _():
        cross = dot(stack_ref[0], stack_ref[1], 1, 1)
        cross = cross + dot(stack_ref[1], stack_ref[0], 1, 1)
        gram_ref[...] = dot(stack_ref[0], stack_ref[0], 1, 1) + cross

    @pl.when(jnp.logical_not(jnp.logical_or(tall, paired)))
    def _():
        total = dot(stack_ref[0], stack_ref[0], 1, 1)
        for block in range(1, blocks):
            total = total + dot(stack_ref[block], stack_ref[block], 1, 1)
        gram_ref[...] = total

    row = lax.broadcasted_iota(jnp.int32, (side, side), 0)
    column = lax.broadcasted_iota(jnp.int32, (side, side), 1)
    eye = (row == column).astype(jnp.float32)
    gram = gram_ref[...]
    inverse = 1.0 / (jnp.sqrt(jnp.sum(gram * eye)) + 1e-07)
    gram_ref[...] = gram * (inverse * inverse)

    @pl.when(tall)
    def _():
        for block in range(blocks):
            rows_ref[block * chunk : (block + 1) * chunk] = stack_ref[block, :chunk].astype(jnp.float32) * inverse

    @pl.when(jnp.logical_not(tall))
    def _():
        rows_ref[...] = eye[: blocks * chunk] * inverse

    def halves(values):
        high = values.astype(jnp.bfloat16)
        return high, (values - high.astype(jnp.float32)).astype(jnp.bfloat16)

    def product(left, right):
        return dot(left[0], right[0]) + (dot(left[1], right[0]) + dot(left[0], right[1]))

    def mix(gram, parts):
        return halves(newton_first * eye + newton_second * gram + newton_third * product(parts, parts))

    def sweep(step, carry):
        gram = gram_ref[...]
        parts = halves(gram)
        mixer = mix(gram, parts)
        rows_ref[...] = product(halves(rows_ref[...]), mixer)
        gram_ref[...] = product(halves(product(parts, mixer)), mixer)
        return carry

    lax.fori_loop(0, 4, sweep, 0)
    gram = gram_ref[...]
    rows = product(halves(rows_ref[...]), mix(gram, halves(gram)))

    @pl.when(tall)
    def _():
        for block in range(blocks):
            out_ref[block] = rows[block * chunk : (block + 1) * chunk].astype(out_ref.dtype)

    @pl.when(jnp.logical_not(tall))
    def _():
        own = halves(rows[:chunk])
        first = dot(own[0], stack_ref[0]) + dot(own[1], stack_ref[0])
        second = dot(own[0], stack_ref[1])
        out_ref[0] = jnp.where(paired, first + second, first).astype(out_ref.dtype)
        out_ref[1] = (second + dot(own[1], stack_ref[1])).astype(out_ref.dtype)
        for block in range(2, blocks):
            out_ref[block] = (dot(own[0], stack_ref[block]) + dot(own[1], stack_ref[block])).astype(out_ref.dtype)


def newton_rows(stack, kind, chunk):
    blocks, side, lanes = stack.shape
    return pl.pallas_call(
        newton_kernel,
        out_shape=jax.ShapeDtypeStruct((blocks, chunk, lanes), jnp.bfloat16),
        in_specs=[
            pl.BlockSpec(memory_space=pltpu.SMEM),
            pl.BlockSpec(memory_space=pltpu.VMEM),
        ],
        out_specs=pl.BlockSpec(memory_space=pltpu.VMEM),
        scratch_shapes=[pltpu.VMEM((side, side), jnp.float32), pltpu.VMEM((blocks * chunk, side), jnp.float32)],
        compiler_params=pltpu.CompilerParams(vmem_limit_bytes=48 << 20),
        cost_estimate=pl.CostEstimate(flops=20 * 10**9, bytes_accessed=1 << 22, transcendentals=0),
        name="newton_rows",
    )(kind, stack)


def add_tree(values):
    while len(values) > 1:
        values = [left + right for left, right in zip(values[::2], values[1::2])]
    return values[0]


def collect(packed, small, rank, devices):
    planes = devices // CELL
    plane = rank // CELL
    rows = packed.shape[1]
    count = small.shape[0]

    def pair(values):
        high, low = split_wide(values)
        return jnp.concatenate([high, low])

    def value(sent):
        return join_wide(sent[:count], sent[count:])

    sent = pair(small)
    pieces, sums = [pick(packed, jnp.minimum(plane, MATRICES - 1), 0)], [value(sent)]
    for step in range(1, planes):
        give = pick(packed, jnp.minimum(plane ^ step, MATRICES - 1), 0)
        got = exchange(jnp.concatenate([give, sent]), devices, CELL * step)
        pieces.append(got[:rows])
        sums.append(value(got[rows:]))
    current = jnp.concatenate(pieces)
    total = add_tree(sums)
    for mask in (4, 2, 1):
        sent = pair(total)
        got = exchange(jnp.concatenate([current, sent]), devices, mask)
        length = current.shape[0]
        current = jnp.concatenate([current, got[:length]])
        total = value(sent) + value(got[length:])
    return current.reshape(CELL, planes, rows, LANE), total


PAD_TOK = 64
KEY_ROWS = 56
PAD_IMG = 256
GROUPS = 4
NEVER = -1e30
f32 = jnp.float32
bf16 = jnp.bfloat16


def window_matrix():
    table = np.zeros((PAD_IMG, PATCHES), np.float32)
    blocks = SIDE // WIN
    for window in range(blocks * blocks):
        for token in range(WIN_TOK):
            row = (window // blocks) * WIN + token // WIN
            column = (window % blocks) * WIN + token % WIN
            patch = ((row + SHIFT) % SIDE) * SIDE + (column + SHIFT) % SIDE
            table[window * PAD_TOK + token, patch] = 1.0
    return table


def dot(left, right, left_dim=1, right_dim=0):
    return lax.dot_general(
        left, right, (((left_dim,), (right_dim,)), ((), ())), preferred_element_type=jnp.float32
    )


def normalize(values):
    center = values - jnp.mean(values, axis=-1, keepdims=True)
    spread = jnp.mean(center * center, axis=-1, keepdims=True)
    factor = lax.rsqrt(spread + 1e-05)
    return center * factor, factor


def normalize_back(grad, gain, hat, factor):
    inner = grad * gain
    return factor * (
        inner
        - jnp.mean(inner, axis=-1, keepdims=True)
        - hat * jnp.mean(inner * hat, axis=-1, keepdims=True)
    )


def head_masks(dtype):
    lane = lax.broadcasted_iota(jnp.int32, (1, 128), 1) // 32
    return [(lane == head).astype(dtype) for head in range(GROUPS)]


def spread_heads(rows, masks):
    return jnp.concatenate([rows * mask for mask in masks], axis=0)


def fold_heads(blocks, masks):
    total = None
    for head, mask in enumerate(masks):
        part = blocks[head * PAD_TOK : (head + 1) * PAD_TOK] * mask
        total = part if total is None else total + part
    return total


def load_image(ref, image, slots):
    return jnp.concatenate([ref[lane, pl.ds(image, PATCHES, stride=slots), :] for lane in range(ref.shape[0])], axis=1)


def store_image(ref, image, slots, values):
    for lane in range(ref.shape[0]):
        ref[lane, pl.ds(image, PATCHES, stride=slots), :] = values[:, lane * 128 : (lane + 1) * 128]


def cut_lanes(ref, values):
    for lane in range(ref.shape[0]):
        ref[lane] = values[:, lane * 128 : (lane + 1) * 128]


def join_lanes(ref):
    return jnp.concatenate([ref[lane] for lane in range(ref.shape[0])], axis=1)


def attend_kernel(
    images_ref, weights_ref, gains_ref, shifts_ref, biases_ref, combined_ref, take_ref, put_ref,
    windows_ref, triple_ref, attention_ref, mixed_ref, features_ref, scratch_ref,
):
    image = pl.program_id(0)
    width = images_ref.shape[-1]
    slots = images_ref.shape[0] // PATCHES
    scale = 1.0 / math.sqrt(width // HEADS)

    @pl.when(image == 0)
    def _():
        cut_lanes(features_ref, images_ref[...].astype(f32))

    features = load_image(features_ref, image, slots)
    hat, _ = normalize(features)
    normed = (hat * gains_ref[0:1] + shifts_ref[0:1]).astype(bf16)
    windows = dot(take_ref[...], normed).astype(bf16)
    windows_ref[0] = windows
    for part in range(3):
        columns = slice(part * width, (part + 1) * width)
        values = dot(windows, weights_ref[part]) + biases_ref[0:1, columns]
        if part == 0:
            values = values * scale
        triple_ref[0, :, columns] = values.astype(bf16)
    masks = head_masks(bf16)
    masks_wide = head_masks(f32)
    for window in range(4):
        rows = slice(window * PAD_TOK, (window + 1) * PAD_TOK)
        for group in range(GROUPS):
            lanes = slice(group * 128, (group + 1) * 128)
            query = triple_ref[0, rows, group * 128 : (group + 1) * 128]
            key = triple_ref[0, rows, width + group * 128 : width + (group + 1) * 128]
            value = triple_ref[0, rows, 2 * width + group * 128 : 2 * width + (group + 1) * 128]
            scores = dot(key, spread_heads(query, masks), 1, 1)[:KEY_ROWS] + combined_ref[window, group]
            top = jnp.max(scores, axis=0, keepdims=True)
            raised = jnp.exp(scores - top)
            attention = raised * (1.0 / jnp.sum(raised, axis=0, keepdims=True))
            attention_ref[0, window, group] = attention
            low = jnp.concatenate([attention, jnp.zeros((PAD_TOK - KEY_ROWS, attention.shape[1]), f32)], axis=0).astype(bf16)
            out = dot(low, value, 0, 0)
            scratch_ref[rows, lanes] = fold_heads(out, masks_wide).astype(bf16)
    store_image(mixed_ref, image, slots, dot(put_ref[...], scratch_ref[...]))


def whole(shape):
    return pl.BlockSpec(shape, lambda i: (0,) * len(shape))


def one(shape):
    return pl.BlockSpec((1,) + shape, lambda i: (i,) + (0,) * len(shape))


def attend_forward(images, weights, gains, shifts, biases, combined, take, put):
    rows, width = images.shape
    slots = rows // PATCHES
    return pl.pallas_call(
        attend_kernel,
        grid=(slots,),
        in_specs=[
            whole(images.shape), whole(weights.shape), whole(gains.shape), whole(shifts.shape),
            whole(biases.shape), whole(combined.shape), whole(take.shape), whole(put.shape),
        ],
        out_specs=[
            one((PAD_IMG, width)), one((PAD_IMG, 3 * width)), one((4, GROUPS, KEY_ROWS, 256)),
            whole((width // 128, rows, 128)),
        ],
        out_shape=[
            jax.ShapeDtypeStruct((slots, PAD_IMG, width), bf16),
            jax.ShapeDtypeStruct((slots, PAD_IMG, 3 * width), bf16),
            jax.ShapeDtypeStruct((slots, 4, GROUPS, KEY_ROWS, 256), f32),
            jax.ShapeDtypeStruct((width // 128, rows, 128), f32),
        ],
        scratch_shapes=[pltpu.VMEM((width // 128, rows, 128), f32), pltpu.VMEM((PAD_IMG, width), bf16)],
        compiler_params=pltpu.CompilerParams(vmem_limit_bytes=56 << 20),
        cost_estimate=pl.CostEstimate(flops=20*10**9, bytes_accessed=1 << 24, transcendentals=0),
        name="attend_forward",
    )(images, weights, gains, shifts, biases, combined, take, put)


def gelu_parts(values):
    size = jnp.abs(values) * math.sqrt(0.5)
    bell = jnp.exp(-0.5 * values * values)
    turn = 1.0 / (1.0 + 0.3275911 * size)
    tail = 1.061405429
    for factor in (-1.453152027, 1.421413741, -0.284496736, 0.254829592):
        tail = tail * turn + factor
    tail = 0.5 * tail * turn * bell
    share = jnp.where(values < 0.0, tail, 1.0 - tail)
    return share, values * bell * (1.0 / math.sqrt(2.0 * math.pi))


def feed_kernel(
    count_ref, mine_ref, images_ref, cotangent_ref, mixed_ref, merge_ref, expand_ref, project_ref, gains_ref, shifts_ref,
    biases_ref, block_ref, grad_middle_ref, grad_mixed_ref, sums_ref, hidden_sums_ref, *grad_refs, slots, shard,
):
    merge_grad_ref, expand_grad_ref, project_grad_ref = grad_refs[-3:]
    step = pl.program_id(0)
    rows, width = cotangent_ref.shape
    pieces, _, piece = expand_ref.shape
    hidden = pieces * piece
    mixed = join_lanes(mixed_ref).astype(bf16)
    branch = dot(mixed, merge_ref[...]) + biases_ref[0:1, 3 * width : 4 * width]
    middle = images_ref[...].astype(f32) + branch
    slot = lax.broadcasted_iota(jnp.int32, (rows, 1), 0) % slots
    live = slot < count_ref[0]

    @pl.when(step == 0)
    def _():
        project_grad_ref[...] = jnp.zeros_like(project_grad_ref)
        expand_grad_ref[...] = jnp.zeros_like(expand_grad_ref)
        merge_grad_ref[...] = jnp.zeros_like(merge_grad_ref)
        sums_ref[...] = jnp.zeros_like(sums_ref)
        hidden_sums_ref[...] = jnp.zeros_like(hidden_sums_ref)

    hat, factor = normalize(middle)
    gain = gains_ref[1:2]
    normed = (hat * gain + shifts_ref[1:2]).astype(bf16)
    grad_out = jnp.where(live, cotangent_ref[...].astype(f32), 0.0)
    grad_low = grad_out.astype(bf16)
    out = biases_ref[0:1, 4 * width + hidden : 5 * width + hidden]
    back = 0.0
    for index in range(pieces):
        columns = slice(index * piece, (index + 1) * piece)
        offset = 4 * width + index * piece
        pre = dot(normed, expand_ref[index]) + biases_ref[0:1, offset : offset + piece]
        share, slope = gelu_parts(pre)
        active = (pre * share).astype(bf16)
        out = out + dot(active, project_ref[columns])
        project_grad_ref[columns] += dot(active, grad_low, 0, 0)
        grad_pre = (dot(grad_low, project_ref[columns], 1, 1) * (share + slope)).astype(bf16)
        expand_grad_ref[index] += dot(normed, grad_pre, 0, 0)
        hidden_sums_ref[0:1, columns] += jnp.sum(grad_pre.astype(f32), axis=0, keepdims=True)
        back = back + dot(grad_pre, expand_ref[index], 1, 1)
    block_ref[...] = jnp.where(live, middle + out, 0.0).astype(bf16)
    grad_middle = grad_out + normalize_back(back, gain, hat, factor)
    cut_lanes(grad_middle_ref, grad_middle)
    grad_branch = grad_middle.astype(bf16)
    merge_grad_ref[...] += dot(mixed, grad_branch, 0, 0)
    cut_lanes(grad_mixed_ref, dot(grad_branch, merge_ref[...], 1, 1))
    sums_ref[0:1] += jnp.sum(back * hat, axis=0, keepdims=True)
    sums_ref[1:2] += jnp.sum(back, axis=0, keepdims=True)
    sums_ref[2:3] += jnp.sum(grad_out, axis=0, keepdims=True)
    sums_ref[3:4] += jnp.sum(grad_branch.astype(f32), axis=0, keepdims=True)
    if shard:

        @pl.when(step == pl.num_programs(0) - 1)
        def _():
            sources = ((merge_grad_ref, 1), (expand_grad_ref, pieces), (project_grad_ref, 1))
            store_core(sources, grad_refs[0], grad_refs[1], BODY, shard, mine_ref[0])


def feed_forward(count, mine, images, cotangent, mixed, merge, expand, project, gains, shifts, biases, slots, tile, devices):
    rows, width = cotangent.shape
    hidden = project.shape[0]
    lanes = pl.BlockSpec((width // 128, tile, 128), lambda i: (0, i, 0))
    shard = width // devices
    raw = [(width, width), expand.shape, (hidden, width)]
    grad_shapes = [jax.ShapeDtypeStruct(shape, f32) for shape in raw]
    scratch = []
    if aligned(shard):
        grad_shapes = [
            jax.ShapeDtypeStruct((devices // 2, 9 * shard, width), f32),
            jax.ShapeDtypeStruct((devices // 2, 10 * shard, width), bf16),
        ]
        scratch = [pltpu.VMEM(shape, f32) for shape in raw]

    def tiled(columns):
        return pl.BlockSpec((tile, columns), lambda i: (i, 0))

    return pl.pallas_call(
        partial(feed_kernel, slots=slots, shard=shard if aligned(shard) else 0),
        grid=(rows // tile,),
        in_specs=[
            pl.BlockSpec(memory_space=pltpu.SMEM), pl.BlockSpec(memory_space=pltpu.SMEM), tiled(width), tiled(width), lanes,
            whole(merge.shape), whole(expand.shape),
            whole(project.shape), whole(gains.shape), whole(shifts.shape), whole(biases.shape),
        ],
        out_specs=[tiled(width), lanes, lanes, whole((8, width)), whole((8, hidden))]
        + [whole(shape.shape) for shape in grad_shapes],
        out_shape=[
            jax.ShapeDtypeStruct((rows, width), bf16),
            jax.ShapeDtypeStruct((width // 128, rows, 128), f32),
            jax.ShapeDtypeStruct((width // 128, rows, 128), f32),
            jax.ShapeDtypeStruct((8, width), f32),
            jax.ShapeDtypeStruct((8, hidden), f32),
        ]
        + grad_shapes,
        scratch_shapes=scratch,
        compiler_params=pltpu.CompilerParams(vmem_limit_bytes=60 << 20),
        cost_estimate=pl.CostEstimate(flops=44*10**9, bytes_accessed=1 << 24, transcendentals=0),
        name="feed_forward",
    )(count, mine, images, cotangent, mixed, merge, expand, project, gains, shifts, biases)


def attend_back_kernel(
    mine_ref, grad_mixed_ref, triple_ref, attention_ref, windows_ref, take_ref,
    grad_triple_ref, table_ref, sums_ref, *grad_refs, shard,
):
    attend_grad_ref = grad_refs[-1]
    step = pl.program_id(0)
    width = windows_ref.shape[-1]
    slots = grad_mixed_ref.shape[1] // PATCHES
    scale = 1.0 / math.sqrt(width // HEADS)

    @pl.when(step == 0)
    def _():
        attend_grad_ref[...] = jnp.zeros_like(attend_grad_ref)
        table_ref[...] = jnp.zeros_like(table_ref)
        sums_ref[...] = jnp.zeros_like(sums_ref)

    grad_mixed = dot(take_ref[...], load_image(grad_mixed_ref, step, slots).astype(bf16)).astype(bf16)
    masks = head_masks(bf16)
    masks_wide = head_masks(f32)
    pad = jnp.zeros((PAD_TOK - KEY_ROWS, 256), f32)
    for group in range(GROUPS):
        table = table_ref[group]
        for window in range(4):
            rows = slice(window * PAD_TOK, (window + 1) * PAD_TOK)
            query = triple_ref[0, rows, group * 128 : (group + 1) * 128]
            key = triple_ref[0, rows, width + group * 128 : width + (group + 1) * 128]
            value = triple_ref[0, rows, 2 * width + group * 128 : 2 * width + (group + 1) * 128]
            grad_heads = spread_heads(grad_mixed[rows, group * 128 : (group + 1) * 128], masks)
            attention = attention_ref[0, window, group]
            grad_attention = dot(value, grad_heads, 1, 1)[:KEY_ROWS]
            inner = jnp.sum(grad_attention * attention, axis=0, keepdims=True)
            grad_scores = attention * (grad_attention - inner)
            low = jnp.concatenate([grad_scores, pad], axis=0).astype(bf16)
            table = table + low.astype(f32)[:KEY_ROWS]
            attention_low = jnp.concatenate([attention, pad], axis=0).astype(bf16)
            grad_value = dot(attention_low, grad_heads)
            grad_key = dot(low, spread_heads(query, masks))
            grad_query = fold_heads(dot(low, key, 0, 0), masks_wide) * scale
            grad_triple_ref[0, rows, group * 128 : (group + 1) * 128] = grad_query.astype(bf16)
            grad_triple_ref[0, rows, width + group * 128 : width + (group + 1) * 128] = grad_key.astype(bf16)
            grad_triple_ref[0, rows, 2 * width + group * 128 : 2 * width + (group + 1) * 128] = grad_value.astype(bf16)
        table_ref[group] = table
    for part in range(3):
        columns = slice(part * width, (part + 1) * width)
        grad = grad_triple_ref[0, :, columns]
        attend_grad_ref[part] += dot(windows_ref[0], grad, 0, 0)
        sums_ref[0:1, columns] += jnp.sum(grad.astype(f32), axis=0, keepdims=True)
    if shard:

        @pl.when(step == pl.num_programs(0) - 1)
        def _():
            store_core(((attend_grad_ref, 3),), grad_refs[0], grad_refs[1], HEAD, shard, mine_ref[0])


def attend_backward(mine, devices, grad_mixed, triple, attention, windows, take):
    width = windows.shape[-1]
    slots = triple.shape[0]
    shard = width // devices
    grad_shapes, scratch = [jax.ShapeDtypeStruct((3, width, width), f32)], []
    if aligned(shard):
        grad_shapes = [
            jax.ShapeDtypeStruct((devices // 2, 3 * shard, width), f32),
            jax.ShapeDtypeStruct((devices // 2, 3 * shard, width), bf16),
        ]
        scratch = [pltpu.VMEM((3, width, width), f32)]
    return pl.pallas_call(
        partial(attend_back_kernel, shard=shard if aligned(shard) else 0),
        grid=(slots,),
        in_specs=[
            pl.BlockSpec(memory_space=pltpu.SMEM), whole(grad_mixed.shape), one((PAD_IMG, 3 * width)),
            one((4, GROUPS, KEY_ROWS, 256)), one((PAD_IMG, width)), whole(take.shape),
        ],
        out_specs=[one((PAD_IMG, 3 * width)), whole((GROUPS, KEY_ROWS, 256)), whole((8, 3 * width))]
        + [whole(shape.shape) for shape in grad_shapes],
        out_shape=[
            jax.ShapeDtypeStruct((slots, PAD_IMG, 3 * width), bf16),
            jax.ShapeDtypeStruct((GROUPS, KEY_ROWS, 256), f32),
            jax.ShapeDtypeStruct((8, 3 * width), f32),
        ]
        + grad_shapes,
        scratch_shapes=scratch,
        compiler_params=pltpu.CompilerParams(vmem_limit_bytes=56 << 20),
        cost_estimate=pl.CostEstimate(flops=37*10**9, bytes_accessed=1 << 24, transcendentals=0),
        name="attend_backward",
    )(mine, grad_mixed, triple, attention, windows, take)


def input_kernel(images_ref, grad_triple_ref, grad_middle_ref, weights_ref, gains_ref, put_ref, out_ref, sums_ref, features_ref, grads_ref):
    step = pl.program_id(0)
    width = images_ref.shape[-1]
    slots = images_ref.shape[0] // PATCHES

    @pl.when(step == 0)
    def _():
        sums_ref[...] = jnp.zeros_like(sums_ref)
        cut_lanes(features_ref, images_ref[...].astype(f32))

    hat, factor = normalize(load_image(features_ref, step, slots))
    grad = 0.0
    for part in range(3):
        grad = grad + dot(grad_triple_ref[0, :, part * width : (part + 1) * width], weights_ref[part], 1, 1)
    high = grad.astype(bf16)
    low = (grad - high.astype(f32)).astype(bf16)
    grad = dot(put_ref[...], high) + dot(put_ref[...], low)
    total = load_image(grad_middle_ref, step, slots) + normalize_back(grad, gains_ref[0:1], hat, factor)
    store_image(grads_ref, step, slots, total)
    sums_ref[0:1] += jnp.sum(grad * hat, axis=0, keepdims=True)
    sums_ref[1:2] += jnp.sum(grad, axis=0, keepdims=True)

    @pl.when(step == slots - 1)
    def _():
        out_ref[...] = join_lanes(grads_ref)


def input_backward(images, grad_triple, grad_middle, weights, gains, put):
    rows, width = images.shape
    slots = rows // PATCHES
    return pl.pallas_call(
        input_kernel,
        grid=(slots,),
        in_specs=[
            whole((rows, width)), one((PAD_IMG, 3 * width)), whole(grad_middle.shape),
            pl.BlockSpec((3, width, width), lambda i: (0, 0, 0)), whole(gains.shape), whole(put.shape),
        ],
        out_specs=[whole((rows, width)), whole((8, width))],
        out_shape=[
            jax.ShapeDtypeStruct((rows, width), f32),
            jax.ShapeDtypeStruct((8, width), f32),
        ],
        scratch_shapes=[pltpu.VMEM((width // 128, rows, 128), f32)] * 2,
        compiler_params=pltpu.CompilerParams(vmem_limit_bytes=56 << 20),
        cost_estimate=pl.CostEstimate(flops=14*10**9, bytes_accessed=1 << 24, transcendentals=0),
        name="input_backward",
    )(images, grad_triple, grad_middle, weights, gains, put)


def combine_bias(bias_table, rel_index, shift_mask):
    one_hot = (rel_index.reshape(-1)[:, None] == jnp.arange(TABLE)[None, :]).astype(f32)
    position = jnp.dot(one_hot, bias_table, precision=lax.Precision.HIGHEST).T
    position = position.reshape(GROUPS, 4, WIN_TOK, WIN_TOK)
    position = jnp.transpose(position, (0, 3, 1, 2))
    position = jnp.pad(
        position, ((0, 0), (0, KEY_ROWS - WIN_TOK), (0, 0), (0, PAD_TOK - WIN_TOK))
    ).reshape(GROUPS, KEY_ROWS, 256)
    mask = jnp.transpose(-100.0 * (1 - shift_mask).astype(f32), (0, 2, 1))
    mask = jnp.pad(mask, ((0, 0), (0, 0), (0, PAD_TOK - WIN_TOK)))
    mask = jnp.pad(mask, ((0, 0), (0, KEY_ROWS - WIN_TOK), (0, 0)), constant_values=NEVER)
    mask = jnp.tile(mask, (1, 1, 4))
    return position[None] + mask[:, None], one_hot


def table_gradient(table, one_hot):
    grad = table.reshape(GROUPS, KEY_ROWS, 4, PAD_TOK)[:, :WIN_TOK, :, :WIN_TOK]
    grad = jnp.transpose(grad, (3, 1, 0, 2)).reshape(WIN_TOK * WIN_TOK, HEADS)
    return jnp.dot(one_hot.T, grad, precision=lax.Precision.HIGHEST)


def flat_rows(images):
    return jnp.transpose(images, (1, 0, 2)).reshape(-1, images.shape[-1])


def image_form(rows, slots):
    return jnp.transpose(rows.reshape(-1, slots, rows.shape[-1]), (1, 0, 2))


def adamw_step(param, grad, first, second, steps):
    first_next = 0.9 * first + 0.1 * grad
    second_next = 0.999 * second + 0.001 * grad * grad
    first_hat = first_next / (1.0 - jnp.power(0.9, steps))
    second_hat = second_next / (1.0 - jnp.power(0.999, steps))
    update = -0.05 * (first_hat / (jnp.sqrt(second_hat) + 1e-08) + 0.05 * param)
    return (first_next, second_next, update)


def column_blocks(matrix):
    rows, columns = matrix.shape
    return jnp.transpose(matrix.reshape(rows, columns // LANE, LANE), (1, 0, 2))


def from_blocks(blocks):
    count, rows, lanes = blocks.shape
    return jnp.transpose(blocks, (1, 0, 2)).reshape(rows, count * lanes)


def local(
    images,
    cotangent,
    image_counts,
    shift_mask,
    rel_index,
    step_count,
    attend_weight,
    merge_weight,
    expand_weight,
    project_weight,
    norm_gains,
    norm_shifts,
    layer_biases,
    bias_table,
    attend_momentum,
    merge_momentum,
    expand_momentum,
    project_momentum,
    gains_mean,
    gains_square,
    shifts_mean,
    shifts_square,
    biases_mean,
    biases_square,
    table_mean,
    table_square,
):
    slots, patches, width = images.shape
    devices = lax.axis_size("dp")
    hidden_units = expand_weight.shape[1]
    grad_scale = 1.0 / math.sqrt(slots * devices * PATCHES)
    rank = lax.axis_index("dp")
    planes = devices // CELL
    plane = rank // CELL
    corner = (rank // 2) % 4
    shard = width // devices
    tall_shard = hidden_units // devices

    attend_rows = column_blocks(attend_weight).reshape(-1, LANE)
    other_rows = jnp.concatenate(
        [column_blocks(merge_weight).reshape(-1, LANE), column_blocks(expand_weight).reshape(-1, LANE), project_weight]
    )
    near = gather_planes(attend_rows, devices)
    near[0], other_rows = lax.optimization_barrier((near[0], other_rows))
    other_near = gather_planes(other_rows, devices)
    near = gather_corners(jnp.stack(near), devices)
    near[0], other_near[1] = lax.optimization_barrier((near[0], other_near[1]))
    near = jnp.stack(near)
    far = exchange(near, devices, 1)
    far, *other_near = lax.optimization_barrier((far, *other_near))
    other_near = gather_corners(jnp.stack(other_near), devices)
    (weights,) = order_rows(near, far, ((3, shard),), rank)

    take = jnp.asarray(window_matrix(), bf16)
    put = jnp.asarray(window_matrix().T, bf16)
    combined, one_hot = combine_bias(bias_table, rel_index, shift_mask)
    bias_row = layer_biases.reshape(1, -1)
    rows = flat_rows(images)
    windows, triple, attention, mixed = attend_forward(rows, weights, norm_gains, norm_shifts, bias_row, combined, take, put)
    mixed, *other_near = lax.optimization_barrier((mixed, *other_near))
    other_near = jnp.stack(other_near)
    other_far = exchange(other_near, devices, 1)
    merge, expand, project = order_rows(
        other_near, other_far, ((1, shard), (hidden_units // LANE, shard), (1, tall_shard)), rank
    )
    mine = (rank & 1).reshape(1)
    block_rows, grad_middle, grad_mixed, feed_sums, hidden_sums, *body_grads = feed_forward(
        image_counts, mine, rows, flat_rows(cotangent), mixed, merge[0], expand, project[0], norm_gains, norm_shifts, bias_row,
        slots, slots * patches // 2, devices,
    )
    block_out = image_form(block_rows, slots)
    if not aligned(shard):
        merge_term, expand_term, project_term = body_grads
        body_grads = pack_core([merge_term[None], expand_term, project_term[None]], BODY, shard, rank & 1)
    body_keep, body_sent = body_grads
    body_got = exchange(body_sent, devices, 1)
    body_own, body_sends = fold(by_corner(body_keep), [by_corner(body_got)], corner, BODY, shard)
    grad_mixed, *body_sends = lax.optimization_barrier((grad_mixed, *body_sends))
    body_got = send_all(body_sends, 2, devices)

    grad_triple, table_sums, triple_sums, *head_grads = attend_backward(
        mine, devices, grad_mixed, triple, attention, windows, take
    )
    if not aligned(shard):
        head_grads = pack_core(head_grads, HEAD, shard, rank & 1)
    head_keep, head_sent = head_grads
    head_got = exchange(head_sent, devices, 1)
    head_own, head_sends = fold(by_corner(head_keep), [by_corner(head_got)], corner, HEAD, shard)
    body_own, body_sends = fold(body_own[None], [got[None] for got in body_got], plane, BODY, shard)
    grad_triple, *sends = lax.optimization_barrier((grad_triple, *head_sends, *body_sends))
    head_got = send_all(sends[:3], 2, devices)
    body_got = send_all(sends[3:], CELL, devices)
    grad_triple, head_got[1] = lax.optimization_barrier((grad_triple, head_got[1]))
    input_rows, input_sums = input_backward(rows, grad_triple, grad_middle, weights, norm_gains, put)
    input_sums, head_got[0], head_got[2], *body_got = lax.optimization_barrier(
        (input_sums, head_got[0], head_got[2], *body_got)
    )
    input_grad = image_form(input_rows, slots)
    table_term = table_gradient(table_sums, one_hot)
    head_own, head_sends = fold(head_own[None], [got[None] for got in head_got], plane, HEAD, shard)
    head_got = send_all(head_sends, CELL, devices)
    momenta = (attend_momentum, merge_momentum, expand_momentum, project_momentum)
    grads, following, packed = finish(head_own, head_got, body_own, body_got, momenta, shard, grad_scale)

    small_parts = (
        jnp.stack([input_sums[0], feed_sums[0]]),
        jnp.stack([input_sums[1], feed_sums[1]]),
        jnp.concatenate([triple_sums[0], feed_sums[3], hidden_sums[0], feed_sums[2]]),
        table_term,
    )
    small = jnp.concatenate([part.reshape(-1) for part in small_parts])
    small = jnp.pad(small, (0, -small.shape[0] % (8 * LANE))).reshape(-1, LANE)

    length = tall_shard
    whole_rows, small = collect(packed, small, rank, devices)
    stack = whole_rows.reshape(CELL * planes, MATRICES, -1, LANE)
    stack = jnp.transpose(stack, (1, 0, 2, 3)).reshape(MATRICES, -1, LANE)
    kind = jnp.minimum(plane, MATRICES - 1).astype(jnp.int32).reshape(1)
    chunk = planes * length // MATRICES
    orth = newton_rows(stack, kind, chunk).reshape(MATRICES, planes, -1, LANE)
    pieces = [orth[:, 0]]
    for step in range(1, planes):
        pieces.append(exchange(orth[:, step], devices, CELL * step))
    received = jnp.stack(pieces)

    flat, start, small_sums = small.reshape(-1), 0, []
    for part in small_parts:
        small_sums.append(flat[start : start + part.size].reshape(part.shape))
        start += part.size
    small_grads = tuple((term * grad_scale for term in small_sums))
    results = [block_out, input_grad]
    for order, (grad, moment_next) in enumerate(zip(grads, following)):
        piece = pick(received, plane ^ order, 0)
        blocks = grad.shape[1] // LANE
        piece = piece.reshape(-1, LANE)[: blocks * grad.shape[0]].reshape(blocks, -1, LANE)
        extent = max(devices * grad.shape[0], grad.shape[1])
        update = -0.02 * math.sqrt(extent) * from_blocks(piece).astype(f32)
        results += [grad, moment_next, update]
    steps = step_count[0].astype(f32)
    params = (norm_gains, norm_shifts, layer_biases, bias_table)
    states = (
        (gains_mean, gains_square),
        (shifts_mean, shifts_square),
        (biases_mean, biases_square),
        (table_mean, table_square),
    )
    for param, grad, state in zip(params, small_grads, states):
        first_next, second_next, update = adamw_step(param, grad, state[0], state[1], steps)
        results += [grad, first_next, second_next, update]
    return tuple(results)


def solution(mesh):
    return jax.shard_map(
        local,
        mesh=mesh,
        in_specs=(
            P("dp", None, None),
            P("dp", None, None),
            P("dp"),
            P(),
            P(),
            P(),
            P("dp", None),
            P("dp", None),
            P("dp", None),
            P("dp", None),
            P(),
            P(),
            P(),
            P(),
            P("dp", None),
            P("dp", None),
            P("dp", None),
            P("dp", None),
            P(),
            P(),
            P(),
            P(),
            P(),
            P(),
            P(),
            P(),
        ),
        out_specs=(
            P("dp", None, None),
            P("dp", None, None),
            P("dp", None),
            P("dp", None),
            P("dp", None),
            P("dp", None),
            P("dp", None),
            P("dp", None),
            P("dp", None),
            P("dp", None),
            P("dp", None),
            P("dp", None),
            P("dp", None),
            P("dp", None),
            P(),
            P(),
            P(),
            P(),
            P(),
            P(),
            P(),
            P(),
            P(),
            P(),
            P(),
            P(),
            P(),
            P(),
            P(),
            P(),
        ),
        check_vma=False,
    )
```

```python
from functools import partial
import math

import jax
import jax.numpy as jnp
import numpy as np
from jax import lax
from jax.experimental import pallas as pl
from jax.experimental.pallas import tpu as pltpu
from jax.sharding import PartitionSpec as P

HEADS = 16
WIN = 7
SIDE = 14
SHIFT = 3
WIN_TOK = 49
PATCHES = 196
TABLE = 169


newton_first = 3.4445
newton_second = -4.775
newton_third = 2.0315


LANE = 512
CELL = 8
MATRICES = 4


def exchange(payload, devices, mask):
    return lax.ppermute(payload, "dp", [(i, i ^ mask) for i in range(devices)])


def pick(values, index, axis):
    return lax.dynamic_index_in_dim(values, index, axis, keepdims=False)


def split_wide(values):
    high = lax.reduce_precision(values, 8, 7)
    return high.astype(jnp.bfloat16), lax.reduce_precision(values - high, 8, 7).astype(jnp.bfloat16)


def join_wide(high, low):
    return high.astype(jnp.float32) + low.astype(jnp.float32)


def place_rows(rank, sources, outs, spans):
    for number, source in enumerate(sources):
        for plane in range(source.shape[0]):
            owner = jnp.bitwise_xor(rank, number // 4 + 2 * (number % 4) + CELL * plane)
            start = 0
            for out_ref, (blocks, rows) in zip(outs, spans):
                place = pl.ds(pl.multiple_of(owner * rows, rows), rows)
                for block in range(blocks):
                    out_ref[block, place, :] = source[plane, start : start + rows, :]
                    start += rows


def order_rows(sources, spans, rank, devices):
    lanes = sources[0].shape[-1]
    offset = jnp.arange(devices) ^ rank
    both = jnp.stack(sources).reshape(devices, -1, lanes)
    both = jnp.take(both, ((offset & 1) * 4 + ((offset >> 1) & 3)) * (devices // CELL) + (offset >> 3), axis=0)
    out, start = [], 0
    for blocks, rows in spans:
        part = both[:, start : start + blocks * rows].reshape(devices, blocks, rows, lanes)
        out.append(jnp.transpose(part, (1, 0, 2, 3)).reshape(blocks, devices * rows, lanes))
        start += blocks * rows
    return out


def gather_planes(rows, devices):
    return [rows] + [exchange(rows, devices, CELL * step) for step in range(1, devices // CELL)]


def gather_corners(rows, devices):
    return [rows] + [exchange(rows, devices, 2 * step) for step in range(1, 4)]


BODY = ((1, True), (4, False), (4, False))
HEAD = ((3, False),)


def encode(values, spans, rows):
    sent, start = [], 0
    for blocks, wide in spans:
        part = values[..., start : start + blocks * rows, :]
        start += blocks * rows
        high = part.astype(jnp.bfloat16)
        sent.append(high)
        if wide:
            sent.append((part - high.astype(jnp.float32)).astype(jnp.bfloat16))
    return sent[0] if len(sent) == 1 else jnp.concatenate(sent, axis=-2)


def decode(payload, spans, rows):
    out, start = [], 0
    for blocks, wide in spans:
        part = payload[..., start : start + blocks * rows, :].astype(jnp.float32)
        start += blocks * rows
        if wide:
            part = part + payload[..., start : start + blocks * rows, :].astype(jnp.float32)
            start += blocks * rows
        out.append(part)
    return out[0] if len(out) == 1 else jnp.concatenate(out, axis=-2)


def aligned(rows):
    return rows % 16 == 0


def pack_core(parts, spans, rows, mine):
    packed = []
    for (blocks, _), part in zip(spans, parts):
        count = part.shape[0]
        per = blocks * rows // count
        part = part.reshape(count, -1, 2, per, LANE)
        packed.append(jnp.transpose(part, (1, 2, 0, 3, 4)).reshape(part.shape[1], 2, blocks * rows, LANE))
    packed = jnp.concatenate(packed, axis=2)
    return pick(packed, mine, 1), encode(pick(packed, 1 - mine, 1), spans, rows)


def store_core(sources, keep_ref, sent_ref, spans, rows, mine):
    for pair in range(keep_ref.shape[0]):
        start, sent = 0, 0
        for (blocks, wide), (source, count) in zip(spans, sources):
            per = blocks * rows // count
            near = pl.ds(pl.multiple_of(pair * 2 * per + mine * per, per), per)
            away = pl.ds(pl.multiple_of(pair * 2 * per + (1 - mine) * per, per), per)
            for block in range(count):
                lead = (block,) if len(source.shape) == 3 else ()
                keep_ref[pair, start : start + per, :] = source[lead + (near, slice(None))]
                values = source[lead + (away, slice(None))]
                high = values.astype(jnp.bfloat16)
                sent_ref[pair, sent : sent + per, :] = high
                if wide:
                    low = (values - high.astype(jnp.float32)).astype(jnp.bfloat16)
                    sent_ref[pair, sent + blocks * rows : sent + blocks * rows + per, :] = low
                start += per
                sent += per
            if wide:
                sent += blocks * rows


def fold_kernel(own_ref, keep_ref, *refs, gots, spans, rows):
    own = own_ref[0]
    total_ref, *sent_refs = refs[gots:]
    for step in range(keep_ref.shape[1]):
        index = jnp.bitwise_xor(own, step)
        total = keep_ref[0, index]
        for got in refs[:gots]:
            total = total + decode(got[0, index], spans, rows)
        if step:
            sent_refs[step - 1][0] = encode(total, spans, rows)
        else:
            total_ref[0] = total


def fold(keep, got, own, spans, rows):
    groups, members, length, lanes = keep.shape
    if not aligned(rows):
        total = keep
        for payload in got:
            total = total + decode(payload, spans, rows)
        return pick(total, own, 1), [encode(pick(total, own ^ step, 1), spans, rows) for step in range(1, members)]
    sent = got[0].shape[2]

    def block(*shape):
        return pl.BlockSpec((1,) + shape, lambda i: (i,) + (0,) * len(shape))

    total, *sends = pl.pallas_call(
        partial(fold_kernel, gots=len(got), spans=spans, rows=rows),
        grid=(groups,),
        in_specs=[pl.BlockSpec(memory_space=pltpu.SMEM), block(members, length, lanes)]
        + [block(members, sent, lanes)] * len(got),
        out_specs=[block(length, lanes)] + [block(sent, lanes)] * (members - 1),
        out_shape=[jax.ShapeDtypeStruct((groups, length, lanes), jnp.float32)]
        + [jax.ShapeDtypeStruct((groups, sent, lanes), jnp.bfloat16)] * (members - 1),
        compiler_params=pltpu.CompilerParams(vmem_limit_bytes=8 << 20),
        cost_estimate=pl.CostEstimate(flops=2 * 10**9, bytes_accessed=8 * keep.size, transcendentals=0),
        name="fold",
    )(own.reshape(1), keep, *got)
    return total, sends


def send_all(payloads, mask, devices):
    return [exchange(payload, devices, mask * (step + 1)) for step, payload in enumerate(payloads)]


def finish_math(head, head_got, body, body_got, momenta, rows, grad_scale):
    for payload in head_got:
        head = head + decode(payload, HEAD, rows)
    for payload in body_got:
        body = body + decode(payload, BODY, rows)
    spans = (head, body[:rows], body[rows : 5 * rows], body[5 * rows :])
    grads, following, packed = [], [], []
    for order, (span, moment) in enumerate(zip(spans, momenta)):
        blocks = moment.shape[1] // LANE
        per = moment.shape[0]
        grad = jnp.concatenate([span[block * per : (block + 1) * per] for block in range(blocks)], axis=1) * grad_scale
        after = 0.95 * moment + grad
        grads.append(grad)
        following.append(after)
        pieces = [after[:, block * LANE : (block + 1) * LANE] for block in range(blocks)]
        if order == 1:
            high = after.astype(jnp.bfloat16)
            pieces = [high, after - high.astype(jnp.float32)]
        pieces = [piece.astype(jnp.bfloat16) for piece in pieces]
        if per * len(pieces) < 4 * rows:
            pieces.append(jnp.zeros((4 * rows - per * len(pieces), LANE), jnp.bfloat16))
        packed.append(jnp.concatenate(pieces, axis=0))
    return grads, following, packed


def finish_kernel(*refs, count, rows, grad_scale):
    head, body = refs[0][0], refs[1][0]
    head_got = [ref[0] for ref in refs[2 : 2 + count]]
    body_got = [ref[0] for ref in refs[2 + count : 2 + 2 * count]]
    momenta = [ref[...] for ref in refs[2 + 2 * count : 6 + 2 * count]]
    outs = refs[6 + 2 * count :]
    grads, following, packed = finish_math(head, head_got, body, body_got, momenta, rows, grad_scale)
    for index in range(4):
        outs[index][...] = grads[index]
        outs[4 + index][...] = following[index]
        outs[8][index] = packed[index]


def finish(head, head_got, body, body_got, momenta, rows, grad_scale):
    if not aligned(rows):
        grads, following, packed = finish_math(
            head[0], [got[0] for got in head_got], body[0], [got[0] for got in body_got], momenta, rows, grad_scale
        )
        return grads, following, jnp.stack(packed)
    shapes = [jax.ShapeDtypeStruct(moment.shape, jnp.float32) for moment in momenta]
    outs = pl.pallas_call(
        partial(finish_kernel, count=len(head_got), rows=rows, grad_scale=grad_scale),
        out_shape=shapes + shapes + [jax.ShapeDtypeStruct((4, 4 * rows, LANE), jnp.bfloat16)],
        compiler_params=pltpu.CompilerParams(vmem_limit_bytes=8 << 20),
        cost_estimate=pl.CostEstimate(flops=10**9, bytes_accessed=1 << 22, transcendentals=0),
        name="finish",
    )(head, body, *head_got, *body_got, *momenta)
    return outs[:4], outs[4:8], outs[8]


def by_corner(packed):
    return packed.reshape((-1, 4) + packed.shape[1:])


def newton_kernel(kind_ref, stack_ref, out_ref, gram_ref, rows_ref):
    kind = kind_ref[0]
    blocks, side, _ = stack_ref.shape
    chunk = out_ref.shape[1]
    tall = kind == 3
    paired = kind == 1

    @pl.when(tall)
    def _():
        total = dot(stack_ref[0], stack_ref[0], 0, 0)
        for block in range(1, blocks):
            total = total + dot(stack_ref[block], stack_ref[block], 0, 0)
        gram_ref[...] = total

    @pl.when(paired)
    def _():
        cross = dot(stack_ref[0], stack_ref[1], 1, 1)
        cross = cross + dot(stack_ref[1], stack_ref[0], 1, 1)
        gram_ref[...] = dot(stack_ref[0], stack_ref[0], 1, 1) + cross

    @pl.when(jnp.logical_not(jnp.logical_or(tall, paired)))
    def _():
        total = dot(stack_ref[0], stack_ref[0], 1, 1)
        for block in range(1, blocks):
            total = total + dot(stack_ref[block], stack_ref[block], 1, 1)
        gram_ref[...] = total

    row = lax.broadcasted_iota(jnp.int32, (side, side), 0)
    column = lax.broadcasted_iota(jnp.int32, (side, side), 1)
    eye = (row == column).astype(jnp.float32)
    gram = gram_ref[...]
    inverse = 1.0 / (jnp.sqrt(jnp.sum(gram * eye)) + 1e-07)
    gram_ref[...] = gram * (inverse * inverse)

    @pl.when(tall)
    def _():
        for block in range(blocks):
            rows_ref[block * chunk : (block + 1) * chunk] = stack_ref[block, :chunk].astype(jnp.float32) * inverse

    @pl.when(jnp.logical_not(tall))
    def _():
        rows_ref[...] = eye[: blocks * chunk] * inverse

    def halves(values):
        high = values.astype(jnp.bfloat16)
        return high, (values - high.astype(jnp.float32)).astype(jnp.bfloat16)

    def product(left, right):
        return dot(left[0], right[0]) + (dot(left[1], right[0]) + dot(left[0], right[1]))

    def mix(gram, parts):
        return halves(newton_first * eye + newton_second * gram + newton_third * product(parts, parts))

    def sweep(step, carry):
        gram = gram_ref[...]
        parts = halves(gram)
        mixer = mix(gram, parts)
        rows_ref[...] = product(halves(rows_ref[...]), mixer)
        gram_ref[...] = product(halves(product(parts, mixer)), mixer)
        return carry

    lax.fori_loop(0, 4, sweep, 0)
    gram = gram_ref[...]
    rows = product(halves(rows_ref[...]), mix(gram, halves(gram)))

    @pl.when(tall)
    def _():
        for block in range(blocks):
            out_ref[block] = rows[block * chunk : (block + 1) * chunk].astype(out_ref.dtype)

    @pl.when(jnp.logical_not(tall))
    def _():
        own = halves(rows[:chunk])
        first = dot(own[0], stack_ref[0]) + dot(own[1], stack_ref[0])
        second = dot(own[0], stack_ref[1])
        out_ref[0] = jnp.where(paired, first + second, first).astype(out_ref.dtype)
        out_ref[1] = (second + dot(own[1], stack_ref[1])).astype(out_ref.dtype)
        for block in range(2, blocks):
            out_ref[block] = (dot(own[0], stack_ref[block]) + dot(own[1], stack_ref[block])).astype(out_ref.dtype)


def newton_rows(stack, kind, chunk):
    blocks, side, lanes = stack.shape
    return pl.pallas_call(
        newton_kernel,
        out_shape=jax.ShapeDtypeStruct((blocks, chunk, lanes), jnp.bfloat16),
        in_specs=[
            pl.BlockSpec(memory_space=pltpu.SMEM),
            pl.BlockSpec(memory_space=pltpu.VMEM),
        ],
        out_specs=pl.BlockSpec(memory_space=pltpu.VMEM),
        scratch_shapes=[pltpu.VMEM((side, side), jnp.float32), pltpu.VMEM((blocks * chunk, side), jnp.float32)],
        compiler_params=pltpu.CompilerParams(vmem_limit_bytes=48 << 20),
        cost_estimate=pl.CostEstimate(flops=20 * 10**9, bytes_accessed=1 << 22, transcendentals=0),
        name="newton_rows",
    )(kind, stack)


def add_tree(values):
    while len(values) > 1:
        values = [left + right for left, right in zip(values[::2], values[1::2])]
    return values[0]


def collect(packed, small, rank, devices):
    planes = devices // CELL
    plane = rank // CELL
    rows = packed.shape[1]
    count = small.shape[0]

    def pair(values):
        high, low = split_wide(values)
        return jnp.concatenate([high, low])

    def value(sent):
        return join_wide(sent[:count], sent[count:])

    sent = pair(small)
    pieces, sums = [pick(packed, jnp.minimum(plane, MATRICES - 1), 0)], [value(sent)]
    for step in range(1, planes):
        give = pick(packed, jnp.minimum(plane ^ step, MATRICES - 1), 0)
        got = exchange(jnp.concatenate([give, sent]), devices, CELL * step)
        pieces.append(got[:rows])
        sums.append(value(got[rows:]))
    current = jnp.concatenate(pieces)
    total = add_tree(sums)
    for mask in (4, 2, 1):
        sent = pair(total)
        got = exchange(jnp.concatenate([current, sent]), devices, mask)
        length = current.shape[0]
        current = jnp.concatenate([current, got[:length]])
        total = value(sent) + value(got[length:])
    return current.reshape(CELL, planes, rows, LANE), total


PAD_TOK = 64
KEY_ROWS = 56
PAD_IMG = 256
GROUPS = 4
NEVER = -1e30
f32 = jnp.float32
bf16 = jnp.bfloat16


def window_matrix():
    table = np.zeros((PAD_IMG, PATCHES), np.float32)
    blocks = SIDE // WIN
    for window in range(blocks * blocks):
        for token in range(WIN_TOK):
            row = (window // blocks) * WIN + token // WIN
            column = (window % blocks) * WIN + token % WIN
            patch = ((row + SHIFT) % SIDE) * SIDE + (column + SHIFT) % SIDE
            table[window * PAD_TOK + token, patch] = 1.0
    return table


def dot(left, right, left_dim=1, right_dim=0):
    return lax.dot_general(
        left, right, (((left_dim,), (right_dim,)), ((), ())), preferred_element_type=jnp.float32
    )


def normalize(values):
    center = values - jnp.mean(values, axis=-1, keepdims=True)
    spread = jnp.mean(center * center, axis=-1, keepdims=True)
    factor = lax.rsqrt(spread + 1e-05)
    return center * factor, factor


def normalize_back(grad, gain, hat, factor):
    inner = grad * gain
    return factor * (
        inner
        - jnp.mean(inner, axis=-1, keepdims=True)
        - hat * jnp.mean(inner * hat, axis=-1, keepdims=True)
    )


def head_masks(dtype):
    lane = lax.broadcasted_iota(jnp.int32, (1, 128), 1) // 32
    return [(lane == head).astype(dtype) for head in range(GROUPS)]


def spread_heads(rows, masks):
    return jnp.concatenate([rows * mask for mask in masks], axis=0)


def fold_heads(blocks, masks):
    total = None
    for head, mask in enumerate(masks):
        part = blocks[head * PAD_TOK : (head + 1) * PAD_TOK] * mask
        total = part if total is None else total + part
    return total


def load_image(ref, image, slots):
    return jnp.concatenate([ref[lane, pl.ds(image, PATCHES, stride=slots), :] for lane in range(ref.shape[0])], axis=1)


def store_image(ref, image, slots, values):
    for lane in range(ref.shape[0]):
        ref[lane, pl.ds(image, PATCHES, stride=slots), :] = values[:, lane * 128 : (lane + 1) * 128]


def cut_lanes(ref, values):
    for lane in range(ref.shape[0]):
        ref[lane] = values[:, lane * 128 : (lane + 1) * 128]


def join_lanes(ref):
    return jnp.concatenate([ref[lane] for lane in range(ref.shape[0])], axis=1)


def attend_kernel(
    rank_ref, images_ref, gains_ref, shifts_ref, biases_ref, combined_ref, take_ref, put_ref, *refs, pieces, shard,
):
    windows_ref, triple_ref, attention_ref, mixed_ref, weights_ref, features_ref, scratch_ref = refs[pieces:]
    step = pl.program_id(0)
    width = images_ref.shape[-1]
    slots = images_ref.shape[0] // PATCHES
    scale = 1.0 / math.sqrt(width // HEADS)

    @pl.when(step == 0)
    def _():
        cut_lanes(features_ref, images_ref[...].astype(f32))
        if pieces > 1:
            place_rows(rank_ref[0], refs[:pieces], (weights_ref,), ((3, shard),))
        else:
            weights_ref[...] = refs[0][...]

    masks = head_masks(bf16)
    masks_wide = head_masks(f32)
    count = windows_ref.shape[0]
    for sub in range(count):
        image = step * count + sub
        features = load_image(features_ref, image, slots)
        hat, _ = normalize(features)
        normed = (hat * gains_ref[0:1] + shifts_ref[0:1]).astype(bf16)
        windows = dot(take_ref[...], normed).astype(bf16)
        windows_ref[sub] = windows
        for part in range(3):
            columns = slice(part * width, (part + 1) * width)
            values = dot(windows, weights_ref[part]) + biases_ref[0:1, columns]
            if part == 0:
                values = values * scale
            triple_ref[sub, :, columns] = values.astype(bf16)
        for window in range(4):
            rows = slice(window * PAD_TOK, (window + 1) * PAD_TOK)
            for group in range(GROUPS):
                lanes = slice(group * 128, (group + 1) * 128)
                query = triple_ref[sub, rows, group * 128 : (group + 1) * 128]
                key = triple_ref[sub, rows, width + group * 128 : width + (group + 1) * 128]
                value = triple_ref[sub, rows, 2 * width + group * 128 : 2 * width + (group + 1) * 128]
                scores = dot(key, spread_heads(query, masks), 1, 1)[:KEY_ROWS] + combined_ref[window, group]
                top = jnp.max(scores, axis=0, keepdims=True)
                raised = jnp.exp(scores - top)
                attention = raised * (1.0 / jnp.sum(raised, axis=0, keepdims=True))
                low = jnp.concatenate([attention, jnp.zeros((PAD_TOK - KEY_ROWS, attention.shape[1]), f32)], axis=0).astype(bf16)
                attention_ref[sub, window, group] = low
                out = dot(low, value, 0, 0)
                scratch_ref[sub, rows, lanes] = fold_heads(out, masks_wide).astype(bf16)
        store_image(mixed_ref, image, slots, dot(put_ref[...], scratch_ref[sub]))


def whole(shape):
    return pl.BlockSpec(shape, lambda i: (0,) * len(shape))


def one(shape, count=1):
    return pl.BlockSpec((count,) + shape, lambda i: (i,) + (0,) * len(shape))


def attend_forward(rank, sources, shard, images, gains, shifts, biases, combined, take, put):
    rows, width = images.shape
    slots = rows // PATCHES
    return pl.pallas_call(
        partial(attend_kernel, pieces=len(sources), shard=shard),
        grid=(slots // 2,),
        in_specs=[
            pl.BlockSpec(memory_space=pltpu.SMEM), whole(images.shape), whole(gains.shape), whole(shifts.shape),
            whole(biases.shape), whole(combined.shape), whole(take.shape), whole(put.shape),
        ]
        + [whole(source.shape) for source in sources],
        out_specs=[
            one((PAD_IMG, width), 2), one((PAD_IMG, 3 * width), 2), one((4, GROUPS, PAD_TOK, 256), 2),
            whole((width // 128, rows, 128)), whole((3, width, width)),
        ],
        out_shape=[
            jax.ShapeDtypeStruct((slots, PAD_IMG, width), bf16),
            jax.ShapeDtypeStruct((slots, PAD_IMG, 3 * width), bf16),
            jax.ShapeDtypeStruct((slots, 4, GROUPS, PAD_TOK, 256), bf16),
            jax.ShapeDtypeStruct((width // 128, rows, 128), f32),
            jax.ShapeDtypeStruct((3, width, width), bf16),
        ],
        scratch_shapes=[pltpu.VMEM((width // 128, rows, 128), f32), pltpu.VMEM((2, PAD_IMG, width), bf16)],
        compiler_params=pltpu.CompilerParams(vmem_limit_bytes=60 << 20),
        cost_estimate=pl.CostEstimate(flops=20*10**9, bytes_accessed=1 << 24, transcendentals=0),
        name="attend_forward",
    )(rank, images, gains, shifts, biases, combined, take, put, *sources)


def gelu_parts(values):
    size = jnp.abs(values) * math.sqrt(0.5)
    bell = jnp.exp(-0.5 * values * values)
    turn = 1.0 / (1.0 + 0.3275911 * size)
    tail = 1.061405429
    for factor in (-1.453152027, 1.421413741, -0.284496736, 0.254829592):
        tail = tail * turn + factor
    tail = 0.5 * tail * turn * bell
    share = jnp.where(values < 0.0, tail, 1.0 - tail)
    return share, values * bell * (1.0 / math.sqrt(2.0 * math.pi))


def feed_kernel(
    count_ref, rank_ref, images_ref, cotangent_ref, mixed_ref, gains_ref, shifts_ref, biases_ref, *refs, slots, shard, sources,
):
    block_ref, grad_middle_ref, grad_mixed_ref, sums_ref, hidden_sums_ref, *grad_refs = refs[sources:]
    merge_ref, expand_ref, project_ref = grad_refs[2:5] if shard else refs[:3]
    merge_grad_ref, expand_grad_ref, project_grad_ref = grad_refs[-3:]
    step = pl.program_id(0)
    rows, width = cotangent_ref.shape
    pieces, _, piece = expand_ref.shape
    hidden = pieces * piece
    @pl.when(step == 0)
    def _():
        project_grad_ref[...] = jnp.zeros_like(project_grad_ref)
        expand_grad_ref[...] = jnp.zeros_like(expand_grad_ref)
        merge_grad_ref[...] = jnp.zeros_like(merge_grad_ref)
        sums_ref[...] = jnp.zeros_like(sums_ref)
        hidden_sums_ref[...] = jnp.zeros_like(hidden_sums_ref)
        if shard:
            spans = ((1, shard), (pieces, shard), (1, project_ref.shape[1] // (width // shard)))
            place_rows(rank_ref[0], refs[:sources], (merge_ref, expand_ref, project_ref), spans)

    mixed = join_lanes(mixed_ref).astype(bf16)
    branch = dot(mixed, merge_ref[0]) + biases_ref[0:1, 3 * width : 4 * width]
    middle = images_ref[...].astype(f32) + branch
    slot = lax.broadcasted_iota(jnp.int32, (rows, 1), 0) % slots
    live = slot < count_ref[0]

    hat, factor = normalize(middle)
    gain = gains_ref[1:2]
    normed = (hat * gain + shifts_ref[1:2]).astype(bf16)
    grad_out = jnp.where(live, cotangent_ref[...].astype(f32), 0.0)
    grad_low = grad_out.astype(bf16)
    out = biases_ref[0:1, 4 * width + hidden : 5 * width + hidden]
    back = 0.0
    for index in range(pieces):
        columns = slice(index * piece, (index + 1) * piece)
        offset = 4 * width + index * piece
        pre = dot(normed, expand_ref[index]) + biases_ref[0:1, offset : offset + piece]
        share, slope = gelu_parts(pre)
        active = (pre * share).astype(bf16)
        out = out + dot(active, project_ref[0, columns])
        project_grad_ref[columns] += dot(active, grad_low, 0, 0)
        grad_pre = (dot(grad_low, project_ref[0, columns], 1, 1) * (share + slope)).astype(bf16)
        expand_grad_ref[index] += dot(normed, grad_pre, 0, 0)
        hidden_sums_ref[0:1, columns] += jnp.sum(grad_pre.astype(f32), axis=0, keepdims=True)
        back = back + dot(grad_pre, expand_ref[index], 1, 1)
    block_ref[...] = jnp.where(live, middle + out, 0.0).astype(bf16)
    grad_middle = grad_out + normalize_back(back, gain, hat, factor)
    cut_lanes(grad_middle_ref, grad_middle)
    grad_branch = grad_middle.astype(bf16)
    merge_grad_ref[...] += dot(mixed, grad_branch, 0, 0)
    cut_lanes(grad_mixed_ref, dot(grad_branch, merge_ref[0], 1, 1))
    sums_ref[0:1] += jnp.sum(back * hat, axis=0, keepdims=True)
    sums_ref[1:2] += jnp.sum(back, axis=0, keepdims=True)
    sums_ref[2:3] += jnp.sum(grad_out, axis=0, keepdims=True)
    sums_ref[3:4] += jnp.sum(grad_branch.astype(f32), axis=0, keepdims=True)
    if shard:

        @pl.when(step == pl.num_programs(0) - 1)
        def _():
            sources = ((merge_grad_ref, 1), (expand_grad_ref, pieces), (project_grad_ref, 1))
            store_core(sources, grad_refs[0], grad_refs[1], BODY, shard, rank_ref[0] & 1)


def feed_forward(count, rank, sources, hidden, images, cotangent, mixed, gains, shifts, biases, slots, tile, devices):
    rows, width = cotangent.shape
    expand_shape = (hidden // LANE, width, LANE)
    lanes = pl.BlockSpec((width // 128, tile, 128), lambda i: (0, i, 0))
    shard = width // devices
    raw = [(width, width), expand_shape, (hidden, width)]
    grad_shapes = [jax.ShapeDtypeStruct(shape, f32) for shape in raw]
    scratch = []
    if aligned(shard):
        grad_shapes = [
            jax.ShapeDtypeStruct((devices // 2, 9 * shard, width), f32),
            jax.ShapeDtypeStruct((devices // 2, 10 * shard, width), bf16),
        ]
        scratch = [pltpu.VMEM(shape, bf16) for shape in ((1, width, width), expand_shape, (1, hidden, width))]
        scratch += [pltpu.VMEM(shape, f32) for shape in raw]

    def tiled(columns):
        return pl.BlockSpec((tile, columns), lambda i: (i, 0))

    return pl.pallas_call(
        partial(feed_kernel, slots=slots, shard=shard if aligned(shard) else 0, sources=len(sources)),
        grid=(rows // tile,),
        in_specs=[
            pl.BlockSpec(memory_space=pltpu.SMEM), pl.BlockSpec(memory_space=pltpu.SMEM), tiled(width), tiled(width), lanes,
            whole(gains.shape), whole(shifts.shape), whole(biases.shape),
        ]
        + [whole(source.shape) for source in sources],
        out_specs=[tiled(width), lanes, lanes, whole((8, width)), whole((8, hidden))]
        + [whole(shape.shape) for shape in grad_shapes],
        out_shape=[
            jax.ShapeDtypeStruct((rows, width), bf16),
            jax.ShapeDtypeStruct((width // 128, rows, 128), f32),
            jax.ShapeDtypeStruct((width // 128, rows, 128), f32),
            jax.ShapeDtypeStruct((8, width), f32),
            jax.ShapeDtypeStruct((8, hidden), f32),
        ]
        + grad_shapes,
        scratch_shapes=scratch,
        compiler_params=pltpu.CompilerParams(vmem_limit_bytes=60 << 20),
        cost_estimate=pl.CostEstimate(flops=44*10**9, bytes_accessed=1 << 24, transcendentals=0),
        name="feed_forward",
    )(count, rank, images, cotangent, mixed, gains, shifts, biases, *sources)


def attend_back_kernel(
    mine_ref, grad_mixed_ref, triple_ref, attention_ref, windows_ref, take_ref,
    grad_triple_ref, table_ref, sums_ref, *grad_refs, shard,
):
    attend_grad_ref = grad_refs[-1]
    step = pl.program_id(0)
    width = windows_ref.shape[-1]
    slots = grad_mixed_ref.shape[1] // PATCHES
    scale = 1.0 / math.sqrt(width // HEADS)

    @pl.when(step == 0)
    def _():
        attend_grad_ref[...] = jnp.zeros_like(attend_grad_ref)
        table_ref[...] = jnp.zeros_like(table_ref)
        sums_ref[...] = jnp.zeros_like(sums_ref)

    grad_mixed = dot(take_ref[...], load_image(grad_mixed_ref, step, slots).astype(bf16)).astype(bf16)
    masks = head_masks(bf16)
    masks_wide = head_masks(f32)
    pad = jnp.zeros((PAD_TOK - KEY_ROWS, 256), f32)
    for group in range(GROUPS):
        table = table_ref[group]
        for window in range(4):
            rows = slice(window * PAD_TOK, (window + 1) * PAD_TOK)
            query = triple_ref[0, rows, group * 128 : (group + 1) * 128]
            key = triple_ref[0, rows, width + group * 128 : width + (group + 1) * 128]
            value = triple_ref[0, rows, 2 * width + group * 128 : 2 * width + (group + 1) * 128]
            grad_heads = spread_heads(grad_mixed[rows, group * 128 : (group + 1) * 128], masks)
            attention_low = attention_ref[0, window, group]
            attention = attention_low.astype(f32)[:KEY_ROWS]
            grad_attention = dot(value, grad_heads, 1, 1)[:KEY_ROWS]
            inner = jnp.sum(grad_attention * attention, axis=0, keepdims=True)
            grad_scores = attention * (grad_attention - inner)
            low = jnp.concatenate([grad_scores, pad], axis=0).astype(bf16)
            table = table + low.astype(f32)[:KEY_ROWS]
            grad_value = dot(attention_low, grad_heads)
            grad_key = dot(low, spread_heads(query, masks))
            grad_query = fold_heads(dot(low, key, 0, 0), masks_wide) * scale
            grad_triple_ref[0, rows, group * 128 : (group + 1) * 128] = grad_query.astype(bf16)
            grad_triple_ref[0, rows, width + group * 128 : width + (group + 1) * 128] = grad_key.astype(bf16)
            grad_triple_ref[0, rows, 2 * width + group * 128 : 2 * width + (group + 1) * 128] = grad_value.astype(bf16)
        table_ref[group] = table
    for part in range(3):
        columns = slice(part * width, (part + 1) * width)
        grad = grad_triple_ref[0, :, columns]
        attend_grad_ref[part] += dot(windows_ref[0], grad, 0, 0)
        sums_ref[0:1, columns] += jnp.sum(grad.astype(f32), axis=0, keepdims=True)
    if shard:

        @pl.when(step == pl.num_programs(0) - 1)
        def _():
            store_core(((attend_grad_ref, 3),), grad_refs[0], grad_refs[1], HEAD, shard, mine_ref[0])


def attend_backward(mine, devices, grad_mixed, triple, attention, windows, take):
    width = windows.shape[-1]
    slots = triple.shape[0]
    shard = width // devices
    grad_shapes, scratch = [jax.ShapeDtypeStruct((3, width, width), f32)], []
    if aligned(shard):
        grad_shapes = [
            jax.ShapeDtypeStruct((devices // 2, 3 * shard, width), f32),
            jax.ShapeDtypeStruct((devices // 2, 3 * shard, width), bf16),
        ]
        scratch = [pltpu.VMEM((3, width, width), f32)]
    return pl.pallas_call(
        partial(attend_back_kernel, shard=shard if aligned(shard) else 0),
        grid=(slots,),
        in_specs=[
            pl.BlockSpec(memory_space=pltpu.SMEM), whole(grad_mixed.shape), one((PAD_IMG, 3 * width)),
            one((4, GROUPS, PAD_TOK, 256)), one((PAD_IMG, width)), whole(take.shape),
        ],
        out_specs=[one((PAD_IMG, 3 * width)), whole((GROUPS, KEY_ROWS, 256)), whole((8, 3 * width))]
        + [whole(shape.shape) for shape in grad_shapes],
        out_shape=[
            jax.ShapeDtypeStruct((slots, PAD_IMG, 3 * width), bf16),
            jax.ShapeDtypeStruct((GROUPS, KEY_ROWS, 256), f32),
            jax.ShapeDtypeStruct((8, 3 * width), f32),
        ]
        + grad_shapes,
        scratch_shapes=scratch,
        compiler_params=pltpu.CompilerParams(vmem_limit_bytes=60 << 20),
        cost_estimate=pl.CostEstimate(flops=37*10**9, bytes_accessed=1 << 24, transcendentals=0),
        name="attend_backward",
    )(mine, grad_mixed, triple, attention, windows, take)


def input_kernel(images_ref, grad_triple_ref, grad_middle_ref, weights_ref, gains_ref, put_ref, out_ref, sums_ref, features_ref, grads_ref):
    step = pl.program_id(0)
    width = images_ref.shape[-1]
    slots = images_ref.shape[0] // PATCHES

    @pl.when(step == 0)
    def _():
        sums_ref[...] = jnp.zeros_like(sums_ref)
        cut_lanes(features_ref, images_ref[...].astype(f32))

    for sub in range(grad_triple_ref.shape[0]):
        image = step * grad_triple_ref.shape[0] + sub
        hat, factor = normalize(load_image(features_ref, image, slots))
        grad = 0.0
        for part in range(3):
            grad = grad + dot(grad_triple_ref[sub, :, part * width : (part + 1) * width], weights_ref[part], 1, 1)
        high = grad.astype(bf16)
        low = (grad - high.astype(f32)).astype(bf16)
        grad = dot(put_ref[...], high) + dot(put_ref[...], low)
        total = load_image(grad_middle_ref, image, slots) + normalize_back(grad, gains_ref[0:1], hat, factor)
        store_image(grads_ref, image, slots, total)
        sums_ref[0:1] += jnp.sum(grad * hat, axis=0, keepdims=True)
        sums_ref[1:2] += jnp.sum(grad, axis=0, keepdims=True)

    @pl.when(step == pl.num_programs(0) - 1)
    def _():
        out_ref[...] = join_lanes(grads_ref)


def input_backward(images, grad_triple, grad_middle, weights, gains, put):
    rows, width = images.shape
    slots = rows // PATCHES
    return pl.pallas_call(
        input_kernel,
        grid=(slots // 2,),
        in_specs=[
            whole((rows, width)), one((PAD_IMG, 3 * width), 2), whole(grad_middle.shape),
            pl.BlockSpec((3, width, width), lambda i: (0, 0, 0)), whole(gains.shape), whole(put.shape),
        ],
        out_specs=[whole((rows, width)), whole((8, width))],
        out_shape=[
            jax.ShapeDtypeStruct((rows, width), f32),
            jax.ShapeDtypeStruct((8, width), f32),
        ],
        scratch_shapes=[pltpu.VMEM((width // 128, rows, 128), f32)] * 2,
        compiler_params=pltpu.CompilerParams(vmem_limit_bytes=60 << 20),
        cost_estimate=pl.CostEstimate(flops=14*10**9, bytes_accessed=1 << 24, transcendentals=0),
        name="input_backward",
    )(images, grad_triple, grad_middle, weights, gains, put)


def combine_bias(bias_table, rel_index, shift_mask):
    one_hot = (rel_index.reshape(-1)[:, None] == jnp.arange(TABLE)[None, :]).astype(f32)
    position = jnp.dot(one_hot, bias_table, precision=lax.Precision.HIGHEST).T
    position = position.reshape(GROUPS, 4, WIN_TOK, WIN_TOK)
    position = jnp.transpose(position, (0, 3, 1, 2))
    position = jnp.pad(
        position, ((0, 0), (0, KEY_ROWS - WIN_TOK), (0, 0), (0, PAD_TOK - WIN_TOK))
    ).reshape(GROUPS, KEY_ROWS, 256)
    mask = jnp.transpose(-100.0 * (1 - shift_mask).astype(f32), (0, 2, 1))
    mask = jnp.pad(mask, ((0, 0), (0, 0), (0, PAD_TOK - WIN_TOK)))
    mask = jnp.pad(mask, ((0, 0), (0, KEY_ROWS - WIN_TOK), (0, 0)), constant_values=NEVER)
    mask = jnp.tile(mask, (1, 1, 4))
    return position[None] + mask[:, None], one_hot


def table_gradient(table, one_hot):
    grad = table.reshape(GROUPS, KEY_ROWS, 4, PAD_TOK)[:, :WIN_TOK, :, :WIN_TOK]
    grad = jnp.transpose(grad, (3, 1, 0, 2)).reshape(WIN_TOK * WIN_TOK, HEADS)
    return jnp.dot(one_hot.T, grad, precision=lax.Precision.HIGHEST)


def flat_rows(images):
    return jnp.transpose(images, (1, 0, 2)).reshape(-1, images.shape[-1])


def image_form(rows, slots):
    return jnp.transpose(rows.reshape(-1, slots, rows.shape[-1]), (1, 0, 2))


def adamw_step(param, grad, first, second, steps):
    first_next = 0.9 * first + 0.1 * grad
    second_next = 0.999 * second + 0.001 * grad * grad
    first_hat = first_next / (1.0 - jnp.power(0.9, steps))
    second_hat = second_next / (1.0 - jnp.power(0.999, steps))
    update = -0.05 * (first_hat / (jnp.sqrt(second_hat) + 1e-08) + 0.05 * param)
    return (first_next, second_next, update)


def column_blocks(matrix):
    rows, columns = matrix.shape
    return jnp.transpose(matrix.reshape(rows, columns // LANE, LANE), (1, 0, 2))


def from_blocks(blocks):
    count, rows, lanes = blocks.shape
    return jnp.transpose(blocks, (1, 0, 2)).reshape(rows, count * lanes)


def local(
    images,
    cotangent,
    image_counts,
    shift_mask,
    rel_index,
    step_count,
    attend_weight,
    merge_weight,
    expand_weight,
    project_weight,
    norm_gains,
    norm_shifts,
    layer_biases,
    bias_table,
    attend_momentum,
    merge_momentum,
    expand_momentum,
    project_momentum,
    gains_mean,
    gains_square,
    shifts_mean,
    shifts_square,
    biases_mean,
    biases_square,
    table_mean,
    table_square,
):
    slots, patches, width = images.shape
    devices = lax.axis_size("dp")
    hidden_units = expand_weight.shape[1]
    grad_scale = 1.0 / math.sqrt(slots * devices * PATCHES)
    rank = lax.axis_index("dp")
    planes = devices // CELL
    plane = rank // CELL
    corner = (rank // 2) % 4
    shard = width // devices
    tall_shard = hidden_units // devices

    attend_rows = column_blocks(attend_weight).reshape(-1, LANE)
    other_rows = jnp.concatenate(
        [column_blocks(merge_weight).reshape(-1, LANE), column_blocks(expand_weight).reshape(-1, LANE), project_weight]
    )
    near = gather_planes(attend_rows, devices)
    near[0], other_rows = lax.optimization_barrier((near[0], other_rows))
    other_near = gather_planes(other_rows, devices)
    near = gather_corners(jnp.stack(near), devices)
    near[0], other_near[1] = lax.optimization_barrier((near[0], other_near[1]))
    far = [exchange(piece, devices, 1) for piece in near]
    far[0], *other_near = lax.optimization_barrier((far[0], *other_near))
    other_near = gather_corners(jnp.stack(other_near), devices)
    other_far = [exchange(other_near[0], devices, 1)]
    attend_sources = near + far
    if not aligned(shard):
        attend_sources = order_rows(attend_sources, ((3, shard),), rank, devices)
    this = rank.reshape(1)

    take = jnp.asarray(window_matrix(), bf16)
    put = jnp.asarray(window_matrix().T, bf16)
    combined, one_hot = combine_bias(bias_table, rel_index, shift_mask)
    bias_row = layer_biases.reshape(1, -1)
    rows = flat_rows(images)
    windows, triple, attention, mixed, weights = attend_forward(
        this, attend_sources, shard, rows, norm_gains, norm_shifts, bias_row, combined, take, put
    )
    mixed, *arrived = lax.optimization_barrier((mixed, *other_near[1:]))
    other_far += [exchange(piece, devices, 1) for piece in arrived]
    sources = other_near[:1] + arrived + other_far
    if not aligned(shard):
        sources = order_rows(
            sources, ((1, shard), (hidden_units // LANE, shard), (1, tall_shard)), rank, devices
        )
    mine = (rank & 1).reshape(1)
    block_rows, grad_middle, grad_mixed, feed_sums, hidden_sums, *body_grads = feed_forward(
        image_counts, this, sources, hidden_units, rows, flat_rows(cotangent), mixed, norm_gains, norm_shifts, bias_row,
        slots, slots * patches // 4, devices,
    )
    block_out = image_form(block_rows, slots)
    if not aligned(shard):
        merge_term, expand_term, project_term = body_grads
        body_grads = pack_core([merge_term[None], expand_term, project_term[None]], BODY, shard, rank & 1)
    body_keep, body_sent = body_grads
    body_got = exchange(body_sent, devices, 1)
    body_own, body_sends = fold(by_corner(body_keep), [by_corner(body_got)], corner, BODY, shard)
    grad_mixed, *body_sends = lax.optimization_barrier((grad_mixed, *body_sends))
    body_got = send_all(body_sends, 2, devices)

    grad_triple, table_sums, triple_sums, *head_grads = attend_backward(
        mine, devices, grad_mixed, triple, attention, windows, take
    )
    if not aligned(shard):
        head_grads = pack_core(head_grads, HEAD, shard, rank & 1)
    head_keep, head_sent = head_grads
    head_got = exchange(head_sent, devices, 1)
    head_own, head_sends = fold(by_corner(head_keep), [by_corner(head_got)], corner, HEAD, shard)
    body_own, body_sends = fold(body_own[None], [got[None] for got in body_got], plane, BODY, shard)
    grad_triple, *sends = lax.optimization_barrier((grad_triple, *head_sends, *body_sends))
    head_got = send_all(sends[:3], 2, devices)
    body_got = send_all(sends[3:], CELL, devices)
    grad_triple, head_got[1] = lax.optimization_barrier((grad_triple, head_got[1]))
    input_rows, input_sums = input_backward(rows, grad_triple, grad_middle, weights, norm_gains, put)
    input_sums, head_got[0], head_got[2], *body_got = lax.optimization_barrier(
        (input_sums, head_got[0], head_got[2], *body_got)
    )
    input_grad = image_form(input_rows, slots)
    table_term = table_gradient(table_sums, one_hot)
    head_own, head_sends = fold(head_own[None], [got[None] for got in head_got], plane, HEAD, shard)
    head_got = send_all(head_sends, CELL, devices)
    momenta = (attend_momentum, merge_momentum, expand_momentum, project_momentum)
    grads, following, packed = finish(head_own, head_got, body_own, body_got, momenta, shard, grad_scale)

    small_parts = (
        jnp.stack([input_sums[0], feed_sums[0]]),
        jnp.stack([input_sums[1], feed_sums[1]]),
        jnp.concatenate([triple_sums[0], feed_sums[3], hidden_sums[0], feed_sums[2]]),
        table_term,
    )
    small = jnp.concatenate([part.reshape(-1) for part in small_parts])
    small = jnp.pad(small, (0, -small.shape[0] % (8 * LANE))).reshape(-1, LANE)

    length = tall_shard
    whole_rows, small = collect(packed, small, rank, devices)
    stack = whole_rows.reshape(CELL * planes, MATRICES, -1, LANE)
    stack = jnp.transpose(stack, (1, 0, 2, 3)).reshape(MATRICES, -1, LANE)
    kind = jnp.minimum(plane, MATRICES - 1).astype(jnp.int32).reshape(1)
    chunk = planes * length // MATRICES
    orth = newton_rows(stack, kind, chunk).reshape(MATRICES, planes, -1, LANE)
    pieces = [orth[:, 0]]
    for step in range(1, planes):
        pieces.append(exchange(orth[:, step], devices, CELL * step))
    received = jnp.stack(pieces)

    flat, start, small_sums = small.reshape(-1), 0, []
    for part in small_parts:
        small_sums.append(flat[start : start + part.size].reshape(part.shape))
        start += part.size
    small_grads = tuple((term * grad_scale for term in small_sums))
    results = [block_out, input_grad]
    for order, (grad, moment_next) in enumerate(zip(grads, following)):
        piece = pick(received, plane ^ order, 0)
        blocks = grad.shape[1] // LANE
        piece = piece.reshape(-1, LANE)[: blocks * grad.shape[0]].reshape(blocks, -1, LANE)
        extent = max(devices * grad.shape[0], grad.shape[1])
        update = -0.02 * math.sqrt(extent) * from_blocks(piece).astype(f32)
        results += [grad, moment_next, update]
    steps = step_count[0].astype(f32)
    params = (norm_gains, norm_shifts, layer_biases, bias_table)
    states = (
        (gains_mean, gains_square),
        (shifts_mean, shifts_square),
        (biases_mean, biases_square),
        (table_mean, table_square),
    )
    for param, grad, state in zip(params, small_grads, states):
        first_next, second_next, update = adamw_step(param, grad, state[0], state[1], steps)
        results += [grad, first_next, second_next, update]
    return tuple(results)


def solution(mesh):
    return jax.shard_map(
        local,
        mesh=mesh,
        in_specs=(
            P("dp", None, None),
            P("dp", None, None),
            P("dp"),
            P(),
            P(),
            P(),
            P("dp", None),
            P("dp", None),
            P("dp", None),
            P("dp", None),
            P(),
            P(),
            P(),
            P(),
            P("dp", None),
            P("dp", None),
            P("dp", None),
            P("dp", None),
            P(),
            P(),
            P(),
            P(),
            P(),
            P(),
            P(),
            P(),
        ),
        out_specs=(
            P("dp", None, None),
            P("dp", None, None),
            P("dp", None),
            P("dp", None),
            P("dp", None),
            P("dp", None),
            P("dp", None),
            P("dp", None),
            P("dp", None),
            P("dp", None),
            P("dp", None),
            P("dp", None),
            P("dp", None),
            P("dp", None),
            P(),
            P(),
            P(),
            P(),
            P(),
            P(),
            P(),
            P(),
            P(),
            P(),
            P(),
            P(),
            P(),
            P(),
            P(),
            P(),
        ),
        check_vma=False,
    )
```

```python
from functools import partial
import math

import jax
import jax.numpy as jnp
import numpy as np
from jax import lax
from jax.experimental import pallas as pl
from jax.experimental.pallas import tpu as pltpu
from jax.sharding import PartitionSpec as P

HEADS = 16
WIN = 7
SIDE = 14
SHIFT = 3
WIN_TOK = 49
PATCHES = 196
TABLE = 169


newton_first = 3.4445
newton_second = -4.775
newton_third = 2.0315


LANE = 512
CELL = 8
MATRICES = 4


def exchange(payload, devices, mask):
    return lax.ppermute(payload, "dp", [(i, i ^ mask) for i in range(devices)])


def pick(values, index, axis):
    return lax.dynamic_index_in_dim(values, index, axis, keepdims=False)


def split_wide(values):
    high = lax.reduce_precision(values, 8, 7)
    return high.astype(jnp.bfloat16), lax.reduce_precision(values - high, 8, 7).astype(jnp.bfloat16)


def join_wide(high, low):
    return high.astype(jnp.float32) + low.astype(jnp.float32)


def place_rows(rank, sources, outs, spans):
    for number, source in enumerate(sources):
        for plane in range(source.shape[0]):
            owner = jnp.bitwise_xor(rank, number // 4 + 2 * (number % 4) + CELL * plane)
            start = 0
            for out_ref, (blocks, rows) in zip(outs, spans):
                place = pl.ds(pl.multiple_of(owner * rows, rows), rows)
                for block in range(blocks):
                    out_ref[block, place, :] = source[plane, start : start + rows, :]
                    start += rows


def order_rows(sources, spans, rank, devices):
    lanes = sources[0].shape[-1]
    offset = jnp.arange(devices) ^ rank
    both = jnp.stack(sources).reshape(devices, -1, lanes)
    both = jnp.take(both, ((offset & 1) * 4 + ((offset >> 1) & 3)) * (devices // CELL) + (offset >> 3), axis=0)
    out, start = [], 0
    for blocks, rows in spans:
        part = both[:, start : start + blocks * rows].reshape(devices, blocks, rows, lanes)
        out.append(jnp.transpose(part, (1, 0, 2, 3)).reshape(blocks, devices * rows, lanes))
        start += blocks * rows
    return out


def gather_planes(rows, devices):
    return [rows] + [exchange(rows, devices, CELL * step) for step in range(1, devices // CELL)]


def gather_corners(rows, devices):
    return [rows] + [exchange(rows, devices, 2 * step) for step in range(1, 4)]


BODY = ((1, True), (4, False), (4, False))
HEAD = ((3, False),)


def encode(values, spans, rows):
    sent, start = [], 0
    for blocks, wide in spans:
        part = values[..., start : start + blocks * rows, :]
        start += blocks * rows
        high = part.astype(jnp.bfloat16)
        sent.append(high)
        if wide:
            sent.append((part - high.astype(jnp.float32)).astype(jnp.bfloat16))
    return sent[0] if len(sent) == 1 else jnp.concatenate(sent, axis=-2)


def decode(payload, spans, rows):
    out, start = [], 0
    for blocks, wide in spans:
        part = payload[..., start : start + blocks * rows, :].astype(jnp.float32)
        start += blocks * rows
        if wide:
            part = part + payload[..., start : start + blocks * rows, :].astype(jnp.float32)
            start += blocks * rows
        out.append(part)
    return out[0] if len(out) == 1 else jnp.concatenate(out, axis=-2)


def aligned(rows):
    return rows % 16 == 0


def pack_core(parts, spans, rows, mine):
    packed = []
    for (blocks, _), part in zip(spans, parts):
        count = part.shape[0]
        per = blocks * rows // count
        part = part.reshape(count, -1, 2, per, LANE)
        packed.append(jnp.transpose(part, (1, 2, 0, 3, 4)).reshape(part.shape[1], 2, blocks * rows, LANE))
    packed = jnp.concatenate(packed, axis=2)
    return pick(packed, mine, 1), encode(pick(packed, 1 - mine, 1), spans, rows)


def store_core(sources, keep_ref, sent_ref, spans, rows, mine):
    for pair in range(keep_ref.shape[0]):
        start, sent = 0, 0
        for (blocks, wide), (source, count) in zip(spans, sources):
            per = blocks * rows // count
            near = pl.ds(pl.multiple_of(pair * 2 * per + mine * per, per), per)
            away = pl.ds(pl.multiple_of(pair * 2 * per + (1 - mine) * per, per), per)
            for block in range(count):
                lead = (block,) if len(source.shape) == 3 else ()
                keep_ref[pair, start : start + per, :] = source[lead + (near, slice(None))]
                values = source[lead + (away, slice(None))]
                high = values.astype(jnp.bfloat16)
                sent_ref[pair, sent : sent + per, :] = high
                if wide:
                    low = (values - high.astype(jnp.float32)).astype(jnp.bfloat16)
                    sent_ref[pair, sent + blocks * rows : sent + blocks * rows + per, :] = low
                start += per
                sent += per
            if wide:
                sent += blocks * rows


def fold_kernel(own_ref, keep_ref, *refs, gots, spans, rows):
    own = own_ref[0]
    total_ref, *sent_refs = refs[gots:]
    for step in range(keep_ref.shape[1]):
        index = jnp.bitwise_xor(own, step)
        total = keep_ref[0, index]
        for got in refs[:gots]:
            total = total + decode(got[0, index], spans, rows)
        if step:
            sent_refs[step - 1][0] = encode(total, spans, rows)
        else:
            total_ref[0] = total


def fold(keep, got, own, spans, rows):
    groups, members, length, lanes = keep.shape
    if not aligned(rows):
        total = keep
        for payload in got:
            total = total + decode(payload, spans, rows)
        return pick(total, own, 1), [encode(pick(total, own ^ step, 1), spans, rows) for step in range(1, members)]
    sent = got[0].shape[2]

    def block(*shape):
        return pl.BlockSpec((1,) + shape, lambda i: (i,) + (0,) * len(shape))

    total, *sends = pl.pallas_call(
        partial(fold_kernel, gots=len(got), spans=spans, rows=rows),
        grid=(groups,),
        in_specs=[pl.BlockSpec(memory_space=pltpu.SMEM), block(members, length, lanes)]
        + [block(members, sent, lanes)] * len(got),
        out_specs=[block(length, lanes)] + [block(sent, lanes)] * (members - 1),
        out_shape=[jax.ShapeDtypeStruct((groups, length, lanes), jnp.float32)]
        + [jax.ShapeDtypeStruct((groups, sent, lanes), jnp.bfloat16)] * (members - 1),
        compiler_params=pltpu.CompilerParams(vmem_limit_bytes=8 << 20),
        cost_estimate=pl.CostEstimate(flops=2 * 10**9, bytes_accessed=8 * keep.size, transcendentals=0),
        name="fold",
    )(own.reshape(1), keep, *got)
    return total, sends


def send_all(payloads, mask, devices):
    return [exchange(payload, devices, mask * (step + 1)) for step, payload in enumerate(payloads)]


def finish_math(head, head_got, body, body_got, momenta, rows, grad_scale):
    for payload in head_got:
        head = head + decode(payload, HEAD, rows)
    for payload in body_got:
        body = body + decode(payload, BODY, rows)
    spans = (head, body[:rows], body[rows : 5 * rows], body[5 * rows :])
    grads, following, packed = [], [], []
    for order, (span, moment) in enumerate(zip(spans, momenta)):
        blocks = moment.shape[1] // LANE
        per = moment.shape[0]
        grad = jnp.concatenate([span[block * per : (block + 1) * per] for block in range(blocks)], axis=1) * grad_scale
        after = 0.95 * moment + grad
        grads.append(grad)
        following.append(after)
        pieces = [after[:, block * LANE : (block + 1) * LANE] for block in range(blocks)]
        if order == 1:
            high = after.astype(jnp.bfloat16)
            pieces = [high, after - high.astype(jnp.float32)]
        pieces = [piece.astype(jnp.bfloat16) for piece in pieces]
        if per * len(pieces) < 4 * rows:
            pieces.append(jnp.zeros((4 * rows - per * len(pieces), LANE), jnp.bfloat16))
        packed.append(jnp.concatenate(pieces, axis=0))
    return grads, following, packed


def finish_kernel(*refs, count, rows, grad_scale):
    head, body = refs[0][0], refs[1][0]
    head_got = [ref[0] for ref in refs[2 : 2 + count]]
    body_got = [ref[0] for ref in refs[2 + count : 2 + 2 * count]]
    momenta = [ref[...] for ref in refs[2 + 2 * count : 6 + 2 * count]]
    outs = refs[6 + 2 * count :]
    grads, following, packed = finish_math(head, head_got, body, body_got, momenta, rows, grad_scale)
    for index in range(4):
        outs[index][...] = grads[index]
        outs[4 + index][...] = following[index]
        outs[8][index] = packed[index]


def finish(head, head_got, body, body_got, momenta, rows, grad_scale):
    if not aligned(rows):
        grads, following, packed = finish_math(
            head[0], [got[0] for got in head_got], body[0], [got[0] for got in body_got], momenta, rows, grad_scale
        )
        return grads, following, jnp.stack(packed)
    shapes = [jax.ShapeDtypeStruct(moment.shape, jnp.float32) for moment in momenta]
    outs = pl.pallas_call(
        partial(finish_kernel, count=len(head_got), rows=rows, grad_scale=grad_scale),
        out_shape=shapes + shapes + [jax.ShapeDtypeStruct((4, 4 * rows, LANE), jnp.bfloat16)],
        compiler_params=pltpu.CompilerParams(vmem_limit_bytes=8 << 20),
        cost_estimate=pl.CostEstimate(flops=10**9, bytes_accessed=1 << 22, transcendentals=0),
        name="finish",
    )(head, body, *head_got, *body_got, *momenta)
    return outs[:4], outs[4:8], outs[8]


def by_corner(packed):
    return packed.reshape((-1, 4) + packed.shape[1:])


def newton_kernel(kind_ref, stack_ref, out_ref, gram_ref, rows_ref):
    kind = kind_ref[0]
    blocks, side, _ = stack_ref.shape
    chunk = out_ref.shape[1]
    tall = kind == 3
    paired = kind == 1

    @pl.when(tall)
    def _():
        total = dot(stack_ref[0], stack_ref[0], 0, 0)
        for block in range(1, blocks):
            total = total + dot(stack_ref[block], stack_ref[block], 0, 0)
        gram_ref[...] = total

    @pl.when(paired)
    def _():
        cross = dot(stack_ref[0], stack_ref[1], 1, 1)
        cross = cross + dot(stack_ref[1], stack_ref[0], 1, 1)
        gram_ref[...] = dot(stack_ref[0], stack_ref[0], 1, 1) + cross

    @pl.when(jnp.logical_not(jnp.logical_or(tall, paired)))
    def _():
        total = dot(stack_ref[0], stack_ref[0], 1, 1)
        for block in range(1, blocks):
            total = total + dot(stack_ref[block], stack_ref[block], 1, 1)
        gram_ref[...] = total

    row = lax.broadcasted_iota(jnp.int32, (side, side), 0)
    column = lax.broadcasted_iota(jnp.int32, (side, side), 1)
    eye = (row == column).astype(jnp.float32)
    gram = gram_ref[...]
    inverse = 1.0 / (jnp.sqrt(jnp.sum(gram * eye)) + 1e-07)
    gram_ref[...] = gram * (inverse * inverse)

    @pl.when(tall)
    def _():
        for block in range(blocks):
            rows_ref[block * chunk : (block + 1) * chunk] = stack_ref[block, :chunk].astype(jnp.float32) * inverse

    @pl.when(jnp.logical_not(tall))
    def _():
        rows_ref[...] = eye[: blocks * chunk] * inverse

    def halves(values):
        high = values.astype(jnp.bfloat16)
        return high, (values - high.astype(jnp.float32)).astype(jnp.bfloat16)

    def product(left, right):
        return dot(
            jnp.concatenate([left[0], left[1], left[0]], axis=1), jnp.concatenate([right[0], right[0], right[1]], axis=0)
        )

    def mix(gram, parts):
        return halves(newton_first * eye + newton_second * gram + newton_third * product(parts, parts))

    def sweep(step, carry):
        gram = gram_ref[...]
        parts = halves(gram)
        mixer = mix(gram, parts)
        rows_ref[...] = product(halves(rows_ref[...]), mixer)
        gram_ref[...] = product(halves(product(parts, mixer)), mixer)
        return carry

    lax.fori_loop(0, 4, sweep, 0)
    gram = gram_ref[...]
    rows = product(halves(rows_ref[...]), mix(gram, halves(gram)))

    @pl.when(tall)
    def _():
        for block in range(blocks):
            out_ref[block] = rows[block * chunk : (block + 1) * chunk].astype(out_ref.dtype)

    @pl.when(jnp.logical_not(tall))
    def _():
        own = halves(rows[:chunk])
        first = dot(own[0], stack_ref[0]) + dot(own[1], stack_ref[0])
        second = dot(own[0], stack_ref[1])
        out_ref[0] = jnp.where(paired, first + second, first).astype(out_ref.dtype)
        out_ref[1] = (second + dot(own[1], stack_ref[1])).astype(out_ref.dtype)
        for block in range(2, blocks):
            out_ref[block] = (dot(own[0], stack_ref[block]) + dot(own[1], stack_ref[block])).astype(out_ref.dtype)


def newton_rows(stack, kind, chunk):
    blocks, side, lanes = stack.shape
    return pl.pallas_call(
        newton_kernel,
        out_shape=jax.ShapeDtypeStruct((blocks, chunk, lanes), jnp.bfloat16),
        in_specs=[
            pl.BlockSpec(memory_space=pltpu.SMEM),
            pl.BlockSpec(memory_space=pltpu.VMEM),
        ],
        out_specs=pl.BlockSpec(memory_space=pltpu.VMEM),
        scratch_shapes=[pltpu.VMEM((side, side), jnp.float32), pltpu.VMEM((blocks * chunk, side), jnp.float32)],
        compiler_params=pltpu.CompilerParams(vmem_limit_bytes=48 << 20),
        cost_estimate=pl.CostEstimate(flops=20 * 10**9, bytes_accessed=1 << 22, transcendentals=0),
        name="newton_rows",
    )(kind, stack)


def add_tree(values):
    while len(values) > 1:
        values = [left + right for left, right in zip(values[::2], values[1::2])]
    return values[0]


def collect(packed, small, rank, devices):
    planes = devices // CELL
    plane = rank // CELL
    rows = packed.shape[1]
    count = small.shape[0]

    def pair(values):
        high, low = split_wide(values)
        return jnp.concatenate([high, low])

    def value(sent):
        return join_wide(sent[:count], sent[count:])

    sent = pair(small)
    pieces, sums = [pick(packed, jnp.minimum(plane, MATRICES - 1), 0)], [value(sent)]
    for step in range(1, planes):
        give = pick(packed, jnp.minimum(plane ^ step, MATRICES - 1), 0)
        got = exchange(jnp.concatenate([give, sent]), devices, CELL * step)
        pieces.append(got[:rows])
        sums.append(value(got[rows:]))
    half = rows // 2
    left = jnp.concatenate([piece[:half] for piece in pieces])
    right = jnp.concatenate([piece[half:] for piece in pieces])
    length = left.shape[0]
    total = add_tree(sums)
    sent = pair(total)
    got = exchange(jnp.concatenate([left, sent]), devices, 4)
    got, right_x = lax.optimization_barrier((got, exchange(right, devices, 2)))
    total = value(sent) + value(got[length:])
    left = jnp.concatenate([left, got[:length]])
    sent = pair(total)
    got = exchange(jnp.concatenate([left, sent]), devices, 2)
    got, right_y = lax.optimization_barrier((got, exchange(jnp.concatenate([right, right_x]), devices, 4)))
    total = value(sent) + value(got[2 * length :])
    left = jnp.concatenate([left, got[: 2 * length]])
    right = jnp.concatenate([right, right_y[:length], right_x, right_y[length:]])
    sent = pair(total)
    current = jnp.concatenate([left, right])
    got = exchange(jnp.concatenate([current, sent]), devices, 1)
    total = value(sent) + value(got[2 * 4 * length :])
    halves = jnp.concatenate(
        [values.reshape(2, 4 * planes, half, LANE) for values in (current, got[: 8 * length])], axis=1
    )
    current = jnp.swapaxes(halves, 0, 1).reshape(CELL, planes, rows, LANE)
    return current, total


PAD_TOK = 64
KEY_ROWS = 56
PAD_IMG = 256
GROUPS = 4
NEVER = -1e30
f32 = jnp.float32
bf16 = jnp.bfloat16


def window_matrix():
    table = np.zeros((PAD_IMG, PATCHES), np.float32)
    blocks = SIDE // WIN
    for window in range(blocks * blocks):
        for token in range(WIN_TOK):
            row = (window // blocks) * WIN + token // WIN
            column = (window % blocks) * WIN + token % WIN
            patch = ((row + SHIFT) % SIDE) * SIDE + (column + SHIFT) % SIDE
            table[window * PAD_TOK + token, patch] = 1.0
    return table


def dot(left, right, left_dim=1, right_dim=0):
    return lax.dot_general(
        left, right, (((left_dim,), (right_dim,)), ((), ())), preferred_element_type=jnp.float32
    )


def normalize(values):
    center = values - jnp.mean(values, axis=-1, keepdims=True)
    spread = jnp.mean(center * center, axis=-1, keepdims=True)
    factor = lax.rsqrt(spread + 1e-05)
    return center * factor, factor


def normalize_back(grad, gain, hat, factor):
    inner = grad * gain
    return factor * (
        inner
        - jnp.mean(inner, axis=-1, keepdims=True)
        - hat * jnp.mean(inner * hat, axis=-1, keepdims=True)
    )


def head_masks(dtype):
    lane = lax.broadcasted_iota(jnp.int32, (1, 128), 1) // 32
    return [(lane == head).astype(dtype) for head in range(GROUPS)]


def spread_heads(rows, masks):
    return jnp.concatenate([rows * mask for mask in masks], axis=0)


def fold_heads(blocks, masks):
    total = None
    for head, mask in enumerate(masks):
        part = blocks[head * PAD_TOK : (head + 1) * PAD_TOK] * mask
        total = part if total is None else total + part
    return total


def load_image(ref, image, slots):
    return jnp.concatenate([ref[lane, pl.ds(image, PATCHES, stride=slots), :] for lane in range(ref.shape[0])], axis=1)


def store_image(ref, image, slots, values):
    for lane in range(ref.shape[0]):
        ref[lane, pl.ds(image, PATCHES, stride=slots), :] = values[:, lane * 128 : (lane + 1) * 128]


def cut_lanes(ref, values):
    for lane in range(ref.shape[0]):
        ref[lane] = values[:, lane * 128 : (lane + 1) * 128]


def join_lanes(ref):
    return jnp.concatenate([ref[lane] for lane in range(ref.shape[0])], axis=1)


def attend_kernel(
    rank_ref, images_ref, gains_ref, shifts_ref, biases_ref, combined_ref, take_ref, put_ref, *refs, pieces, shard,
):
    windows_ref, triple_ref, attention_ref, mixed_ref, weights_ref, features_ref, scratch_ref = refs[pieces:]
    step = pl.program_id(0)
    width = images_ref.shape[-1]
    slots = images_ref.shape[0] // PATCHES
    scale = 1.0 / math.sqrt(width // HEADS)

    @pl.when(step == 0)
    def _():
        cut_lanes(features_ref, images_ref[...].astype(f32))
        if pieces > 1:
            place_rows(rank_ref[0], refs[:pieces], (weights_ref,), ((3, shard),))
        else:
            weights_ref[...] = refs[0][...]

    masks = head_masks(bf16)
    masks_wide = head_masks(f32)
    count = windows_ref.shape[0]
    for sub in range(count):
        image = step * count + sub
        features = load_image(features_ref, image, slots)
        hat, _ = normalize(features)
        normed = (hat * gains_ref[0:1] + shifts_ref[0:1]).astype(bf16)
        windows = dot(take_ref[...], normed).astype(bf16)
        windows_ref[sub] = windows
        for part in range(3):
            columns = slice(part * width, (part + 1) * width)
            values = dot(windows, weights_ref[part]) + biases_ref[0:1, columns]
            if part == 0:
                values = values * scale
            triple_ref[sub, :, columns] = values.astype(bf16)
        for window in range(4):
            rows = slice(window * PAD_TOK, (window + 1) * PAD_TOK)
            for group in range(GROUPS):
                lanes = slice(group * 128, (group + 1) * 128)
                query = triple_ref[sub, rows, group * 128 : (group + 1) * 128]
                key = triple_ref[sub, rows, width + group * 128 : width + (group + 1) * 128]
                value = triple_ref[sub, rows, 2 * width + group * 128 : 2 * width + (group + 1) * 128]
                scores = dot(key, spread_heads(query, masks), 1, 1)[:KEY_ROWS] + combined_ref[window, group]
                top = jnp.max(scores, axis=0, keepdims=True)
                raised = jnp.exp(scores - top)
                attention = raised * (1.0 / jnp.sum(raised, axis=0, keepdims=True))
                low = jnp.concatenate([attention, jnp.zeros((PAD_TOK - KEY_ROWS, attention.shape[1]), f32)], axis=0).astype(bf16)
                attention_ref[sub, window, group] = low
                out = dot(low, value, 0, 0)
                scratch_ref[sub, rows, lanes] = fold_heads(out, masks_wide).astype(bf16)
        store_image(mixed_ref, image, slots, dot(put_ref[...], scratch_ref[sub]))


def whole(shape):
    return pl.BlockSpec(shape, lambda i: (0,) * len(shape))


def one(shape, count=1):
    return pl.BlockSpec((count,) + shape, lambda i: (i,) + (0,) * len(shape))


def attend_forward(rank, sources, shard, images, gains, shifts, biases, combined, take, put):
    rows, width = images.shape
    slots = rows // PATCHES
    return pl.pallas_call(
        partial(attend_kernel, pieces=len(sources), shard=shard),
        grid=(slots // 2,),
        in_specs=[
            pl.BlockSpec(memory_space=pltpu.SMEM), whole(images.shape), whole(gains.shape), whole(shifts.shape),
            whole(biases.shape), whole(combined.shape), whole(take.shape), whole(put.shape),
        ]
        + [whole(source.shape) for source in sources],
        out_specs=[
            one((PAD_IMG, width), 2), one((PAD_IMG, 3 * width), 2), one((4, GROUPS, PAD_TOK, 256), 2),
            whole((width // 128, rows, 128)), whole((3, width, width)),
        ],
        out_shape=[
            jax.ShapeDtypeStruct((slots, PAD_IMG, width), bf16),
            jax.ShapeDtypeStruct((slots, PAD_IMG, 3 * width), bf16),
            jax.ShapeDtypeStruct((slots, 4, GROUPS, PAD_TOK, 256), bf16),
            jax.ShapeDtypeStruct((width // 128, rows, 128), f32),
            jax.ShapeDtypeStruct((3, width, width), bf16),
        ],
        scratch_shapes=[pltpu.VMEM((width // 128, rows, 128), f32), pltpu.VMEM((2, PAD_IMG, width), bf16)],
        compiler_params=pltpu.CompilerParams(vmem_limit_bytes=60 << 20),
        cost_estimate=pl.CostEstimate(flops=20*10**9, bytes_accessed=1 << 24, transcendentals=0),
        name="attend_forward",
    )(rank, images, gains, shifts, biases, combined, take, put, *sources)


def gelu_parts(values):
    size = jnp.abs(values) * math.sqrt(0.5)
    bell = jnp.exp(-0.5 * values * values)
    turn = 1.0 / (1.0 + 0.3275911 * size)
    tail = 1.061405429
    for factor in (-1.453152027, 1.421413741, -0.284496736, 0.254829592):
        tail = tail * turn + factor
    tail = 0.5 * tail * turn * bell
    share = jnp.where(values < 0.0, tail, 1.0 - tail)
    return share, values * bell * (1.0 / math.sqrt(2.0 * math.pi))


def feed_kernel(
    count_ref, rank_ref, images_ref, cotangent_ref, mixed_ref, gains_ref, shifts_ref, biases_ref, *refs, slots, shard, sources,
):
    block_ref, grad_middle_ref, grad_mixed_ref, sums_ref, hidden_sums_ref, *grad_refs = refs[sources:]
    merge_ref, expand_ref, project_ref = grad_refs[2:5] if shard else refs[:3]
    merge_grad_ref, expand_grad_ref, project_grad_ref = grad_refs[-3:]
    step = pl.program_id(0)
    rows, width = cotangent_ref.shape
    pieces, _, piece = expand_ref.shape
    hidden = pieces * piece
    @pl.when(step == 0)
    def _():
        project_grad_ref[...] = jnp.zeros_like(project_grad_ref)
        expand_grad_ref[...] = jnp.zeros_like(expand_grad_ref)
        merge_grad_ref[...] = jnp.zeros_like(merge_grad_ref)
        sums_ref[...] = jnp.zeros_like(sums_ref)
        hidden_sums_ref[...] = jnp.zeros_like(hidden_sums_ref)
        if shard:
            spans = ((1, shard), (pieces, shard), (1, project_ref.shape[1] // (width // shard)))
            place_rows(rank_ref[0], refs[:sources], (merge_ref, expand_ref, project_ref), spans)

    mixed = join_lanes(mixed_ref).astype(bf16)
    branch = dot(mixed, merge_ref[0]) + biases_ref[0:1, 3 * width : 4 * width]
    middle = images_ref[...].astype(f32) + branch
    slot = lax.broadcasted_iota(jnp.int32, (rows, 1), 0) % slots
    live = slot < count_ref[0]

    hat, factor = normalize(middle)
    gain = gains_ref[1:2]
    normed = (hat * gain + shifts_ref[1:2]).astype(bf16)
    grad_out = jnp.where(live, cotangent_ref[...].astype(f32), 0.0)
    grad_low = grad_out.astype(bf16)
    out = biases_ref[0:1, 4 * width + hidden : 5 * width + hidden]
    back = 0.0
    for index in range(pieces):
        columns = slice(index * piece, (index + 1) * piece)
        offset = 4 * width + index * piece
        pre = dot(normed, expand_ref[index]) + biases_ref[0:1, offset : offset + piece]
        share, slope = gelu_parts(pre)
        active = (pre * share).astype(bf16)
        out = out + dot(active, project_ref[0, columns])
        project_grad_ref[columns] += dot(active, grad_low, 0, 0)
        grad_pre = (dot(grad_low, project_ref[0, columns], 1, 1) * (share + slope)).astype(bf16)
        expand_grad_ref[index] += dot(normed, grad_pre, 0, 0)
        hidden_sums_ref[0:1, columns] += jnp.sum(grad_pre.astype(f32), axis=0, keepdims=True)
        back = back + dot(grad_pre, expand_ref[index], 1, 1)
    block_ref[...] = jnp.where(live, middle + out, 0.0).astype(bf16)
    grad_middle = grad_out + normalize_back(back, gain, hat, factor)
    cut_lanes(grad_middle_ref, grad_middle)
    grad_branch = grad_middle.astype(bf16)
    merge_grad_ref[...] += dot(mixed, grad_branch, 0, 0)
    cut_lanes(grad_mixed_ref, dot(grad_branch, merge_ref[0], 1, 1))
    sums_ref[0:1] += jnp.sum(back * hat, axis=0, keepdims=True)
    sums_ref[1:2] += jnp.sum(back, axis=0, keepdims=True)
    sums_ref[2:3] += jnp.sum(grad_out, axis=0, keepdims=True)
    sums_ref[3:4] += jnp.sum(grad_branch.astype(f32), axis=0, keepdims=True)
    if shard:

        @pl.when(step == pl.num_programs(0) - 1)
        def _():
            sources = ((merge_grad_ref, 1), (expand_grad_ref, pieces), (project_grad_ref, 1))
            store_core(sources, grad_refs[0], grad_refs[1], BODY, shard, rank_ref[0] & 1)


def feed_forward(count, rank, sources, hidden, images, cotangent, mixed, gains, shifts, biases, slots, tile, devices):
    rows, width = cotangent.shape
    expand_shape = (hidden // LANE, width, LANE)
    lanes = pl.BlockSpec((width // 128, tile, 128), lambda i: (0, i, 0))
    shard = width // devices
    raw = [(width, width), expand_shape, (hidden, width)]
    grad_shapes = [jax.ShapeDtypeStruct(shape, f32) for shape in raw]
    scratch = []
    if aligned(shard):
        grad_shapes = [
            jax.ShapeDtypeStruct((devices // 2, 9 * shard, width), f32),
            jax.ShapeDtypeStruct((devices // 2, 10 * shard, width), bf16),
        ]
        scratch = [pltpu.VMEM(shape, bf16) for shape in ((1, width, width), expand_shape, (1, hidden, width))]
        scratch += [pltpu.VMEM(shape, f32) for shape in raw]

    def tiled(columns):
        return pl.BlockSpec((tile, columns), lambda i: (i, 0))

    return pl.pallas_call(
        partial(feed_kernel, slots=slots, shard=shard if aligned(shard) else 0, sources=len(sources)),
        grid=(rows // tile,),
        in_specs=[
            pl.BlockSpec(memory_space=pltpu.SMEM), pl.BlockSpec(memory_space=pltpu.SMEM), tiled(width), tiled(width), lanes,
            whole(gains.shape), whole(shifts.shape), whole(biases.shape),
        ]
        + [whole(source.shape) for source in sources],
        out_specs=[tiled(width), lanes, lanes, whole((8, width)), whole((8, hidden))]
        + [whole(shape.shape) for shape in grad_shapes],
        out_shape=[
            jax.ShapeDtypeStruct((rows, width), bf16),
            jax.ShapeDtypeStruct((width // 128, rows, 128), f32),
            jax.ShapeDtypeStruct((width // 128, rows, 128), f32),
            jax.ShapeDtypeStruct((8, width), f32),
            jax.ShapeDtypeStruct((8, hidden), f32),
        ]
        + grad_shapes,
        scratch_shapes=scratch,
        compiler_params=pltpu.CompilerParams(vmem_limit_bytes=60 << 20),
        cost_estimate=pl.CostEstimate(flops=44*10**9, bytes_accessed=1 << 24, transcendentals=0),
        name="feed_forward",
    )(count, rank, images, cotangent, mixed, gains, shifts, biases, *sources)


def attend_back_kernel(
    mine_ref, grad_mixed_ref, triple_ref, attention_ref, windows_ref, take_ref,
    grad_triple_ref, table_ref, sums_ref, *grad_refs, shard,
):
    attend_grad_ref = grad_refs[-1]
    step = pl.program_id(0)
    width = windows_ref.shape[-1]
    slots = grad_mixed_ref.shape[1] // PATCHES
    scale = 1.0 / math.sqrt(width // HEADS)

    @pl.when(step == 0)
    def _():
        attend_grad_ref[...] = jnp.zeros_like(attend_grad_ref)
        table_ref[...] = jnp.zeros_like(table_ref)
        sums_ref[...] = jnp.zeros_like(sums_ref)

    grad_mixed = dot(take_ref[...], load_image(grad_mixed_ref, step, slots).astype(bf16)).astype(bf16)
    masks = head_masks(bf16)
    masks_wide = head_masks(f32)
    pad = jnp.zeros((PAD_TOK - KEY_ROWS, 256), f32)
    for group in range(GROUPS):
        table = table_ref[group]
        for window in range(4):
            rows = slice(window * PAD_TOK, (window + 1) * PAD_TOK)
            query = triple_ref[0, rows, group * 128 : (group + 1) * 128]
            key = triple_ref[0, rows, width + group * 128 : width + (group + 1) * 128]
            value = triple_ref[0, rows, 2 * width + group * 128 : 2 * width + (group + 1) * 128]
            grad_heads = spread_heads(grad_mixed[rows, group * 128 : (group + 1) * 128], masks)
            attention_low = attention_ref[0, window, group]
            attention = attention_low.astype(f32)[:KEY_ROWS]
            grad_attention = dot(value, grad_heads, 1, 1)[:KEY_ROWS]
            inner = jnp.sum(grad_attention * attention, axis=0, keepdims=True)
            grad_scores = attention * (grad_attention - inner)
            low = jnp.concatenate([grad_scores, pad], axis=0).astype(bf16)
            table = table + low.astype(f32)[:KEY_ROWS]
            grad_value = dot(attention_low, grad_heads)
            grad_key = dot(low, spread_heads(query, masks))
            grad_query = fold_heads(dot(low, key, 0, 0), masks_wide) * scale
            grad_triple_ref[0, rows, group * 128 : (group + 1) * 128] = grad_query.astype(bf16)
            grad_triple_ref[0, rows, width + group * 128 : width + (group + 1) * 128] = grad_key.astype(bf16)
            grad_triple_ref[0, rows, 2 * width + group * 128 : 2 * width + (group + 1) * 128] = grad_value.astype(bf16)
        table_ref[group] = table
    for part in range(3):
        columns = slice(part * width, (part + 1) * width)
        grad = grad_triple_ref[0, :, columns]
        attend_grad_ref[part] += dot(windows_ref[0], grad, 0, 0)
        sums_ref[0:1, columns] += jnp.sum(grad.astype(f32), axis=0, keepdims=True)
    if shard:

        @pl.when(step == pl.num_programs(0) - 1)
        def _():
            store_core(((attend_grad_ref, 3),), grad_refs[0], grad_refs[1], HEAD, shard, mine_ref[0])


def attend_backward(mine, devices, grad_mixed, triple, attention, windows, take):
    width = windows.shape[-1]
    slots = triple.shape[0]
    shard = width // devices
    grad_shapes, scratch = [jax.ShapeDtypeStruct((3, width, width), f32)], []
    if aligned(shard):
        grad_shapes = [
            jax.ShapeDtypeStruct((devices // 2, 3 * shard, width), f32),
            jax.ShapeDtypeStruct((devices // 2, 3 * shard, width), bf16),
        ]
        scratch = [pltpu.VMEM((3, width, width), f32)]
    return pl.pallas_call(
        partial(attend_back_kernel, shard=shard if aligned(shard) else 0),
        grid=(slots,),
        in_specs=[
            pl.BlockSpec(memory_space=pltpu.SMEM), whole(grad_mixed.shape), one((PAD_IMG, 3 * width)),
            one((4, GROUPS, PAD_TOK, 256)), one((PAD_IMG, width)), whole(take.shape),
        ],
        out_specs=[one((PAD_IMG, 3 * width)), whole((GROUPS, KEY_ROWS, 256)), whole((8, 3 * width))]
        + [whole(shape.shape) for shape in grad_shapes],
        out_shape=[
            jax.ShapeDtypeStruct((slots, PAD_IMG, 3 * width), bf16),
            jax.ShapeDtypeStruct((GROUPS, KEY_ROWS, 256), f32),
            jax.ShapeDtypeStruct((8, 3 * width), f32),
        ]
        + grad_shapes,
        scratch_shapes=scratch,
        compiler_params=pltpu.CompilerParams(vmem_limit_bytes=60 << 20),
        cost_estimate=pl.CostEstimate(flops=37*10**9, bytes_accessed=1 << 24, transcendentals=0),
        name="attend_backward",
    )(mine, grad_mixed, triple, attention, windows, take)


def input_kernel(images_ref, grad_triple_ref, grad_middle_ref, weights_ref, gains_ref, put_ref, out_ref, sums_ref, features_ref, grads_ref):
    step = pl.program_id(0)
    width = images_ref.shape[-1]
    slots = images_ref.shape[0] // PATCHES

    @pl.when(step == 0)
    def _():
        sums_ref[...] = jnp.zeros_like(sums_ref)
        cut_lanes(features_ref, images_ref[...].astype(f32))

    for sub in range(grad_triple_ref.shape[0]):
        image = step * grad_triple_ref.shape[0] + sub
        hat, factor = normalize(load_image(features_ref, image, slots))
        grad = 0.0
        for part in range(3):
            grad = grad + dot(grad_triple_ref[sub, :, part * width : (part + 1) * width], weights_ref[part], 1, 1)
        high = grad.astype(bf16)
        low = (grad - high.astype(f32)).astype(bf16)
        grad = dot(put_ref[...], high) + dot(put_ref[...], low)
        total = load_image(grad_middle_ref, image, slots) + normalize_back(grad, gains_ref[0:1], hat, factor)
        store_image(grads_ref, image, slots, total)
        sums_ref[0:1] += jnp.sum(grad * hat, axis=0, keepdims=True)
        sums_ref[1:2] += jnp.sum(grad, axis=0, keepdims=True)

    @pl.when(step == pl.num_programs(0) - 1)
    def _():
        out_ref[...] = join_lanes(grads_ref)


def input_backward(images, grad_triple, grad_middle, weights, gains, put):
    rows, width = images.shape
    slots = rows // PATCHES
    return pl.pallas_call(
        input_kernel,
        grid=(slots // 2,),
        in_specs=[
            whole((rows, width)), one((PAD_IMG, 3 * width), 2), whole(grad_middle.shape),
            pl.BlockSpec((3, width, width), lambda i: (0, 0, 0)), whole(gains.shape), whole(put.shape),
        ],
        out_specs=[whole((rows, width)), whole((8, width))],
        out_shape=[
            jax.ShapeDtypeStruct((rows, width), f32),
            jax.ShapeDtypeStruct((8, width), f32),
        ],
        scratch_shapes=[pltpu.VMEM((width // 128, rows, 128), f32)] * 2,
        compiler_params=pltpu.CompilerParams(vmem_limit_bytes=60 << 20),
        cost_estimate=pl.CostEstimate(flops=14*10**9, bytes_accessed=1 << 24, transcendentals=0),
        name="input_backward",
    )(images, grad_triple, grad_middle, weights, gains, put)


def combine_bias(bias_table, rel_index, shift_mask):
    one_hot = (rel_index.reshape(-1)[:, None] == jnp.arange(TABLE)[None, :]).astype(f32)
    position = jnp.dot(one_hot, bias_table, precision=lax.Precision.HIGHEST).T
    position = position.reshape(GROUPS, 4, WIN_TOK, WIN_TOK)
    position = jnp.transpose(position, (0, 3, 1, 2))
    position = jnp.pad(
        position, ((0, 0), (0, KEY_ROWS - WIN_TOK), (0, 0), (0, PAD_TOK - WIN_TOK))
    ).reshape(GROUPS, KEY_ROWS, 256)
    mask = jnp.transpose(-100.0 * (1 - shift_mask).astype(f32), (0, 2, 1))
    mask = jnp.pad(mask, ((0, 0), (0, 0), (0, PAD_TOK - WIN_TOK)))
    mask = jnp.pad(mask, ((0, 0), (0, KEY_ROWS - WIN_TOK), (0, 0)), constant_values=NEVER)
    mask = jnp.tile(mask, (1, 1, 4))
    return position[None] + mask[:, None], one_hot


def table_gradient(table, one_hot):
    grad = table.reshape(GROUPS, KEY_ROWS, 4, PAD_TOK)[:, :WIN_TOK, :, :WIN_TOK]
    grad = jnp.transpose(grad, (3, 1, 0, 2)).reshape(WIN_TOK * WIN_TOK, HEADS)
    return jnp.dot(one_hot.T, grad, precision=lax.Precision.HIGHEST)


def flat_rows(images):
    return jnp.transpose(images, (1, 0, 2)).reshape(-1, images.shape[-1])


def image_form(rows, slots):
    return jnp.transpose(rows.reshape(-1, slots, rows.shape[-1]), (1, 0, 2))


def adamw_step(param, grad, first, second, steps):
    first_next = 0.9 * first + 0.1 * grad
    second_next = 0.999 * second + 0.001 * grad * grad
    first_hat = first_next / (1.0 - jnp.power(0.9, steps))
    second_hat = second_next / (1.0 - jnp.power(0.999, steps))
    update = -0.05 * (first_hat / (jnp.sqrt(second_hat) + 1e-08) + 0.05 * param)
    return (first_next, second_next, update)


def column_blocks(matrix):
    rows, columns = matrix.shape
    return jnp.transpose(matrix.reshape(rows, columns // LANE, LANE), (1, 0, 2))


def from_blocks(blocks):
    count, rows, lanes = blocks.shape
    return jnp.transpose(blocks, (1, 0, 2)).reshape(rows, count * lanes)


def local(
    images,
    cotangent,
    image_counts,
    shift_mask,
    rel_index,
    step_count,
    attend_weight,
    merge_weight,
    expand_weight,
    project_weight,
    norm_gains,
    norm_shifts,
    layer_biases,
    bias_table,
    attend_momentum,
    merge_momentum,
    expand_momentum,
    project_momentum,
    gains_mean,
    gains_square,
    shifts_mean,
    shifts_square,
    biases_mean,
    biases_square,
    table_mean,
    table_square,
):
    slots, patches, width = images.shape
    devices = lax.axis_size("dp")
    hidden_units = expand_weight.shape[1]
    grad_scale = 1.0 / math.sqrt(slots * devices * PATCHES)
    rank = lax.axis_index("dp")
    planes = devices // CELL
    plane = rank // CELL
    corner = (rank // 2) % 4
    shard = width // devices
    tall_shard = hidden_units // devices

    attend_rows = column_blocks(attend_weight).reshape(-1, LANE)
    other_rows = jnp.concatenate(
        [column_blocks(merge_weight).reshape(-1, LANE), column_blocks(expand_weight).reshape(-1, LANE), project_weight]
    )
    near = gather_planes(attend_rows, devices)
    near[0], other_rows = lax.optimization_barrier((near[0], other_rows))
    other_near = gather_planes(other_rows, devices)
    near = gather_corners(jnp.stack(near), devices)
    near[0], other_near[1] = lax.optimization_barrier((near[0], other_near[1]))
    far = [exchange(piece, devices, 1) for piece in near]
    far[0], *other_near = lax.optimization_barrier((far[0], *other_near))
    other_near = gather_corners(jnp.stack(other_near), devices)
    other_far = [exchange(other_near[0], devices, 1)]
    attend_sources = near + far
    if not aligned(shard):
        attend_sources = order_rows(attend_sources, ((3, shard),), rank, devices)
    this = rank.reshape(1)

    take = jnp.asarray(window_matrix(), bf16)
    put = jnp.asarray(window_matrix().T, bf16)
    combined, one_hot = combine_bias(bias_table, rel_index, shift_mask)
    bias_row = layer_biases.reshape(1, -1)
    rows = flat_rows(images)
    windows, triple, attention, mixed, weights = attend_forward(
        this, attend_sources, shard, rows, norm_gains, norm_shifts, bias_row, combined, take, put
    )
    mixed, *arrived = lax.optimization_barrier((mixed, *other_near[1:]))
    other_far += [exchange(piece, devices, 1) for piece in arrived]
    sources = other_near[:1] + arrived + other_far
    if not aligned(shard):
        sources = order_rows(
            sources, ((1, shard), (hidden_units // LANE, shard), (1, tall_shard)), rank, devices
        )
    mine = (rank & 1).reshape(1)
    block_rows, grad_middle, grad_mixed, feed_sums, hidden_sums, *body_grads = feed_forward(
        image_counts, this, sources, hidden_units, rows, flat_rows(cotangent), mixed, norm_gains, norm_shifts, bias_row,
        slots, slots * patches // 4, devices,
    )
    block_out = image_form(block_rows, slots)
    if not aligned(shard):
        merge_term, expand_term, project_term = body_grads
        body_grads = pack_core([merge_term[None], expand_term, project_term[None]], BODY, shard, rank & 1)
    body_keep, body_sent = body_grads
    body_got = exchange(body_sent, devices, 1)
    body_own, body_sends = fold(by_corner(body_keep), [by_corner(body_got)], corner, BODY, shard)
    grad_mixed, *body_sends = lax.optimization_barrier((grad_mixed, *body_sends))
    body_got = send_all(body_sends, 2, devices)

    grad_triple, table_sums, triple_sums, *head_grads = attend_backward(
        mine, devices, grad_mixed, triple, attention, windows, take
    )
    if not aligned(shard):
        head_grads = pack_core(head_grads, HEAD, shard, rank & 1)
    head_keep, head_sent = head_grads
    head_got = exchange(head_sent, devices, 1)
    head_own, head_sends = fold(by_corner(head_keep), [by_corner(head_got)], corner, HEAD, shard)
    body_own, body_sends = fold(body_own[None], [got[None] for got in body_got], plane, BODY, shard)
    grad_triple, *sends = lax.optimization_barrier((grad_triple, *head_sends, *body_sends))
    head_got = send_all(sends[:3], 2, devices)
    body_got = send_all(sends[3:], CELL, devices)
    grad_triple, head_got[1] = lax.optimization_barrier((grad_triple, head_got[1]))
    input_rows, input_sums = input_backward(rows, grad_triple, grad_middle, weights, norm_gains, put)
    input_sums, head_got[0], head_got[2], *body_got = lax.optimization_barrier(
        (input_sums, head_got[0], head_got[2], *body_got)
    )
    input_grad = image_form(input_rows, slots)
    head_own, head_sends = fold(head_own[None], [got[None] for got in head_got], plane, HEAD, shard)
    head_got = send_all(head_sends, CELL, devices)
    head_got[0], table_sums, triple_sums, hidden_sums = lax.optimization_barrier(
        (head_got[0], table_sums, triple_sums, hidden_sums)
    )
    table_term = table_gradient(table_sums, one_hot)
    momenta = (attend_momentum, merge_momentum, expand_momentum, project_momentum)
    grads, following, packed = finish(head_own, head_got, body_own, body_got, momenta, shard, grad_scale)

    small_parts = (
        jnp.stack([input_sums[0], feed_sums[0]]),
        jnp.stack([input_sums[1], feed_sums[1]]),
        jnp.concatenate([triple_sums[0], feed_sums[3], hidden_sums[0], feed_sums[2]]),
        table_term,
    )
    small = jnp.concatenate([part.reshape(-1) for part in small_parts])
    small = jnp.pad(small, (0, -small.shape[0] % (8 * LANE))).reshape(-1, LANE)

    length = tall_shard
    whole_rows, small = collect(packed, small, rank, devices)
    stack = whole_rows.reshape(CELL * planes, MATRICES, -1, LANE)
    stack = jnp.transpose(stack, (1, 0, 2, 3)).reshape(MATRICES, -1, LANE)
    kind = jnp.minimum(plane, MATRICES - 1).astype(jnp.int32).reshape(1)
    chunk = planes * length // MATRICES
    orth = newton_rows(stack, kind, chunk).reshape(MATRICES, planes, -1, LANE)
    pieces = [orth[:, 0]]
    for step in range(1, planes):
        pieces.append(exchange(orth[:, step], devices, CELL * step))
    received = jnp.stack(pieces)

    flat, start, small_sums = small.reshape(-1), 0, []
    for part in small_parts:
        small_sums.append(flat[start : start + part.size].reshape(part.shape))
        start += part.size
    small_grads = tuple((term * grad_scale for term in small_sums))
    results = [block_out, input_grad]
    for order, (grad, moment_next) in enumerate(zip(grads, following)):
        piece = pick(received, plane ^ order, 0)
        blocks = grad.shape[1] // LANE
        piece = piece.reshape(-1, LANE)[: blocks * grad.shape[0]].reshape(blocks, -1, LANE)
        extent = max(devices * grad.shape[0], grad.shape[1])
        update = -0.02 * math.sqrt(extent) * from_blocks(piece).astype(f32)
        results += [grad, moment_next, update]
    steps = step_count[0].astype(f32)
    params = (norm_gains, norm_shifts, layer_biases, bias_table)
    states = (
        (gains_mean, gains_square),
        (shifts_mean, shifts_square),
        (biases_mean, biases_square),
        (table_mean, table_square),
    )
    for param, grad, state in zip(params, small_grads, states):
        first_next, second_next, update = adamw_step(param, grad, state[0], state[1], steps)
        results += [grad, first_next, second_next, update]
    return tuple(results)


def solution(mesh):
    return jax.shard_map(
        local,
        mesh=mesh,
        in_specs=(
            P("dp", None, None),
            P("dp", None, None),
            P("dp"),
            P(),
            P(),
            P(),
            P("dp", None),
            P("dp", None),
            P("dp", None),
            P("dp", None),
            P(),
            P(),
            P(),
            P(),
            P("dp", None),
            P("dp", None),
            P("dp", None),
            P("dp", None),
            P(),
            P(),
            P(),
            P(),
            P(),
            P(),
            P(),
            P(),
        ),
        out_specs=(
            P("dp", None, None),
            P("dp", None, None),
            P("dp", None),
            P("dp", None),
            P("dp", None),
            P("dp", None),
            P("dp", None),
            P("dp", None),
            P("dp", None),
            P("dp", None),
            P("dp", None),
            P("dp", None),
            P("dp", None),
            P("dp", None),
            P(),
            P(),
            P(),
            P(),
            P(),
            P(),
            P(),
            P(),
            P(),
            P(),
            P(),
            P(),
            P(),
            P(),
            P(),
            P(),
        ),
        check_vma=False,
    )
```
